32 devices in a mesh: groups: 2 (over y), snap: 4 (over x, core), space: 4 (over z).
Axes of the slice: x: 2, y: 2, z: 4, core: 2. Of those that a mesh axis runs over, the one named last changes fastest.
Arguments:
- snapshots: bfloat16 [16384, 4096], P('space', ('groups', 'snap')), parts along dimension 1, may hold values from -12 to 12
- factor_blocks: bfloat16 [128, 4, 128, 128], P('space'), may hold values from -0.375 to 0.375
- factor_cols: int32 [128, 4], P('space'), may hold values from 0 to 31, as said below
- factor_counts: int32 [128], P('space'), may hold values from 1 to 4, as said below
- start_basis: float32 [4096, 128], P(('groups', 'snap')), parts along dimension 0, may hold values from -150 to 150
- merge_starts: float32 [3, 256, 128], replicated, may hold values from -150 to 150
Outputs:
- modes: bfloat16 [16384, 256], P(('space', 'snap'), 'groups'), parts along dimension 1
The draws below stay inside these ranges and needn't reach their ends.
There are 2 independent parts, one for each index of `groups`. The reference program is written for one: setup_inputs(seed, part) draws one part's arguments, and reference() takes and returns one part's arrays. A program takes and returns all parts, laid end to end along the dimension named above; an argument that names none is the same for every part. Nothing has to cross between parts.
Inputs may be any that keep to these rules, and one draw needn't show every extreme that they name: `factor_cols`: each entry names one of the 32 row blocks of the same group as its row block. `factor_counts`: slots at or after the count are not part of the factor.
All inputs are finite; a program needn't handle non-finite values.
Results may differ from the reference program's by a relative error of at most 0.011.
Values may be sent and summed in bfloat16 or wider, within the bound.
A program may use at most 128 MiB of HBM per device.

```python
import jax
import jax.numpy as jnp
from jax import lax

BS = 128
NNZ = 4
K = 128
RB_DEV = 32
S_DEV = 512
ROWS = 16384
NRB = 128
SNAPS = 2048
MERGES = 3
LEVELS = 2
N_SNAP = 4


def draw_factor_cols(key, part):
    others = jax.random.randint(key, (NRB, NNZ), 0, RB_DEV, dtype=jnp.int32)
    own_block = jnp.arange(NRB, dtype=jnp.int32) % RB_DEV
    return others.at[:, 0].set(own_block)


def draw_factor_counts(key, part):
    counts = jax.random.randint(key, (NRB,), 1, NNZ + 1, dtype=jnp.int32)
    return counts.at[0].set(NNZ).at[1].set(1)


def noise_field(key, shape):
    return jnp.clip(jax.random.normal(key, shape, jnp.float32), -6.0, 6.0)


def draw_snapshots(key, part):
    values = noise_field(jax.random.fold_in(key, 11), (ROWS, SNAPS))
    return values.astype(jnp.bfloat16)


def dominant_start(key, count, height, width):
    values = noise_field(key, (count, height, width))
    rows = jnp.arange(height, dtype=jnp.int32)[:, None]
    cols = jnp.arange(width, dtype=jnp.int32)[None, :]
    diagonal = (rows == cols).astype(jnp.float32) * (3.0 * jnp.sqrt(jnp.float32(height)))
    return values + diagonal[None]


def draw_start_basis(key, part):
    return dominant_start(jax.random.fold_in(key, 21), N_SNAP, S_DEV, K).reshape(SNAPS, K)


def draw_merge_starts(key, part):
    return dominant_start(jax.random.fold_in(key, 31), MERGES, 2 * K, K)


def shard_levels(stream_key, dims, cuts, least, high):
    loudness = 1.0
    for position, shards_of in cuts:
        steps = jax.random.uniform(jax.random.fold_in(jax.random.fold_in(stream_key, 6), position), (shards_of,), jnp.float32, least / len(cuts), high / len(cuts))
        loudness = loudness * jnp.repeat(jnp.exp(steps), dims[position] // shards_of).reshape((-1,) + (1,) * (len(dims) - 1 - position))
    return loudness


def centred(stream_key, dims, scale, bound, shards=(), kind=jnp.bfloat16):
    loudness = shard_levels(stream_key, dims, shards, -0.22, 0.18) if shards else 1.0
    array = jax.random.normal(stream_key, dims, jnp.float32) * scale * loudness
    return jnp.minimum(jnp.maximum(array, -bound), bound).astype(kind)


def setup_inputs(seed: int = 0, part: int = 0) -> dict:
    key_list = jax.random.split(jax.random.key(seed), 7)
    own_keys = jax.random.split(jax.random.fold_in(key_list[6], part), 7)
    snapshots = draw_snapshots(jax.random.fold_in(jax.random.fold_in(key_list[6], part), 71), part)
    factor_blocks = centred(key_list[1], (NRB, NNZ, BS, BS), (2 * BS) ** -0.5, 0.375, ((0, 4),))
    factor_cols = draw_factor_cols(jax.random.fold_in(key_list[6], 71), part)
    factor_counts = draw_factor_counts(jax.random.fold_in(key_list[6], 71), part)
    start_basis = draw_start_basis(jax.random.fold_in(jax.random.fold_in(key_list[6], part), 71), part)
    merge_starts = draw_merge_starts(jax.random.fold_in(key_list[6], 71), part)
    return dict(snapshots=snapshots, factor_blocks=factor_blocks, factor_cols=factor_cols, factor_counts=factor_counts, start_basis=start_basis, merge_starts=merge_starts)


HIGH = lax.Precision.HIGHEST

def orthonormal(matrix):
    cross_gram = jnp.dot(matrix.T, matrix, precision=HIGH)
    lower_factor = jnp.linalg.cholesky(cross_gram)
    return lax.linalg.triangular_solve(lower_factor, matrix, left_side=False, lower=True, transpose_a=True)

def weigh(group, factor_blocks, factor_cols, factor_counts):
    blocks_in = group.reshape(NRB, BS, S_DEV)
    base_block = jnp.arange(NRB, dtype=jnp.int32) // RB_DEV * RB_DEV
    accumulated = jnp.zeros((NRB, BS, S_DEV), jnp.float32)
    for slot_index in range(NNZ):
        live_mask = (slot_index < factor_counts).astype(jnp.float32)
        factor = factor_blocks[:, slot_index].astype(jnp.float32) * live_mask[:, None, None]
        source = jnp.take(blocks_in, (base_block + factor_cols[:, slot_index]).astype(jnp.int32), axis=0)
        accumulated = accumulated + jnp.einsum('bij,bjs->bis', factor, source.astype(jnp.float32))
    return accumulated.astype(jnp.bfloat16).reshape(ROWS, S_DEV)

def merge(left_node, right_node, start_vectors):
    paired = jnp.concatenate([left_node, right_node], axis=1)
    cross_gram = jnp.dot(paired.T.astype(jnp.float32), paired.astype(jnp.float32), preferred_element_type=jnp.float32)
    mixing = orthonormal(jnp.dot(cross_gram, start_vectors, precision=HIGH)).astype(jnp.bfloat16)
    return jnp.dot(paired.astype(jnp.float32), mixing.astype(jnp.float32), preferred_element_type=jnp.float32).astype(jnp.bfloat16)

def reference(snapshots, factor_blocks, factor_cols, factor_counts, start_basis, merge_starts):

    def compress(group_index):
        group = lax.dynamic_slice_in_dim(snapshots, group_index * S_DEV, S_DEV, 1)
        basis = lax.dynamic_slice_in_dim(start_basis, group_index * S_DEV, S_DEV, 0)
        weighted = weigh(group, factor_blocks, factor_cols, factor_counts)
        group_gram = jnp.dot(weighted.T.astype(jnp.float32), weighted.astype(jnp.float32), preferred_element_type=jnp.float32)
        for sweep_index in range(2):
            basis = orthonormal(jnp.dot(group_gram, basis, precision=HIGH))
        return jnp.dot(weighted.astype(jnp.float32), basis.astype(jnp.bfloat16).astype(jnp.float32), preferred_element_type=jnp.float32).astype(jnp.bfloat16)
    panels = lax.map(compress, jnp.arange(N_SNAP, dtype=jnp.int32))
    nodes = [panels[index] for index in range(N_SNAP)]
    offset_index = 0
    for level_index in range(LEVELS):
        pair_count = len(nodes) // 2
        nodes = [merge(nodes[2 * index], nodes[2 * index + 1], merge_starts[offset_index + index]) for index in range(pair_count)]
        offset_index = offset_index + pair_count
    return nodes[0]
```

```python
import functools

import jax
import jax.numpy as jnp
from jax import lax
from jax.experimental import pallas as pl
from jax.experimental.pallas import tpu as pltpu
from jax.sharding import PartitionSpec as P

HIGH = lax.Precision.HIGHEST
MESH = pl.DeviceIdType.MESH
F32 = jnp.float32
BF16 = jnp.bfloat16
VMEM = pl.BlockSpec(memory_space=pltpu.VMEM)
SMEM = pl.BlockSpec(memory_space=pltpu.SMEM)
ANY = pl.BlockSpec(memory_space=pl.ANY)
CHUNKS = 4
RIDGE = 1e-4
TN = (((0,), (0,)), ((), ()))
NT = (((1,), (1,)), ((), ()))
NN = (((1,), (0,)), ((), ()))


def dot(a, b, dims=NN, precision=None):
    return lax.dot_general(a, b, dims, precision=precision, preferred_element_type=F32)


def split(x):
    high = x.astype(BF16)
    return high, (x - high.astype(F32)).astype(BF16)


def wide(a, x):
    size = x.shape[1]
    both = dot(a, jnp.concatenate(split(x), axis=1))
    return both[:, :size] + both[:, size:]


def upper_blocks(count):
    return [(i, j) for i in range(count) for j in range(i, count)]


def flipped(index, bit):
    return index + (1 - 2 * (index // (1 << bit) % 2)) * (1 << bit)


def remote(source, target, send, recv, device):
    return pltpu.make_async_remote_copy(
        src_ref=source,
        dst_ref=target,
        send_sem=send,
        recv_sem=recv,
        device_id=device,
        device_id_type=MESH,
    )


def eye(size):
    row = lax.broadcasted_iota(jnp.int32, (size, size), 0)
    col = lax.broadcasted_iota(jnp.int32, (size, size), 1)
    return row == col


def trace(x):
    return jnp.sum(jnp.where(eye(x.shape[0]), x, 0.0))


def rows_of(block):
    return pl.ds(block * 128, 128)


def eliminate(a, e, lane):
    a, e = list(a), list(e)
    groups = len(a)
    row = lax.broadcasted_iota(jnp.int32, (8, 128), 0)
    scale = [jnp.zeros((8, 128), F32)] * groups
    for g in range(groups):
        cols = {
            h: [
                jnp.broadcast_to(a[h][:, lane + 8 * g + k : lane + 8 * g + k + 1], (8, 128))
                for k in range(8)
            ]
            for h in range(g, groups)
        }
        for k in range(8):
            pivot = jnp.broadcast_to(cols[g][k][k : k + 1, :], (8, 128))
            inverse = 1.0 / pivot
            scale[g] = jnp.where(row == k, lax.rsqrt(pivot), scale[g])
            a_row = jnp.broadcast_to(a[g][k : k + 1, :], (8, 128))
            e_row = jnp.broadcast_to(e[g][k : k + 1, :], (8, 128))
            heads = {
                m: jnp.broadcast_to(cols[g][m][k : k + 1, :], (8, 128)) for m in range(k + 1, 8)
            }
            for h in range(g, groups):
                if h == g and k == 7:
                    continue
                f = cols[h][k] * inverse
                if h == g:
                    f = jnp.where(row > k, f, 0.0)
                for m in range(k + 1, 8):
                    cols[h][m] = cols[h][m] - f * heads[m]
                a[h] = a[h] - f * a_row
                e[h] = e[h] - f * e_row
    return [x * s for x, s in zip(a, scale)], [x * s for x, s in zip(e, scale)]


def inverse_factor(cross):
    size = cross.shape[0]
    row = lax.broadcasted_iota(jnp.int32, (size, size), 0)
    col = lax.broadcasted_iota(jnp.int32, (size, size), 1)
    both = jnp.concatenate([cross, (row == col).astype(F32)], axis=1)
    done = []
    for p in range(size // 32):
        rows = [both[p * 32 + 8 * g : p * 32 + 8 * g + 8] for g in range(4)]
        a, e = eliminate([r[:, :size] for r in rows], [r[:, size:] for r in rows], p * 32)
        a, e = jnp.concatenate(a, axis=0), jnp.concatenate(e, axis=0)
        done.append(e)
        if p < size // 32 - 1:
            both = both - dot(a, jnp.concatenate([a, e], axis=1), TN, HIGH)
    return jnp.concatenate(done, axis=0)


def orthonormal(z):
    return dot(z, inverse_factor(dot(z, z, TN, HIGH)), NT, HIGH)


def sandwich(outer, inner):
    return dot(outer, dot(inner, outer, NT, HIGH), precision=HIGH)


def load_and_weigh(cols, counts, snaps_in, blocks_in, snaps, blocks, weighted, gram, sems, greet):
    row_blocks, slots, width, _ = blocks.shape
    per = row_blocks // CHUNKS
    size = snaps.shape[2]
    rows = per * width
    tall = min(256, size)

    def snap_load(c):
        at = pl.ds(c * per, per)
        return pltpu.make_async_copy(snaps_in.at[at], snaps.at[at], sems.at[0, c])

    def block_load(c):
        at = pl.ds(c * per, per)
        return pltpu.make_async_copy(blocks_in.at[at], blocks.at[at], sems.at[1, c])

    for c in range(CHUNKS):
        snap_load(c).start()
    for c in range(CHUNKS):
        block_load(c).start()
    greet()
    gram[...] = jnp.zeros_like(gram)
    for c in range(CHUNKS):
        snap_load(c).wait()

    def chunk(c, carry):
        block_load(c).wait()

        def weigh(k, carry):
            row = c * per + k
            count = counts[row]
            factors = []
            sources = []
            for slot in range(slots):
                factor = blocks[row, slot]
                live = jnp.full(factor.shape, count, jnp.int32) > slot
                factors.append(jnp.where(live, factor, jnp.zeros_like(factor)))
                sources.append(snaps[cols[slot, row]])
            product = dot(jnp.concatenate(factors, axis=1), jnp.concatenate(sources, axis=0))
            weighted[pl.ds(pl.multiple_of(row * width, width), width), :] = product.astype(BF16)
            return carry

        lax.fori_loop(0, per, weigh, 0, unroll=2)
        at = pl.ds(pl.multiple_of(c * rows, rows), rows)
        for low in range(0, size, tall):
            gram[low : low + tall, low:] += dot(
                weighted[at, low : low + tall], weighted[at, low:], TN
            )
        return carry

    lax.fori_loop(0, CHUNKS, chunk, 0)


def unpack(flat, full):
    size = full.shape[0]
    for index, (i, j) in enumerate(upper_blocks(size // 128)):
        block = flat[index * 128 : (index + 1) * 128, :]
        full[i * 128 : (i + 1) * 128, j * 128 : (j + 1) * 128] = block
        if i != j:
            full[j * 128 : (j + 1) * 128, i * 128 : (i + 1) * 128] = block.T


def kernel(n, s, cols, counts, snaps_in, blocks_in, start, starts, out, *scratch):
    (snaps, blocks, weighted, gram, load_sems) = scratch[:5]
    y = scratch[47]
    (g_own, g_out, g_in, g_all, full, vectors, t_out, t_in, g_sems, a_sems, t_sems) = scratch[5:16]
    (panels, got, p_sems, q_sems) = scratch[16:20]
    (mine_all, c_out, c_came, z_out, z_came, sum_out, sum_came, cross_all) = scratch[20:28]
    (c_sems, z_sems, s_sems) = scratch[28:31]
    (e_mine, e_got, d_mine, d_got, e_sems) = scratch[31:36]
    (x_own, x_out, x_in, x_all, xr_sems, xa_sems) = scratch[36:42]
    (cf_mine, cf_got, b_mine, b_got, b_sems) = scratch[42:47]
    snap = lax.axis_index("snap")
    space = lax.axis_index("space")
    total = s * n
    me = snap * n + space
    half = s // 2
    bit = snap % 2
    upper = bit == 1
    partner = flipped(snap, 0)
    modes = vectors.shape[1]
    size = gram.shape[0]
    rows = panels.shape[1]
    barrier = pltpu.get_barrier_semaphore()

    def device(k):
        other = lax.rem(me + k, total)
        return {"snap": other // n, "space": lax.rem(other, n)}

    def greet():
        def signal(k, carry):
            pl.semaphore_signal(barrier, inc=1, device_id=device(k), device_id_type=MESH)
            return carry

        lax.fori_loop(1, total, signal, 0)

    load_and_weigh(
        cols, counts, snaps_in, blocks_in, snaps, blocks, weighted, gram, load_sems, greet
    )

    share = g_in.shape[1]
    used = len(upper_blocks(size // 128)) * 128
    for index, (i, j) in enumerate(upper_blocks(size // 128)):
        block = gram[i * 128 : (i + 1) * 128, j * 128 : (j + 1) * 128]
        g_own[index * 128 : (index + 1) * 128, :] = block
        g_out[index * 128 : (index + 1) * 128, :] = block.astype(BF16)
    if used < g_own.shape[0]:
        g_own[used:, :] = jnp.zeros((g_own.shape[0] - used, 128), F32)
        g_out[used:, :] = jnp.zeros((g_own.shape[0] - used, 128), BF16)
    pl.semaphore_wait(barrier, total - 1)

    def share_of(index):
        return pl.ds(pl.multiple_of(index * share, share), share)

    spread = []
    for k in range(1, n):
        other = lax.rem(space + k, n)
        spread.append(
            remote(
                g_out.at[share_of(other)],
                g_in.at[k - 1],
                g_sems.at[0, k - 1],
                g_sems.at[1, k - 1],
                {"space": other},
            )
        )
    for c in spread:
        c.start()

    chosen = n // 2
    begin = start[...] * (1.0 / jnp.max(jnp.abs(start[...])))
    told = [
        remote(t_out, t_in, t_sems.at[0, k - 1], t_sems.at[1, 0], {"space": lax.rem(chosen + k, n)})
        for k in range(1, n)
    ]

    @pl.when(space == chosen)
    def _():
        unpack(g_out, full)
        first = dot(full[...], begin.astype(BF16)).astype(BF16)
        cross = dot(first, first, TN)
        scale = modes / jnp.maximum(trace(cross), 1e-30)
        factor = inverse_factor(cross * scale + jnp.where(eye(modes), RIDGE, 0.0))
        t_out[...] = factor.astype(BF16)
        t_in[...] = factor.astype(BF16)
        for c in told:
            c.start()

    mine = g_own[share_of(space), :]
    for k, c in enumerate(spread):
        c.wait_recv()
        mine = mine + g_in[k].astype(F32)
    g_all[share_of(space), :] = mine.astype(BF16)
    gathered = [
        remote(
            g_all.at[share_of(space)],
            g_all.at[share_of(space)],
            a_sems.at[0, k - 1],
            a_sems.at[1, k - 1],
            {"space": lax.rem(space + k, n)},
        )
        for k in range(1, n)
    ]
    for c in gathered:
        c.start()
    for c in gathered:
        c.wait_recv()
    unpack(g_all, full)
    trace_of = 0.0
    for i in range(size // 128):
        trace_of = trace_of + trace(
            full[i * 128 : (i + 1) * 128, i * 128 : (i + 1) * 128].astype(F32)
        )
    scale = size / trace_of
    first = wide(full[...], begin) * scale

    @pl.when(space != chosen)
    def _():
        told[0].wait_recv()

    high, low = split(first)
    between = dot(high, t_in[...], NT) + dot(low, t_in[...], NT)
    vectors[...] = (wide(full[...], between) * scale).astype(BF16)

    def rows_at(q):
        return pl.ds(pl.multiple_of(q * rows, rows), rows)

    def piece(q):
        return dot(weighted[rows_at(q), :], vectors[...]).astype(BF16)

    def mine_at(q):
        return y.at[rows_at(q)]

    out_copies = []
    arrivals = []
    for h in range(1, half):
        for side in (0, 1):
            q = lax.rem(snap // 2 + h, half) * 2 + side
            source = lax.rem(snap // 2 + half - h, half) * 2 + side
            y[rows_at(q), :] = piece(q)
            send = p_sems.at[0, 2 * h + side]
            c = remote(mine_at(q), panels.at[snap], send, p_sems.at[1, 2 * h + bit], {"snap": q})
            c.start()
            out_copies.append(c)
            arrivals.append(
                remote(mine_at(q), panels.at[source], send, p_sems.at[1, 2 * h + side], {"snap": q})
            )
    pair_copies = []
    for h in range(half):
        q = lax.rem(snap // 2 + h, half) * 2 + 1 - bit
        if h == 0:
            y[rows_at(q), :] = piece(q)
        c = remote(mine_at(q), got.at[h], q_sems.at[0, h], q_sems.at[1, h], {"snap": partner})
        c.start()
        pair_copies.append(c)
    y[rows_at(snap), :] = piece(snap)

    cross = jnp.zeros((modes, modes), F32)
    for h in range(half):
        q = lax.rem(snap // 2 + h, half) * 2 + bit
        pair_copies[h].wait_recv()
        cross = cross + dot(y[rows_at(q), :], got[h], TN)
    panels[snap] = y[rows_at(snap), :]
    panels[partner] = got[0]
    cross = jnp.where(upper, cross.T, cross)
    part_rows = modes // 2

    def part_of(index):
        return pl.ds(pl.multiple_of(index * part_rows, part_rows), part_rows)

    mine_all[...] = cross
    c_out[...] = cross.astype(BF16)
    swap = remote(
        c_out.at[part_of(1 - bit)], c_came, c_sems.at[0], c_sems.at[1], {"snap": partner}
    )
    swap.start()
    moved = dot(full[...], vectors[...])
    product = wide(vectors[...].T, moved)
    square = dot(vectors[...], vectors[...], TN)
    swap.wait_recv()
    part = mine_all[part_of(bit), :] + c_came[...].astype(F32)
    z_out[...] = part.astype(BF16)
    steps = [
        remote(
            z_out,
            z_came.at[k - 1],
            z_sems.at[0, k - 1],
            z_sems.at[1, k - 1],
            {"space": lax.rem(space + k, n)},
        )
        for k in range(1, n)
    ]
    for c in steps:
        c.start()
    e_mine[...] = inverse_factor(square)
    d_mine[...] = sandwich(e_mine[...], product)
    tell = [
        remote(e_mine, e_got, e_sems.at[0, 0], e_sems.at[1, 0], {"snap": partner}),
        remote(d_mine, d_got, e_sems.at[0, 1], e_sems.at[1, 1], {"snap": partner}),
    ]
    for c in tell:
        c.start()
    for k, c in enumerate(steps):
        c.wait_recv()
        part = part + z_came[k].astype(F32)
    sum_out[...] = part.astype(BF16)
    collect = remote(sum_out, sum_came, s_sems.at[0], s_sems.at[1], {"snap": partner})
    collect.start()
    for c in tell:
        c.wait_recv()
    collect.wait_recv()
    cross_all[part_of(bit), :] = sum_out[...].astype(F32)
    cross_all[part_of(1 - bit), :] = sum_came[...].astype(F32)
    e_low = jnp.where(upper, e_got[...], e_mine[...])
    e_high = jnp.where(upper, e_mine[...], e_got[...])
    d_low = jnp.where(upper, d_got[...], d_mine[...])
    d_high = jnp.where(upper, d_mine[...], d_got[...])
    cross = dot(e_low, dot(cross_all[...], e_high, NT, HIGH), precision=HIGH)

    def merged(level, d_low, cross, d_high):
        index = s - (s >> level) + snap // (1 << (level + 1))
        pair = jnp.concatenate(
            [
                jnp.concatenate([d_low, cross], axis=1),
                jnp.concatenate([cross.T, d_high], axis=1),
            ],
            axis=0,
        )
        return pair, orthonormal(dot(pair, starts[index], precision=HIGH))

    def diagonal(pair, mixing):
        return dot(mixing, dot(pair, mixing, precision=HIGH), TN, HIGH)

    for c in arrivals:
        c.wait_recv()
    done = 0
    for low_pair in range(half):
        for high_pair in range(low_pair + 1, half):
            sides = [
                jnp.concatenate([panels[2 * p], panels[2 * p + 1]], axis=1)
                for p in (low_pair, high_pair)
            ]
            blocks_of = dot(sides[0], sides[1], TN)
            for i in range(2):
                for j in range(2):
                    at = slice(done * 128, (done + 1) * 128)
                    block = blocks_of[i * modes : (i + 1) * modes, j * modes : (j + 1) * modes]
                    x_own[at, :] = block
                    x_out[at, :] = block.astype(BF16)
                    done = done + 1
    if done * 128 < x_own.shape[0]:
        x_own[done * 128 :, :] = jnp.zeros((x_own.shape[0] - done * 128, 128), F32)
        x_out[done * 128 :, :] = jnp.zeros((x_own.shape[0] - done * 128, 128), BF16)
    x_share = x_in.shape[1]

    def x_part(index):
        return pl.ds(pl.multiple_of(index * x_share, x_share), x_share)

    def x_spread(k):
        return remote(
            x_out.at[x_part(lax.rem(me + k, total))],
            x_in.at[k - 1],
            xr_sems.at[0, k - 1],
            xr_sems.at[1, k - 1],
            device(k),
        )

    def x_gather(k):
        return remote(
            x_all.at[x_part(me)],
            x_all.at[x_part(me)],
            xa_sems.at[0, k - 1],
            xa_sems.at[1, k - 1],
            device(k),
        )

    def each(act):
        def step(k, carry):
            act(k)
            return carry

        lax.fori_loop(1, total, step, 0)

    each(lambda k: x_spread(k).start())
    pair, mixing = merged(0, d_low, cross, d_high)

    def add(k, so_far):
        x_spread(k).wait_recv()
        return so_far + x_in[k - 1].astype(F32)

    x_all[x_part(me), :] = lax.fori_loop(1, total, add, x_own[x_part(me), :]).astype(BF16)
    each(lambda k: x_gather(k).start())
    factors = [dot(e_low, mixing[:modes], TN, HIGH), dot(e_high, mixing[modes:], TN, HIGH)]
    levels = s.bit_length() - 1
    sent = []
    for level in range(1, levels):
        count = 1 << level
        for i in range(count):
            cf_mine[level - 1, i] = factors[i].astype(BF16)
        b_mine[level - 1] = diagonal(pair, mixing).astype(BF16)
        other = {"snap": flipped(snap, level)}
        pass_on = [
            remote(
                cf_mine.at[level - 1, pl.ds(0, count)],
                cf_got.at[level - 1, pl.ds(0, count)],
                b_sems.at[0, level - 1, 0],
                b_sems.at[1, level - 1, 0],
                other,
            ),
            remote(
                b_mine.at[level - 1],
                b_got.at[level - 1],
                b_sems.at[0, level - 1, 1],
                b_sems.at[1, level - 1, 1],
                other,
            ),
        ]
        for c in pass_on:
            c.start()
        sent += pass_on
        for c in pass_on:
            c.wait_recv()
        high_side = snap // count % 2 == 1
        lows, highs = [], []
        for i in range(count):
            own, theirs = cf_mine[level - 1, i], cf_got[level - 1, i]
            lows.append(jnp.where(high_side, theirs, own))
            highs.append(jnp.where(high_side, own, theirs))
        own, theirs = b_mine[level - 1].astype(F32), b_got[level - 1].astype(F32)
        d_low = jnp.where(high_side, theirs, own)
        d_high = jnp.where(high_side, own, theirs)
        if level == 1:
            each(lambda k: x_gather(k).wait_recv())
        base = snap // (2 * count) * count
        cross = jnp.zeros((modes, modes), F32)
        for a in range(count // 2):
            pa = base + a
            for i in range(2):
                right = jnp.zeros((modes, modes), F32)
                for b in range(count // 2):
                    pb = base + count // 2 + b
                    place = pa * (2 * half - pa - 1) // 2 + pb - pa - 1
                    for j in range(2):
                        at = pl.multiple_of((place * 4 + i * 2 + j) * 128, 128)
                        right = right + dot(x_all[pl.ds(at, 128), :], highs[2 * b + j])
                cross = cross + wide(lows[2 * a + i].T, right)
        pair, mixing = merged(level, d_low, cross, d_high)
        low_mix, high_mix = mixing[:modes], mixing[modes:]
        factors = [wide(f, low_mix) for f in lows] + [wide(f, high_mix) for f in highs]
    depth = jnp.concatenate([f.astype(BF16) for f in factors], axis=0)
    out[...] = dot(jnp.concatenate([panels[i] for i in range(s)], axis=1), depth).astype(BF16)

    @pl.when(space == chosen)
    def _():
        for c in told:
            c.wait_send()

    for c in spread + gathered + out_copies + pair_copies + [swap] + steps + tell + [collect] + sent:
        c.wait_send()
    each(lambda k: x_spread(k).wait_send())
    each(lambda k: x_gather(k).wait_send())


def padded(rows, parts):
    share = -(-rows // parts)
    return -(-share // 16) * 16


def local(snapshots, factor_blocks, factor_cols, factor_counts, start_basis, merge_starts):
    n = lax.axis_size("space")
    s = lax.axis_size("snap")
    total = s * n
    size, modes = start_basis.shape
    rows = snapshots.shape[0] // s
    half = s // 2
    width = factor_blocks.shape[2]
    blocked = snapshots.reshape(snapshots.shape[0] // width, width, size)
    levels = s.bit_length() - 1
    share = padded(len(upper_blocks(size // 128)) * 128, n)
    x_share = padded(4 * (half * (half - 1) // 2) * 128, total)
    dma = pltpu.SemaphoreType.DMA
    scratch = [
        pltpu.VMEM(blocked.shape, BF16),
        pltpu.VMEM(factor_blocks.shape, BF16),
        pltpu.VMEM(snapshots.shape, BF16),
        pltpu.VMEM((size, size), F32),
        dma((2, CHUNKS)),
        pltpu.VMEM((share * n, 128), F32),
        pltpu.VMEM((share * n, 128), BF16),
        pltpu.VMEM((n - 1, share, 128), BF16),
        pltpu.VMEM((share * n, 128), BF16),
        pltpu.VMEM((size, size), BF16),
        pltpu.VMEM((size, modes), BF16),
        pltpu.VMEM((modes, modes), BF16),
        pltpu.VMEM((modes, modes), BF16),
        dma((2, n - 1)),
        dma((2, n - 1)),
        dma((2, n - 1)),
        pltpu.VMEM((s, rows, modes), BF16),
        pltpu.VMEM((half, rows, modes), BF16),
        dma((2, s)),
        dma((2, half)),
        pltpu.VMEM((modes, modes), F32),
        pltpu.VMEM((modes, modes), BF16),
        pltpu.VMEM((modes // 2, modes), BF16),
        pltpu.VMEM((modes // 2, modes), BF16),
        pltpu.VMEM((n - 1, modes // 2, modes), BF16),
        pltpu.VMEM((modes // 2, modes), BF16),
        pltpu.VMEM((modes // 2, modes), BF16),
        pltpu.VMEM((modes, modes), F32),
        dma((2,)),
        dma((2, n - 1)),
        dma((2,)),
        pltpu.VMEM((modes, modes), F32),
        pltpu.VMEM((modes, modes), F32),
        pltpu.VMEM((modes, modes), F32),
        pltpu.VMEM((modes, modes), F32),
        dma((2, 2)),
        pltpu.VMEM((x_share * total, 128), F32),
        pltpu.VMEM((x_share * total, 128), BF16),
        pltpu.VMEM((total - 1, x_share, 128), BF16),
        pltpu.VMEM((x_share * total, 128), BF16),
        dma((2, total - 1)),
        dma((2, total - 1)),
        pltpu.VMEM((levels - 1, half, modes, modes), BF16),
        pltpu.VMEM((levels - 1, half, modes, modes), BF16),
        pltpu.VMEM((levels - 1, modes, modes), BF16),
        pltpu.VMEM((levels - 1, modes, modes), BF16),
        dma((2, levels - 1, 2)),
        pltpu.VMEM((snapshots.shape[0], modes), BF16),
    ]
    return pl.pallas_call(
        functools.partial(kernel, n, s),
        in_specs=[SMEM, SMEM, ANY, ANY, VMEM, VMEM],
        out_specs=VMEM,
        out_shape=jax.ShapeDtypeStruct((rows, modes), BF16),
        scratch_shapes=scratch,
        compiler_params=pltpu.CompilerParams(
            collective_id=0, has_side_effects=True, vmem_limit_bytes=48 << 20
        ),
        name="modes",
    )(factor_cols.T, factor_counts, blocked, factor_blocks, start_basis, merge_starts)


def solution(mesh):
    return jax.shard_map(
        local,
        mesh=mesh,
        in_specs=(
            P("space", ("groups", "snap")),
            P("space", None, None, None),
            P("space", None),
            P("space"),
            P(("groups", "snap"), None),
            P(),
        ),
        out_specs=P(("space", "snap"), "groups"),
        check_vma=False,
    )
```

```python
import functools

import jax
import jax.numpy as jnp
from jax import lax
from jax.experimental import pallas as pl
from jax.experimental.pallas import tpu as pltpu
from jax.sharding import PartitionSpec as P

HIGH = lax.Precision.HIGHEST
MESH = pl.DeviceIdType.MESH
F32 = jnp.float32
BF16 = jnp.bfloat16
VMEM = pl.BlockSpec(memory_space=pltpu.VMEM)
SMEM = pl.BlockSpec(memory_space=pltpu.SMEM)
ANY = pl.BlockSpec(memory_space=pl.ANY)
CHUNKS = 4
VMEM_LIMIT = 56 << 20
RIDGE = 1e-4
TN = (((0,), (0,)), ((), ()))
NT = (((1,), (1,)), ((), ()))
NN = (((1,), (0,)), ((), ()))


def dot(a, b, dims=NN, precision=None):
    return lax.dot_general(a, b, dims, precision=precision, preferred_element_type=F32)


def split(x):
    high = x.astype(BF16)
    return high, (x - high.astype(F32)).astype(BF16)


def wide(a, x):
    size = x.shape[1]
    both = dot(a, jnp.concatenate(split(x), axis=1))
    return both[:, :size] + both[:, size:]


def upper_blocks(count):
    return [(i, j) for i in range(count) for j in range(i, count)]


def flipped(index, bit):
    return index + (1 - 2 * (index // (1 << bit) % 2)) * (1 << bit)


def remote(source, target, send, recv, device):
    return pltpu.make_async_remote_copy(
        src_ref=source,
        dst_ref=target,
        send_sem=send,
        recv_sem=recv,
        device_id=device,
        device_id_type=MESH,
    )


def eye(size):
    row = lax.broadcasted_iota(jnp.int32, (size, size), 0)
    col = lax.broadcasted_iota(jnp.int32, (size, size), 1)
    return row == col


def trace(x):
    return jnp.sum(jnp.where(eye(x.shape[0]), x, 0.0))


def rows_of(block):
    return pl.ds(block * 128, 128)


def eliminate(a, e, lane):
    a, e = list(a), list(e)
    groups = len(a)
    row = lax.broadcasted_iota(jnp.int32, (8, 128), 0)
    scale = [jnp.zeros((8, 128), F32)] * groups
    for g in range(groups):
        cols = {
            h: [
                jnp.broadcast_to(a[h][:, lane + 8 * g + k : lane + 8 * g + k + 1], (8, 128))
                for k in range(8)
            ]
            for h in range(g, groups)
        }
        for k in range(8):
            pivot = jnp.broadcast_to(cols[g][k][k : k + 1, :], (8, 128))
            inverse = 1.0 / pivot
            scale[g] = jnp.where(row == k, lax.rsqrt(pivot), scale[g])
            a_row = jnp.broadcast_to(a[g][k : k + 1, :], (8, 128))
            e_row = jnp.broadcast_to(e[g][k : k + 1, :], (8, 128))
            heads = {
                m: jnp.broadcast_to(cols[g][m][k : k + 1, :], (8, 128)) for m in range(k + 1, 8)
            }
            for h in range(g, groups):
                if h == g and k == 7:
                    continue
                f = cols[h][k] * inverse
                if h == g:
                    f = jnp.where(row > k, f, 0.0)
                for m in range(k + 1, 8):
                    cols[h][m] = cols[h][m] - f * heads[m]
                a[h] = a[h] - f * a_row
                e[h] = e[h] - f * e_row
    return [x * s for x, s in zip(a, scale)], [x * s for x, s in zip(e, scale)]


def inverse_factor(cross):
    size = cross.shape[0]
    row = lax.broadcasted_iota(jnp.int32, (size, size), 0)
    col = lax.broadcasted_iota(jnp.int32, (size, size), 1)
    both = jnp.concatenate([cross, (row == col).astype(F32)], axis=1)
    done = []
    for p in range(size // 32):
        rows = [both[p * 32 + 8 * g : p * 32 + 8 * g + 8] for g in range(4)]
        a, e = eliminate([r[:, :size] for r in rows], [r[:, size:] for r in rows], p * 32)
        a, e = jnp.concatenate(a, axis=0), jnp.concatenate(e, axis=0)
        done.append(e)
        if p < size // 32 - 1:
            both = both - dot(a, jnp.concatenate([a, e], axis=1), TN, HIGH)
    return jnp.concatenate(done, axis=0)


def orthonormal(z):
    return dot(z, inverse_factor(dot(z, z, TN, HIGH)), NT, HIGH)


def sandwich(outer, inner):
    return dot(outer, dot(inner, outer, NT, HIGH), precision=HIGH)


def load_and_weigh(cols, counts, snaps_in, blocks_in, snaps, blocks, weighted, gram, sems, greet):
    row_blocks, slots, width, _ = blocks.shape
    per = row_blocks // CHUNKS
    size = snaps.shape[2]
    tall = min(256, size)

    def snap_load(c):
        at = pl.ds(c * per, per)
        return pltpu.make_async_copy(snaps_in.at[at], snaps.at[at], sems.at[0, c])

    def block_load(c):
        at = pl.ds(c * per, per)
        return pltpu.make_async_copy(blocks_in.at[at], blocks.at[at], sems.at[1, c])

    for c in range(CHUNKS):
        snap_load(c).start()
    for c in range(CHUNKS):
        block_load(c).start()
    greet()
    for c in range(CHUNKS):
        snap_load(c).wait()

    def chunk(c, carry):
        block_load(c).wait()

        def weigh(k, carry):
            row = c * per + k
            count = counts[row]
            factors = []
            sources = []
            for slot in range(slots):
                factor = blocks[row, slot]
                live = jnp.full(factor.shape, count, jnp.int32) > slot
                factors.append(jnp.where(live, factor, jnp.zeros_like(factor)))
                sources.append(snaps[cols[slot, row]])
            product = dot(jnp.concatenate(factors, axis=1), jnp.concatenate(sources, axis=0))
            weighted[pl.ds(pl.multiple_of(row * width, width), width), :] = product.astype(BF16)
            return carry

        lax.fori_loop(0, per, weigh, 0, unroll=8)
        return carry

    lax.fori_loop(0, CHUNKS, chunk, 0)
    for low in range(0, size, tall):
        gram[low : low + tall, low:] = dot(weighted[:, low : low + tall], weighted[:, low:], TN)


def unpack(flat, full):
    size = full.shape[0]
    for index, (i, j) in enumerate(upper_blocks(size // 128)):
        block = flat[index * 128 : (index + 1) * 128, :]
        full[i * 128 : (i + 1) * 128, j * 128 : (j + 1) * 128] = block
        if i != j:
            full[j * 128 : (j + 1) * 128, i * 128 : (i + 1) * 128] = block.T


def kernel(n, s, cols, counts, snaps_in, blocks_in, start_in, starts_in, out, *scratch):
    (snaps, blocks, weighted, gram, load_sems) = scratch[:5]
    y, start, starts, start_sems = scratch[47:]
    (g_own, g_out, g_in, g_all, full, vectors, t_out, t_in, g_sems, a_sems, t_sems) = scratch[5:16]
    (panels, got, p_sems, q_sems) = scratch[16:20]
    (mine_all, c_out, c_came, z_out, z_came, sum_out, sum_came, cross_all) = scratch[20:28]
    (c_sems, z_sems, s_sems) = scratch[28:31]
    (e_mine, e_got, d_mine, d_got, e_sems) = scratch[31:36]
    (x_own, x_out, x_in, x_all, xr_sems, xa_sems) = scratch[36:42]
    (cf_mine, cf_got, b_mine, b_got, b_sems) = scratch[42:47]
    snap = lax.axis_index("snap")
    space = lax.axis_index("space")
    total = s * n
    me = snap * n + space
    half = s // 2
    bit = snap % 2
    upper = bit == 1
    partner = flipped(snap, 0)
    modes = vectors.shape[1]
    size = gram.shape[0]
    rows = panels.shape[1]
    barrier = pltpu.get_barrier_semaphore()

    def device(k):
        other = lax.rem(me + k, total)
        return {"snap": other // n, "space": lax.rem(other, n)}

    small_loads = [
        pltpu.make_async_copy(start_in, start, start_sems.at[0]),
        pltpu.make_async_copy(starts_in, starts, start_sems.at[1]),
    ]

    def greet():
        for c in small_loads:
            c.start()

        def signal(k, carry):
            pl.semaphore_signal(barrier, inc=1, device_id=device(k), device_id_type=MESH)
            return carry

        lax.fori_loop(1, total, signal, 0)

    load_and_weigh(
        cols, counts, snaps_in, blocks_in, snaps, blocks, weighted, gram, load_sems, greet
    )

    share = g_in.shape[1]
    used = len(upper_blocks(size // 128)) * 128
    for index, (i, j) in enumerate(upper_blocks(size // 128)):
        block = gram[i * 128 : (i + 1) * 128, j * 128 : (j + 1) * 128]
        g_own[index * 128 : (index + 1) * 128, :] = block
        g_out[index * 128 : (index + 1) * 128, :] = block.astype(BF16)
    if used < g_own.shape[0]:
        g_own[used:, :] = jnp.zeros((g_own.shape[0] - used, 128), F32)
        g_out[used:, :] = jnp.zeros((g_own.shape[0] - used, 128), BF16)
    pl.semaphore_wait(barrier, total - 1)

    def share_of(index):
        return pl.ds(pl.multiple_of(index * share, share), share)

    spread = []
    for k in range(1, n):
        other = lax.rem(space + k, n)
        spread.append(
            remote(
                g_out.at[share_of(other)],
                g_in.at[k - 1],
                g_sems.at[0, k - 1],
                g_sems.at[1, k - 1],
                {"space": other},
            )
        )
    for c in spread:
        c.start()

    chosen = n // 2
    for c in small_loads:
        c.wait()
    begin = start[...] * (1.0 / jnp.max(jnp.abs(start[...])))
    told = [
        remote(t_out, t_in, t_sems.at[0, k - 1], t_sems.at[1, 0], {"space": lax.rem(chosen + k, n)})
        for k in range(1, n)
    ]

    @pl.when(space == chosen)
    def _():
        unpack(g_out, full)
        first = dot(full[...], begin.astype(BF16)).astype(BF16)
        cross = dot(first, first, TN)
        scale = modes / jnp.maximum(trace(cross), 1e-30)
        factor = inverse_factor(cross * scale + jnp.where(eye(modes), RIDGE, 0.0))
        t_out[...] = factor.astype(BF16)
        t_in[...] = factor.astype(BF16)
        for c in told:
            c.start()

    mine = g_own[share_of(space), :]
    for k, c in enumerate(spread):
        c.wait_recv()
        mine = mine + g_in[k].astype(F32)
    g_all[share_of(space), :] = mine.astype(BF16)
    gathered = [
        remote(
            g_all.at[share_of(space)],
            g_all.at[share_of(space)],
            a_sems.at[0, k - 1],
            a_sems.at[1, k - 1],
            {"space": lax.rem(space + k, n)},
        )
        for k in range(1, n)
    ]
    for c in gathered:
        c.start()
    for c in gathered:
        c.wait_recv()
    unpack(g_all, full)
    trace_of = 0.0
    for i in range(size // 128):
        trace_of = trace_of + trace(
            full[i * 128 : (i + 1) * 128, i * 128 : (i + 1) * 128].astype(F32)
        )
    scale = size / trace_of
    first = wide(full[...], begin) * scale

    @pl.when(space != chosen)
    def _():
        told[0].wait_recv()

    high, low = split(first)
    between = dot(high, t_in[...], NT) + dot(low, t_in[...], NT)
    vectors[...] = (wide(full[...], between) * scale).astype(BF16)

    def rows_at(q):
        return pl.ds(pl.multiple_of(q * rows, rows), rows)

    def piece(q):
        return dot(weighted[rows_at(q), :], vectors[...]).astype(BF16)

    def mine_at(q):
        return y.at[rows_at(q)]

    out_copies = []
    arrivals = []
    for h in range(1, half):
        for side in (0, 1):
            q = lax.rem(snap // 2 + h, half) * 2 + side
            source = lax.rem(snap // 2 + half - h, half) * 2 + side
            y[rows_at(q), :] = piece(q)
            send = p_sems.at[0, 2 * h + side]
            c = remote(mine_at(q), panels.at[snap], send, p_sems.at[1, 2 * h + bit], {"snap": q})
            c.start()
            out_copies.append(c)
            arrivals.append(
                remote(mine_at(q), panels.at[source], send, p_sems.at[1, 2 * h + side], {"snap": q})
            )
    pair_copies = []
    for h in range(half):
        q = lax.rem(snap // 2 + h, half) * 2 + 1 - bit
        if h == 0:
            y[rows_at(q), :] = piece(q)
        c = remote(mine_at(q), got.at[h], q_sems.at[0, h], q_sems.at[1, h], {"snap": partner})
        c.start()
        pair_copies.append(c)
    y[rows_at(snap), :] = piece(snap)

    cross = jnp.zeros((modes, modes), F32)
    for h in range(half):
        q = lax.rem(snap // 2 + h, half) * 2 + bit
        pair_copies[h].wait_recv()
        cross = cross + dot(y[rows_at(q), :], got[h], TN)
    panels[snap] = y[rows_at(snap), :]
    panels[partner] = got[0]
    cross = jnp.where(upper, cross.T, cross)
    part_rows = modes // 2

    def part_of(index):
        return pl.ds(pl.multiple_of(index * part_rows, part_rows), part_rows)

    mine_all[...] = cross
    c_out[...] = cross.astype(BF16)
    swap = remote(
        c_out.at[part_of(1 - bit)], c_came, c_sems.at[0], c_sems.at[1], {"snap": partner}
    )
    swap.start()
    moved = dot(full[...], vectors[...])
    product = wide(vectors[...].T, moved)
    square = dot(vectors[...], vectors[...], TN)
    swap.wait_recv()
    part = mine_all[part_of(bit), :] + c_came[...].astype(F32)
    z_out[...] = part.astype(BF16)
    steps = [
        remote(
            z_out,
            z_came.at[k - 1],
            z_sems.at[0, k - 1],
            z_sems.at[1, k - 1],
            {"space": lax.rem(space + k, n)},
        )
        for k in range(1, n)
    ]
    for c in steps:
        c.start()
    e_mine[...] = inverse_factor(square)
    d_mine[...] = sandwich(e_mine[...], product)
    tell = [
        remote(e_mine, e_got, e_sems.at[0, 0], e_sems.at[1, 0], {"snap": partner}),
        remote(d_mine, d_got, e_sems.at[0, 1], e_sems.at[1, 1], {"snap": partner}),
    ]
    for c in tell:
        c.start()
    for k, c in enumerate(steps):
        c.wait_recv()
        part = part + z_came[k].astype(F32)
    sum_out[...] = part.astype(BF16)
    collect = remote(sum_out, sum_came, s_sems.at[0], s_sems.at[1], {"snap": partner})
    collect.start()
    for c in tell:
        c.wait_recv()
    collect.wait_recv()
    cross_all[part_of(bit), :] = sum_out[...].astype(F32)
    cross_all[part_of(1 - bit), :] = sum_came[...].astype(F32)
    e_low = jnp.where(upper, e_got[...], e_mine[...])
    e_high = jnp.where(upper, e_mine[...], e_got[...])
    d_low = jnp.where(upper, d_got[...], d_mine[...])
    d_high = jnp.where(upper, d_mine[...], d_got[...])
    cross = dot(e_low, dot(cross_all[...], e_high, NT, HIGH), precision=HIGH)

    def merged(level, d_low, cross, d_high):
        index = s - (s >> level) + snap // (1 << (level + 1))
        pair = jnp.concatenate(
            [
                jnp.concatenate([d_low, cross], axis=1),
                jnp.concatenate([cross.T, d_high], axis=1),
            ],
            axis=0,
        )
        return pair, orthonormal(dot(pair, starts[index], precision=HIGH))

    def diagonal(pair, mixing):
        return dot(mixing, dot(pair, mixing, precision=HIGH), TN, HIGH)

    for c in arrivals:
        c.wait_recv()
    done = 0
    for low_pair in range(half):
        for high_pair in range(low_pair + 1, half):
            sides = [
                jnp.concatenate([panels[2 * p], panels[2 * p + 1]], axis=1)
                for p in (low_pair, high_pair)
            ]
            blocks_of = dot(sides[0], sides[1], TN)
            for i in range(2):
                for j in range(2):
                    at = slice(done * 128, (done + 1) * 128)
                    block = blocks_of[i * modes : (i + 1) * modes, j * modes : (j + 1) * modes]
                    x_own[at, :] = block
                    x_out[at, :] = block.astype(BF16)
                    done = done + 1
    if done * 128 < x_own.shape[0]:
        x_own[done * 128 :, :] = jnp.zeros((x_own.shape[0] - done * 128, 128), F32)
        x_out[done * 128 :, :] = jnp.zeros((x_own.shape[0] - done * 128, 128), BF16)
    x_share = x_in.shape[1]

    def x_part(index):
        return pl.ds(pl.multiple_of(index * x_share, x_share), x_share)

    def x_spread(k):
        return remote(
            x_out.at[x_part(lax.rem(me + k, total))],
            x_in.at[k - 1],
            xr_sems.at[0, k - 1],
            xr_sems.at[1, k - 1],
            device(k),
        )

    def x_gather(k):
        return remote(
            x_all.at[x_part(me)],
            x_all.at[x_part(me)],
            xa_sems.at[0, k - 1],
            xa_sems.at[1, k - 1],
            device(k),
        )

    def each(act):
        def step(k, carry):
            act(k)
            return carry

        lax.fori_loop(1, total, step, 0)

    each(lambda k: x_spread(k).start())
    pair, mixing = merged(0, d_low, cross, d_high)

    def add(k, so_far):
        x_spread(k).wait_recv()
        return so_far + x_in[k - 1].astype(F32)

    x_all[x_part(me), :] = lax.fori_loop(1, total, add, x_own[x_part(me), :]).astype(BF16)
    each(lambda k: x_gather(k).start())
    factors = [dot(e_low, mixing[:modes], TN, HIGH), dot(e_high, mixing[modes:], TN, HIGH)]
    levels = s.bit_length() - 1
    sent = []
    for level in range(1, levels):
        count = 1 << level
        for i in range(count):
            cf_mine[level - 1, i] = factors[i].astype(BF16)
        b_mine[level - 1] = diagonal(pair, mixing).astype(BF16)
        other = {"snap": flipped(snap, level)}
        pass_on = [
            remote(
                cf_mine.at[level - 1, pl.ds(0, count)],
                cf_got.at[level - 1, pl.ds(0, count)],
                b_sems.at[0, level - 1, 0],
                b_sems.at[1, level - 1, 0],
                other,
            ),
            remote(
                b_mine.at[level - 1],
                b_got.at[level - 1],
                b_sems.at[0, level - 1, 1],
                b_sems.at[1, level - 1, 1],
                other,
            ),
        ]
        for c in pass_on:
            c.start()
        sent += pass_on
        for c in pass_on:
            c.wait_recv()
        high_side = snap // count % 2 == 1
        lows, highs = [], []
        for i in range(count):
            own, theirs = cf_mine[level - 1, i], cf_got[level - 1, i]
            lows.append(jnp.where(high_side, theirs, own))
            highs.append(jnp.where(high_side, own, theirs))
        own, theirs = b_mine[level - 1].astype(F32), b_got[level - 1].astype(F32)
        d_low = jnp.where(high_side, theirs, own)
        d_high = jnp.where(high_side, own, theirs)
        if level == 1:
            each(lambda k: x_gather(k).wait_recv())
        base = snap // (2 * count) * count
        cross = jnp.zeros((modes, modes), F32)
        for a in range(count // 2):
            pa = base + a
            for i in range(2):
                right = jnp.zeros((modes, modes), F32)
                for b in range(count // 2):
                    pb = base + count // 2 + b
                    place = pa * (2 * half - pa - 1) // 2 + pb - pa - 1
                    for j in range(2):
                        at = pl.multiple_of((place * 4 + i * 2 + j) * 128, 128)
                        right = right + dot(x_all[pl.ds(at, 128), :], highs[2 * b + j])
                cross = cross + wide(lows[2 * a + i].T, right)
        pair, mixing = merged(level, d_low, cross, d_high)
        low_mix, high_mix = mixing[:modes], mixing[modes:]
        factors = [wide(f, low_mix) for f in lows] + [wide(f, high_mix) for f in highs]
    depth = jnp.concatenate([f.astype(BF16) for f in factors], axis=0)
    out[...] = dot(jnp.concatenate([panels[i] for i in range(s)], axis=1), depth).astype(BF16)

    @pl.when(space == chosen)
    def _():
        for c in told:
            c.wait_send()

    for c in spread + gathered + out_copies + pair_copies + [swap] + steps + tell + [collect] + sent:
        c.wait_send()
    each(lambda k: x_spread(k).wait_send())
    each(lambda k: x_gather(k).wait_send())


def padded(rows, parts):
    share = -(-rows // parts)
    return -(-share // 16) * 16


def local(snapshots, factor_blocks, factor_cols, factor_counts, start_basis, merge_starts):
    n = lax.axis_size("space")
    s = lax.axis_size("snap")
    total = s * n
    size, modes = start_basis.shape
    rows = snapshots.shape[0] // s
    half = s // 2
    width = factor_blocks.shape[2]
    blocked = snapshots.reshape(snapshots.shape[0] // width, width, size)
    levels = s.bit_length() - 1
    share = padded(len(upper_blocks(size // 128)) * 128, n)
    x_share = padded(4 * (half * (half - 1) // 2) * 128, total)
    dma = pltpu.SemaphoreType.DMA
    scratch = [
        pltpu.VMEM(blocked.shape, BF16),
        pltpu.VMEM(factor_blocks.shape, BF16),
        pltpu.VMEM(snapshots.shape, BF16),
        pltpu.VMEM((size, size), F32),
        dma((2, CHUNKS)),
        pltpu.VMEM((share * n, 128), F32),
        pltpu.VMEM((share * n, 128), BF16),
        pltpu.VMEM((n - 1, share, 128), BF16),
        pltpu.VMEM((share * n, 128), BF16),
        pltpu.VMEM((size, size), BF16),
        pltpu.VMEM((size, modes), BF16),
        pltpu.VMEM((modes, modes), BF16),
        pltpu.VMEM((modes, modes), BF16),
        dma((2, n - 1)),
        dma((2, n - 1)),
        dma((2, n - 1)),
        pltpu.VMEM((s, rows, modes), BF16),
        pltpu.VMEM((half, rows, modes), BF16),
        dma((2, s)),
        dma((2, half)),
        pltpu.VMEM((modes, modes), F32),
        pltpu.VMEM((modes, modes), BF16),
        pltpu.VMEM((modes // 2, modes), BF16),
        pltpu.VMEM((modes // 2, modes), BF16),
        pltpu.VMEM((n - 1, modes // 2, modes), BF16),
        pltpu.VMEM((modes // 2, modes), BF16),
        pltpu.VMEM((modes // 2, modes), BF16),
        pltpu.VMEM((modes, modes), F32),
        dma((2,)),
        dma((2, n - 1)),
        dma((2,)),
        pltpu.VMEM((modes, modes), F32),
        pltpu.VMEM((modes, modes), F32),
        pltpu.VMEM((modes, modes), F32),
        pltpu.VMEM((modes, modes), F32),
        dma((2, 2)),
        pltpu.VMEM((x_share * total, 128), F32),
        pltpu.VMEM((x_share * total, 128), BF16),
        pltpu.VMEM((total - 1, x_share, 128), BF16),
        pltpu.VMEM((x_share * total, 128), BF16),
        dma((2, total - 1)),
        dma((2, total - 1)),
        pltpu.VMEM((levels - 1, half, modes, modes), BF16),
        pltpu.VMEM((levels - 1, half, modes, modes), BF16),
        pltpu.VMEM((levels - 1, modes, modes), BF16),
        pltpu.VMEM((levels - 1, modes, modes), BF16),
        dma((2, levels - 1, 2)),
        pltpu.VMEM((snapshots.shape[0], modes), BF16),
        pltpu.VMEM(start_basis.shape, F32),
        pltpu.VMEM(merge_starts.shape, F32),
        dma((2,)),
    ]
    return pl.pallas_call(
        functools.partial(kernel, n, s),
        in_specs=[SMEM, SMEM, ANY, ANY, ANY, ANY],
        out_specs=VMEM,
        out_shape=jax.ShapeDtypeStruct((rows, modes), BF16),
        scratch_shapes=scratch,
        compiler_params=pltpu.CompilerParams(
            collective_id=0, has_side_effects=True, vmem_limit_bytes=VMEM_LIMIT
        ),
        name="modes",
    )(factor_cols.T, factor_counts, blocked, factor_blocks, start_basis, merge_starts)


def solution(mesh):
    return jax.shard_map(
        local,
        mesh=mesh,
        in_specs=(
            P("space", ("groups", "snap")),
            P("space", None, None, None),
            P("space", None),
            P("space"),
            P(("groups", "snap"), None),
            P(),
        ),
        out_specs=P(("space", "snap"), "groups"),
        check_vma=False,
    )
```

```python
import functools

import jax
import jax.numpy as jnp
from jax import lax
from jax.experimental import pallas as pl
from jax.experimental.pallas import tpu as pltpu
from jax.sharding import PartitionSpec as P

HIGH = lax.Precision.HIGHEST
MESH = pl.DeviceIdType.MESH
F32 = jnp.float32
BF16 = jnp.bfloat16
VMEM = pl.BlockSpec(memory_space=pltpu.VMEM)
SMEM = pl.BlockSpec(memory_space=pltpu.SMEM)
ANY = pl.BlockSpec(memory_space=pl.ANY)
CHUNKS = 4
VMEM_LIMIT = 56 << 20
RIDGE = 1e-4
TN = (((0,), (0,)), ((), ()))
NT = (((1,), (1,)), ((), ()))
NN = (((1,), (0,)), ((), ()))


def dot(a, b, dims=NN, precision=None):
    return lax.dot_general(a, b, dims, precision=precision, preferred_element_type=F32)


def split(x):
    high = x.astype(BF16)
    return high, (x - high.astype(F32)).astype(BF16)


def wide(a, x):
    size = x.shape[1]
    both = dot(a, jnp.concatenate(split(x), axis=1))
    return both[:, :size] + both[:, size:]


def upper_blocks(count):
    return [(i, j) for i in range(count) for j in range(i, count)]


def flipped(index, bit):
    return index + (1 - 2 * (index // (1 << bit) % 2)) * (1 << bit)


def remote(source, target, send, recv, device):
    return pltpu.make_async_remote_copy(
        src_ref=source,
        dst_ref=target,
        send_sem=send,
        recv_sem=recv,
        device_id=device,
        device_id_type=MESH,
    )


def eye(size):
    row = lax.broadcasted_iota(jnp.int32, (size, size), 0)
    col = lax.broadcasted_iota(jnp.int32, (size, size), 1)
    return row == col


def trace(x):
    return jnp.sum(jnp.where(eye(x.shape[0]), x, 0.0))


def rows_of(block):
    return pl.ds(block * 128, 128)


def eliminate(a, e, lane):
    a, e = list(a), list(e)
    groups = len(a)
    row = lax.broadcasted_iota(jnp.int32, (8, 128), 0)
    scale = [jnp.zeros((8, 128), F32)] * groups

    def spread(x, k):
        return jnp.broadcast_to(x[k : k + 1, :], (8, 128))

    for g in range(groups):
        cols = {
            h: [
                jnp.broadcast_to(a[h][:, lane + 8 * g + k : lane + 8 * g + k + 1], (8, 128))
                for k in range(8)
            ]
            for h in range(g, groups)
        }
        for k in range(0, 8, 2):
            p, q, r = spread(cols[g][k], k), spread(cols[g][k], k + 1), spread(cols[g][k + 1], k + 1)
            det = p * r - q * q
            over_det = 1.0 / det
            over_p = 1.0 / p
            i, j, l = r * over_det, q * over_det, p * over_det
            scale[g] = jnp.where(row == k, lax.rsqrt(p), scale[g])
            scale[g] = jnp.where(row == k + 1, lax.rsqrt(det * over_p), scale[g])
            a_rows = spread(a[g], k), spread(a[g], k + 1)
            e_rows = spread(e[g], k), spread(e[g], k + 1)
            heads = {
                m: (spread(cols[g][m], k), spread(cols[g][m], k + 1)) for m in range(k + 2, 8)
            }
            for h in range(g, groups):
                c, d = cols[h][k], cols[h][k + 1]
                f1 = c * i - d * j
                f2 = d * l - c * j
                if h == g:
                    f1 = jnp.where(row > k + 1, f1, jnp.where(row == k + 1, q * over_p, 0.0))
                    f2 = jnp.where(row > k + 1, f2, 0.0)
                for m in range(k + 2, 8):
                    cols[h][m] = cols[h][m] - (f1 * heads[m][0] + f2 * heads[m][1])
                a[h] = a[h] - (f1 * a_rows[0] + f2 * a_rows[1])
                e[h] = e[h] - (f1 * e_rows[0] + f2 * e_rows[1])
    return [x * s for x, s in zip(a, scale)], [x * s for x, s in zip(e, scale)]


def thirds(x):
    high = x.astype(BF16)
    rest = x - high.astype(F32)
    middle = rest.astype(BF16)
    return high, middle, (rest - middle.astype(F32)).astype(BF16)


def outer(a, b):
    a, b = thirds(a), thirds(b)
    left = jnp.concatenate([a[0], a[0], a[1], a[0], a[2], a[1]], axis=0)
    right = jnp.concatenate([b[0], b[1], b[0], b[2], b[0], b[1]], axis=0)
    return dot(left, right, TN)


def inverse_factor(cross):
    size = cross.shape[0]
    diagonal = jnp.where(eye(size), cross, 0.0)
    down = lax.rsqrt(jnp.sum(diagonal, axis=1, keepdims=True))
    along = lax.rsqrt(jnp.sum(diagonal, axis=0, keepdims=True))
    both = jnp.concatenate(
        [cross * down * along, jnp.where(eye(size), jnp.broadcast_to(along, cross.shape), 0.0)],
        axis=1,
    )
    done = []
    for p in range(size // 32):
        rows = [both[p * 32 + 8 * g : p * 32 + 8 * g + 8] for g in range(4)]
        a, e = eliminate([r[:, :size] for r in rows], [r[:, size:] for r in rows], p * 32)
        a, e = jnp.concatenate(a, axis=0), jnp.concatenate(e, axis=0)
        done.append(e)
        if p < size // 32 - 1:
            both = both - outer(a, jnp.concatenate([a, e], axis=1))
    return jnp.concatenate(done, axis=0)


def near(a, b, dims=NN):
    a, b = split(a), split(b)
    return dot(a[0], b[0], dims) + (dot(a[0], b[1], dims) + dot(a[1], b[0], dims))


def orthonormal(z):
    return near(z, inverse_factor(near(z, z, TN)), NT)


def sandwich(outer, inner):
    return dot(outer, dot(inner, outer, NT, HIGH), precision=HIGH)


def load_and_weigh(cols, counts, snaps_in, blocks_in, snaps, blocks, weighted, gram, sems, greet):
    row_blocks, slots, width, _ = blocks.shape
    per = row_blocks // CHUNKS
    size = snaps.shape[2]
    tall = min(256, size)

    def snap_load(c):
        at = pl.ds(c * per, per)
        return pltpu.make_async_copy(snaps_in.at[at], snaps.at[at], sems.at[0, c])

    def block_load(c):
        at = pl.ds(c * per, per)
        return pltpu.make_async_copy(blocks_in.at[at], blocks.at[at], sems.at[1, c])

    for c in range(CHUNKS):
        snap_load(c).start()
    for c in range(CHUNKS):
        block_load(c).start()
    greet()
    for c in range(CHUNKS):
        snap_load(c).wait()

    def chunk(c, carry):
        block_load(c).wait()

        def weigh(k, carry):
            row = c * per + k
            count = counts[row]
            factors = []
            sources = []
            for slot in range(slots):
                factor = blocks[row, slot]
                live = jnp.full(factor.shape, count, jnp.int32) > slot
                factors.append(jnp.where(live, factor, jnp.zeros_like(factor)))
                sources.append(snaps[cols[slot, row]])
            product = dot(jnp.concatenate(factors, axis=1), jnp.concatenate(sources, axis=0))
            weighted[pl.ds(pl.multiple_of(row * width, width), width), :] = product.astype(BF16)
            return carry

        lax.fori_loop(0, per, weigh, 0, unroll=8)
        return carry

    lax.fori_loop(0, CHUNKS, chunk, 0)
    for low in range(0, size, tall):
        gram[low : low + tall, low:] = dot(weighted[:, low : low + tall], weighted[:, low:], TN)


def unpack(flat, full):
    size = full.shape[0]
    for index, (i, j) in enumerate(upper_blocks(size // 128)):
        block = flat[index * 128 : (index + 1) * 128, :]
        full[i * 128 : (i + 1) * 128, j * 128 : (j + 1) * 128] = block
        if i != j:
            full[j * 128 : (j + 1) * 128, i * 128 : (i + 1) * 128] = block.T


def kernel(n, s, cols, counts, snaps_in, blocks_in, start_in, starts_in, out, *scratch):
    (snaps, blocks, weighted, gram, load_sems) = scratch[:5]
    y, start, starts, start_sems = scratch[47:]
    (g_own, g_out, g_in, g_all, full, vectors, t_out, t_in, g_sems, a_sems, t_sems) = scratch[5:16]
    (panels, got, p_sems, q_sems) = scratch[16:20]
    (mine_all, c_out, c_came, z_out, z_came, sum_out, sum_came, cross_all) = scratch[20:28]
    (c_sems, z_sems, s_sems) = scratch[28:31]
    (e_mine, e_got, d_mine, d_got, e_sems) = scratch[31:36]
    (x_own, x_out, x_in, x_all, xr_sems, xa_sems) = scratch[36:42]
    (cf_mine, cf_got, b_mine, b_got, b_sems) = scratch[42:47]
    snap = lax.axis_index("snap")
    space = lax.axis_index("space")
    total = s * n
    me = snap * n + space
    half = s // 2
    bit = snap % 2
    upper = bit == 1
    partner = flipped(snap, 0)
    modes = vectors.shape[1]
    size = gram.shape[0]
    rows = panels.shape[1]
    barrier = pltpu.get_barrier_semaphore()

    def device(k):
        other = lax.rem(me + k, total)
        return {"snap": other // n, "space": lax.rem(other, n)}

    small_loads = [
        pltpu.make_async_copy(start_in, start, start_sems.at[0]),
        pltpu.make_async_copy(starts_in, starts, start_sems.at[1]),
    ]

    def greet():
        for c in small_loads:
            c.start()

        def signal(k, carry):
            pl.semaphore_signal(barrier, inc=1, device_id=device(k), device_id_type=MESH)
            return carry

        lax.fori_loop(1, total, signal, 0)

    load_and_weigh(
        cols, counts, snaps_in, blocks_in, snaps, blocks, weighted, gram, load_sems, greet
    )

    share = g_in.shape[1]
    used = len(upper_blocks(size // 128)) * 128
    for index, (i, j) in enumerate(upper_blocks(size // 128)):
        block = gram[i * 128 : (i + 1) * 128, j * 128 : (j + 1) * 128]
        g_own[index * 128 : (index + 1) * 128, :] = block
        g_out[index * 128 : (index + 1) * 128, :] = block.astype(BF16)
    if used < g_own.shape[0]:
        g_own[used:, :] = jnp.zeros((g_own.shape[0] - used, 128), F32)
        g_out[used:, :] = jnp.zeros((g_own.shape[0] - used, 128), BF16)
    pl.semaphore_wait(barrier, total - 1)

    def share_of(index):
        return pl.ds(pl.multiple_of(index * share, share), share)

    spread = []
    for k in range(1, n):
        other = lax.rem(space + k, n)
        spread.append(
            remote(
                g_out.at[share_of(other)],
                g_in.at[k - 1],
                g_sems.at[0, k - 1],
                g_sems.at[1, k - 1],
                {"space": other},
            )
        )
    for c in spread:
        c.start()

    chosen = n // 2
    for c in small_loads:
        c.wait()
    begin = start[...] * (1.0 / jnp.max(jnp.abs(start[...])))
    told = [
        remote(t_out, t_in, t_sems.at[0, k - 1], t_sems.at[1, 0], {"space": lax.rem(chosen + k, n)})
        for k in range(1, n)
    ]

    @pl.when(space == chosen)
    def _():
        unpack(g_out, full)
        first = dot(full[...], begin.astype(BF16)).astype(BF16)
        cross = dot(first, first, TN)
        scale = modes / jnp.maximum(trace(cross), 1e-30)
        factor = inverse_factor(cross * scale + jnp.where(eye(modes), RIDGE, 0.0))
        t_out[...] = factor.astype(BF16)
        t_in[...] = factor.astype(BF16)
        for c in told:
            c.start()

    mine = g_own[share_of(space), :]
    for k, c in enumerate(spread):
        c.wait_recv()
        mine = mine + g_in[k].astype(F32)
    g_all[share_of(space), :] = mine.astype(BF16)
    gathered = [
        remote(
            g_all.at[share_of(space)],
            g_all.at[share_of(space)],
            a_sems.at[0, k - 1],
            a_sems.at[1, k - 1],
            {"space": lax.rem(space + k, n)},
        )
        for k in range(1, n)
    ]
    for c in gathered:
        c.start()
    for c in gathered:
        c.wait_recv()
    unpack(g_all, full)
    trace_of = 0.0
    for i in range(size // 128):
        trace_of = trace_of + trace(
            full[i * 128 : (i + 1) * 128, i * 128 : (i + 1) * 128].astype(F32)
        )
    scale = size / trace_of
    first = wide(full[...], begin) * scale

    @pl.when(space != chosen)
    def _():
        told[0].wait_recv()

    high, low = split(first)
    between = dot(high, t_in[...], NT) + dot(low, t_in[...], NT)
    vectors[...] = (wide(full[...], between) * scale).astype(BF16)

    def rows_at(q):
        return pl.ds(pl.multiple_of(q * rows, rows), rows)

    def piece(q):
        return dot(weighted[rows_at(q), :], vectors[...]).astype(BF16)

    def mine_at(q):
        return y.at[rows_at(q)]

    out_copies = []
    arrivals = []
    for h in range(1, half):
        for side in (0, 1):
            q = lax.rem(snap // 2 + h, half) * 2 + side
            source = lax.rem(snap // 2 + half - h, half) * 2 + side
            y[rows_at(q), :] = piece(q)
            send = p_sems.at[0, 2 * h + side]
            c = remote(mine_at(q), panels.at[snap], send, p_sems.at[1, 2 * h + bit], {"snap": q})
            c.start()
            out_copies.append(c)
            arrivals.append(
                remote(mine_at(q), panels.at[source], send, p_sems.at[1, 2 * h + side], {"snap": q})
            )
    pair_copies = []
    for h in range(half):
        q = lax.rem(snap // 2 + h, half) * 2 + 1 - bit
        if h == 0:
            y[rows_at(q), :] = piece(q)
        c = remote(mine_at(q), got.at[h], q_sems.at[0, h], q_sems.at[1, h], {"snap": partner})
        c.start()
        pair_copies.append(c)
    y[rows_at(snap), :] = piece(snap)

    cross = jnp.zeros((modes, modes), F32)
    for h in range(half):
        q = lax.rem(snap // 2 + h, half) * 2 + bit
        pair_copies[h].wait_recv()
        cross = cross + dot(y[rows_at(q), :], got[h], TN)
    panels[snap] = y[rows_at(snap), :]
    panels[partner] = got[0]
    cross = jnp.where(upper, cross.T, cross)
    part_rows = modes // 2

    def part_of(index):
        return pl.ds(pl.multiple_of(index * part_rows, part_rows), part_rows)

    mine_all[...] = cross
    c_out[...] = cross.astype(BF16)
    swap = remote(
        c_out.at[part_of(1 - bit)], c_came, c_sems.at[0], c_sems.at[1], {"snap": partner}
    )
    swap.start()
    moved = dot(full[...], vectors[...])
    product = wide(vectors[...].T, moved)
    square = dot(vectors[...], vectors[...], TN)
    swap.wait_recv()
    part = mine_all[part_of(bit), :] + c_came[...].astype(F32)
    z_out[...] = part.astype(BF16)
    steps = [
        remote(
            z_out,
            z_came.at[k - 1],
            z_sems.at[0, k - 1],
            z_sems.at[1, k - 1],
            {"space": lax.rem(space + k, n)},
        )
        for k in range(1, n)
    ]
    for c in steps:
        c.start()
    e_mine[...] = inverse_factor(square)
    d_mine[...] = sandwich(e_mine[...], product)
    tell = [
        remote(e_mine, e_got, e_sems.at[0, 0], e_sems.at[1, 0], {"snap": partner}),
        remote(d_mine, d_got, e_sems.at[0, 1], e_sems.at[1, 1], {"snap": partner}),
    ]
    for c in tell:
        c.start()
    for k, c in enumerate(steps):
        c.wait_recv()
        part = part + z_came[k].astype(F32)
    sum_out[...] = part.astype(BF16)
    collect = remote(sum_out, sum_came, s_sems.at[0], s_sems.at[1], {"snap": partner})
    collect.start()
    for c in tell:
        c.wait_recv()
    collect.wait_recv()
    cross_all[part_of(bit), :] = sum_out[...].astype(F32)
    cross_all[part_of(1 - bit), :] = sum_came[...].astype(F32)
    e_low = jnp.where(upper, e_got[...], e_mine[...])
    e_high = jnp.where(upper, e_mine[...], e_got[...])
    d_low = jnp.where(upper, d_got[...], d_mine[...])
    d_high = jnp.where(upper, d_mine[...], d_got[...])
    cross = dot(e_low, dot(cross_all[...], e_high, NT, HIGH), precision=HIGH)

    def merged(level, d_low, cross, d_high):
        index = s - (s >> level) + snap // (1 << (level + 1))
        pair = jnp.concatenate(
            [
                jnp.concatenate([d_low, cross], axis=1),
                jnp.concatenate([cross.T, d_high], axis=1),
            ],
            axis=0,
        )
        return pair, orthonormal(near(pair, starts[index]))

    def diagonal(pair, mixing):
        return dot(mixing, dot(pair, mixing, precision=HIGH), TN, HIGH)

    for c in arrivals:
        c.wait_recv()
    done = 0
    for low_pair in range(half):
        for high_pair in range(low_pair + 1, half):
            sides = [
                jnp.concatenate([panels[2 * p], panels[2 * p + 1]], axis=1)
                for p in (low_pair, high_pair)
            ]
            blocks_of = dot(sides[0], sides[1], TN)
            for i in range(2):
                for j in range(2):
                    at = slice(done * 128, (done + 1) * 128)
                    block = blocks_of[i * modes : (i + 1) * modes, j * modes : (j + 1) * modes]
                    x_own[at, :] = block
                    x_out[at, :] = block.astype(BF16)
                    done = done + 1
    if done * 128 < x_own.shape[0]:
        x_own[done * 128 :, :] = jnp.zeros((x_own.shape[0] - done * 128, 128), F32)
        x_out[done * 128 :, :] = jnp.zeros((x_own.shape[0] - done * 128, 128), BF16)
    x_share = x_in.shape[1]

    def x_part(index):
        return pl.ds(pl.multiple_of(index * x_share, x_share), x_share)

    def x_spread(k):
        return remote(
            x_out.at[x_part(lax.rem(me + k, total))],
            x_in.at[k - 1],
            xr_sems.at[0, k - 1],
            xr_sems.at[1, k - 1],
            device(k),
        )

    def x_gather(k):
        return remote(
            x_all.at[x_part(me)],
            x_all.at[x_part(me)],
            xa_sems.at[0, k - 1],
            xa_sems.at[1, k - 1],
            device(k),
        )

    def each(act):
        if total <= 16:
            for k in range(1, total):
                act(k)
            return

        def step(k, carry):
            act(k)
            return carry

        lax.fori_loop(1, total, step, 0)

    each(lambda k: x_spread(k).start())
    pair, mixing = merged(0, d_low, cross, d_high)

    def add(k, so_far):
        x_spread(k).wait_recv()
        return so_far + x_in[k - 1].astype(F32)

    shared = x_own[x_part(me), :]
    if total <= 16:
        for k in range(1, total):
            shared = add(k, shared)
    else:
        shared = lax.fori_loop(1, total, add, shared)
    x_all[x_part(me), :] = shared.astype(BF16)
    each(lambda k: x_gather(k).start())
    factors = [dot(e_low, mixing[:modes], TN, HIGH), dot(e_high, mixing[modes:], TN, HIGH)]
    levels = s.bit_length() - 1
    sent = []
    for level in range(1, levels):
        count = 1 << level
        for i in range(count):
            cf_mine[level - 1, i] = factors[i].astype(BF16)
        b_mine[level - 1] = diagonal(pair, mixing).astype(BF16)
        other = {"snap": flipped(snap, level)}
        pass_on = [
            remote(
                cf_mine.at[level - 1, pl.ds(0, count)],
                cf_got.at[level - 1, pl.ds(0, count)],
                b_sems.at[0, level - 1, 0],
                b_sems.at[1, level - 1, 0],
                other,
            ),
            remote(
                b_mine.at[level - 1],
                b_got.at[level - 1],
                b_sems.at[0, level - 1, 1],
                b_sems.at[1, level - 1, 1],
                other,
            ),
        ]
        for c in pass_on:
            c.start()
        sent += pass_on
        for c in pass_on:
            c.wait_recv()
        high_side = snap // count % 2 == 1
        lows, highs = [], []
        for i in range(count):
            own, theirs = cf_mine[level - 1, i], cf_got[level - 1, i]
            lows.append(jnp.where(high_side, theirs, own))
            highs.append(jnp.where(high_side, own, theirs))
        own, theirs = b_mine[level - 1].astype(F32), b_got[level - 1].astype(F32)
        d_low = jnp.where(high_side, theirs, own)
        d_high = jnp.where(high_side, own, theirs)
        if level == 1:
            each(lambda k: x_gather(k).wait_recv())
        base = snap // (2 * count) * count
        cross = jnp.zeros((modes, modes), F32)
        for a in range(count // 2):
            pa = base + a
            for i in range(2):
                right = jnp.zeros((modes, modes), F32)
                for b in range(count // 2):
                    pb = base + count // 2 + b
                    place = pa * (2 * half - pa - 1) // 2 + pb - pa - 1
                    for j in range(2):
                        at = pl.multiple_of((place * 4 + i * 2 + j) * 128, 128)
                        right = right + dot(x_all[pl.ds(at, 128), :], highs[2 * b + j])
                cross = cross + wide(lows[2 * a + i].T, right)
        pair, mixing = merged(level, d_low, cross, d_high)
        low_mix, high_mix = mixing[:modes], mixing[modes:]
        factors = [wide(f, low_mix) for f in lows] + [wide(f, high_mix) for f in highs]
    depth = jnp.concatenate([f.astype(BF16) for f in factors], axis=0)
    out[...] = dot(jnp.concatenate([panels[i] for i in range(s)], axis=1), depth).astype(BF16)

    @pl.when(space == chosen)
    def _():
        for c in told:
            c.wait_send()

    for c in spread + gathered + out_copies + pair_copies + [swap] + steps + tell + [collect] + sent:
        c.wait_send()
    each(lambda k: x_spread(k).wait_send())
    each(lambda k: x_gather(k).wait_send())


def padded(rows, parts):
    share = -(-rows // parts)
    return -(-share // 16) * 16


def local(snapshots, factor_blocks, factor_cols, factor_counts, start_basis, merge_starts):
    n = lax.axis_size("space")
    s = lax.axis_size("snap")
    total = s * n
    size, modes = start_basis.shape
    rows = snapshots.shape[0] // s
    half = s // 2
    width = factor_blocks.shape[2]
    blocked = snapshots.reshape(snapshots.shape[0] // width, width, size)
    levels = s.bit_length() - 1
    share = padded(len(upper_blocks(size // 128)) * 128, n)
    x_share = padded(4 * (half * (half - 1) // 2) * 128, total)
    dma = pltpu.SemaphoreType.DMA
    scratch = [
        pltpu.VMEM(blocked.shape, BF16),
        pltpu.VMEM(factor_blocks.shape, BF16),
        pltpu.VMEM(snapshots.shape, BF16),
        pltpu.VMEM((size, size), F32),
        dma((2, CHUNKS)),
        pltpu.VMEM((share * n, 128), F32),
        pltpu.VMEM((share * n, 128), BF16),
        pltpu.VMEM((n - 1, share, 128), BF16),
        pltpu.VMEM((share * n, 128), BF16),
        pltpu.VMEM((size, size), BF16),
        pltpu.VMEM((size, modes), BF16),
        pltpu.VMEM((modes, modes), BF16),
        pltpu.VMEM((modes, modes), BF16),
        dma((2, n - 1)),
        dma((2, n - 1)),
        dma((2, n - 1)),
        pltpu.VMEM((s, rows, modes), BF16),
        pltpu.VMEM((half, rows, modes), BF16),
        dma((2, s)),
        dma((2, half)),
        pltpu.VMEM((modes, modes), F32),
        pltpu.VMEM((modes, modes), BF16),
        pltpu.VMEM((modes // 2, modes), BF16),
        pltpu.VMEM((modes // 2, modes), BF16),
        pltpu.VMEM((n - 1, modes // 2, modes), BF16),
        pltpu.VMEM((modes // 2, modes), BF16),
        pltpu.VMEM((modes // 2, modes), BF16),
        pltpu.VMEM((modes, modes), F32),
        dma((2,)),
        dma((2, n - 1)),
        dma((2,)),
        pltpu.VMEM((modes, modes), F32),
        pltpu.VMEM((modes, modes), F32),
        pltpu.VMEM((modes, modes), F32),
        pltpu.VMEM((modes, modes), F32),
        dma((2, 2)),
        pltpu.VMEM((x_share * total, 128), F32),
        pltpu.VMEM((x_share * total, 128), BF16),
        pltpu.VMEM((total - 1, x_share, 128), BF16),
        pltpu.VMEM((x_share * total, 128), BF16),
        dma((2, total - 1)),
        dma((2, total - 1)),
        pltpu.VMEM((levels - 1, half, modes, modes), BF16),
        pltpu.VMEM((levels - 1, half, modes, modes), BF16),
        pltpu.VMEM((levels - 1, modes, modes), BF16),
        pltpu.VMEM((levels - 1, modes, modes), BF16),
        dma((2, levels - 1, 2)),
        pltpu.VMEM((snapshots.shape[0], modes), BF16),
        pltpu.VMEM(start_basis.shape, F32),
        pltpu.VMEM(merge_starts.shape, F32),
        dma((2,)),
    ]
    return pl.pallas_call(
        functools.partial(kernel, n, s),
        in_specs=[SMEM, SMEM, ANY, ANY, ANY, ANY],
        out_specs=VMEM,
        out_shape=jax.ShapeDtypeStruct((rows, modes), BF16),
        scratch_shapes=scratch,
        compiler_params=pltpu.CompilerParams(
            collective_id=0, has_side_effects=True, vmem_limit_bytes=VMEM_LIMIT
        ),
        name="modes",
    )(factor_cols.T, factor_counts, blocked, factor_blocks, start_basis, merge_starts)


def solution(mesh):
    return jax.shard_map(
        local,
        mesh=mesh,
        in_specs=(
            P("space", ("groups", "snap")),
            P("space", None, None, None),
            P("space", None),
            P("space"),
            P(("groups", "snap"), None),
            P(),
        ),
        out_specs=P(("space", "snap"), "groups"),
        check_vma=False,
    )
```

```python
import functools

import jax
import jax.numpy as jnp
from jax import lax
from jax.experimental import pallas as pl
from jax.experimental.pallas import tpu as pltpu
from jax.sharding import PartitionSpec as P

HIGH = lax.Precision.HIGHEST
MESH = pl.DeviceIdType.MESH
F32 = jnp.float32
BF16 = jnp.bfloat16
VMEM = pl.BlockSpec(memory_space=pltpu.VMEM)
SMEM = pl.BlockSpec(memory_space=pltpu.SMEM)
ANY = pl.BlockSpec(memory_space=pl.ANY)
CHUNKS = 4
VMEM_LIMIT = 56 << 20
RIDGE = 1e-4
TN = (((0,), (0,)), ((), ()))
NT = (((1,), (1,)), ((), ()))
NN = (((1,), (0,)), ((), ()))


def dot(a, b, dims=NN, precision=None):
    return lax.dot_general(a, b, dims, precision=precision, preferred_element_type=F32)


def split(x):
    high = x.astype(BF16)
    return high, (x - high.astype(F32)).astype(BF16)


def wide(a, x):
    size = x.shape[1]
    both = dot(a, jnp.concatenate(split(x), axis=1))
    return both[:, :size] + both[:, size:]


def upper_blocks(count):
    return [(i, j) for i in range(count) for j in range(i, count)]


def flipped(index, bit):
    return index + (1 - 2 * (index // (1 << bit) % 2)) * (1 << bit)


def remote(source, target, send, recv, device):
    return pltpu.make_async_remote_copy(
        src_ref=source,
        dst_ref=target,
        send_sem=send,
        recv_sem=recv,
        device_id=device,
        device_id_type=MESH,
    )


def eye(size):
    row = lax.broadcasted_iota(jnp.int32, (size, size), 0)
    col = lax.broadcasted_iota(jnp.int32, (size, size), 1)
    return row == col


def trace(x):
    return jnp.sum(jnp.where(eye(x.shape[0]), x, 0.0))


def rows_of(block):
    return pl.ds(block * 128, 128)


def eliminate(a, e, lane):
    a, e = list(a), list(e)
    groups = len(a)
    row = lax.broadcasted_iota(jnp.int32, (8, 128), 0)
    scale = [jnp.zeros((8, 128), F32)] * groups

    def spread(x, k):
        return jnp.broadcast_to(x[k : k + 1, :], (8, 128))

    for g in range(groups):
        cols = {
            h: [
                jnp.broadcast_to(a[h][:, lane + 8 * g + k : lane + 8 * g + k + 1], (8, 128))
                for k in range(8)
            ]
            for h in range(g, groups)
        }
        for k in range(0, 8, 2):
            p, q, r = spread(cols[g][k], k), spread(cols[g][k], k + 1), spread(cols[g][k + 1], k + 1)
            det = p * r - q * q
            over_det = 1.0 / det
            over_p = 1.0 / p
            i, j, l = r * over_det, q * over_det, p * over_det
            scale[g] = jnp.where(row == k, lax.rsqrt(p), scale[g])
            scale[g] = jnp.where(row == k + 1, lax.rsqrt(det * over_p), scale[g])
            a_rows = spread(a[g], k), spread(a[g], k + 1)
            e_rows = spread(e[g], k), spread(e[g], k + 1)
            heads = {
                m: (spread(cols[g][m], k), spread(cols[g][m], k + 1)) for m in range(k + 2, 8)
            }
            for h in range(g, groups):
                c, d = cols[h][k], cols[h][k + 1]
                f1 = c * i - d * j
                f2 = d * l - c * j
                if h == g:
                    f1 = jnp.where(row > k + 1, f1, jnp.where(row == k + 1, q * over_p, 0.0))
                    f2 = jnp.where(row > k + 1, f2, 0.0)
                for m in range(k + 2, 8):
                    cols[h][m] = cols[h][m] - (f1 * heads[m][0] + f2 * heads[m][1])
                a[h] = a[h] - (f1 * a_rows[0] + f2 * a_rows[1])
                e[h] = e[h] - (f1 * e_rows[0] + f2 * e_rows[1])
    return [x * s for x, s in zip(a, scale)], [x * s for x, s in zip(e, scale)]


def thirds(x):
    high = x.astype(BF16)
    rest = x - high.astype(F32)
    middle = rest.astype(BF16)
    return high, middle, (rest - middle.astype(F32)).astype(BF16)


def outer(a, b):
    a, b = thirds(a), thirds(b)
    left = jnp.concatenate([a[0], a[0], a[1], a[0], a[2], a[1]], axis=0)
    right = jnp.concatenate([b[0], b[1], b[0], b[2], b[0], b[1]], axis=0)
    return dot(left, right, TN)


def inverse_factor(cross):
    size = cross.shape[0]
    diagonal = jnp.where(eye(size), cross, 0.0)
    down = lax.rsqrt(jnp.sum(diagonal, axis=1, keepdims=True))
    along = lax.rsqrt(jnp.sum(diagonal, axis=0, keepdims=True))
    both = jnp.concatenate(
        [cross * down * along, jnp.where(eye(size), jnp.broadcast_to(along, cross.shape), 0.0)],
        axis=1,
    )
    done = []
    for p in range(size // 32):
        rows = [both[p * 32 + 8 * g : p * 32 + 8 * g + 8] for g in range(4)]
        a, e = eliminate([r[:, :size] for r in rows], [r[:, size:] for r in rows], p * 32)
        a, e = jnp.concatenate(a, axis=0), jnp.concatenate(e, axis=0)
        done.append(e)
        if p < size // 32 - 1:
            both = both - outer(a, jnp.concatenate([a, e], axis=1))
    return jnp.concatenate(done, axis=0)


def near(a, b, dims=NN):
    a, b = split(a), split(b)
    return dot(a[0], b[0], dims) + (dot(a[0], b[1], dims) + dot(a[1], b[0], dims))


def packed_factor(unit):
    half = unit.shape[0] // 2
    row = lax.broadcasted_iota(jnp.int32, (half, half), 0)
    col = lax.broadcasted_iota(jnp.int32, (half, half), 1)
    first = jnp.where(row > col, unit[:half, :half], 0.0)
    second = jnp.where(row > col, unit[half:, half:], 0.0)
    return jnp.concatenate([first + second.T, unit[half:, :half]], axis=1)


def unpacked_factor(packed):
    half = packed.shape[0]
    row = lax.broadcasted_iota(jnp.int32, (half, half), 0)
    col = lax.broadcasted_iota(jnp.int32, (half, half), 1)
    both = packed[:, :half]
    ones = (row == col).astype(F32)
    first = jnp.where(row > col, both, ones)
    second = jnp.where(row > col, both.T, ones)
    top = jnp.concatenate([first, jnp.zeros((half, half), F32)], axis=1)
    return jnp.concatenate([top, jnp.concatenate([packed[:, half:], second], axis=1)], axis=0)


def orthonormal(z):
    return near(z, inverse_factor(near(z, z, TN)), NT)


def sandwich(outer, inner):
    return dot(outer, dot(inner, outer, NT, HIGH), precision=HIGH)


def load_and_weigh(cols, counts, snaps_in, blocks_in, snaps, blocks, weighted, sems, greet, use):
    row_blocks, slots, width, _ = blocks.shape
    per = row_blocks // CHUNKS
    side = snaps[0].shape[2]

    def snap_load(h, c):
        at = pl.ds(c * per, per)
        source = snaps_in.at[at, pl.ds(0, width), pl.ds(h * side, side)]
        return pltpu.make_async_copy(source, snaps[h].at[at], sems.at[h, c])

    def block_load(c):
        at = pl.ds(c * per, per)
        return pltpu.make_async_copy(blocks_in.at[at], blocks.at[at], sems.at[2, c])

    for c in range(CHUNKS):
        snap_load(0, c).start()
    for c in range(CHUNKS):
        block_load(c).start()
    for c in range(CHUNKS):
        snap_load(1, c).start()
    greet()
    for h in (0, 1):
        for c in range(CHUNKS):
            snap_load(h, c).wait()

        def chunk(c, carry):
            if h == 0:
                block_load(c).wait()

            def weigh(k, carry):
                row = c * per + k
                count = counts[row]
                factors = []
                sources = []
                for slot in range(slots):
                    factor = blocks[row, slot]
                    live = jnp.full(factor.shape, count, jnp.int32) > slot
                    factors.append(jnp.where(live, factor, jnp.zeros_like(factor)))
                    sources.append(snaps[h][cols[slot, row]])
                product = dot(jnp.concatenate(factors, axis=1), jnp.concatenate(sources, axis=0))
                at = pl.ds(pl.multiple_of(row * width, width), width)
                weighted[at, h * side : (h + 1) * side] = product.astype(BF16)
                return carry

            lax.fori_loop(0, per, weigh, 0, unroll=8)
            return carry

        lax.fori_loop(0, CHUNKS, chunk, 0)
        use(h)


def parts_of(size):
    blocks = upper_blocks(size // 128)
    half = size // 256
    return [b for b in blocks if b[1] < half], [b for b in blocks if b[1] >= half]


def unpack(flats, full):
    for flat, blocks in zip(flats, parts_of(full.shape[0])):
        for index, (i, j) in enumerate(blocks):
            block = flat[index * 128 : (index + 1) * 128, :]
            full[i * 128 : (i + 1) * 128, j * 128 : (j + 1) * 128] = block
            if i != j:
                full[j * 128 : (j + 1) * 128, i * 128 : (i + 1) * 128] = block.T


def kernel(n, s, cols, counts, snaps_in, blocks_in, start_in, starts_in, out, *scratch):
    (blocks, weighted, load_sems) = scratch[1:4]
    snaps = scratch[0], scratch[56]
    y, start, starts, start_sems = scratch[42:46]
    firsts = (4, 46, 48, 50, 52, 54)
    g_own, g_out, g_in, g_all, g_sems, a_sems = [scratch[a : a + 2] for a in firsts]
    (full, vectors, t_out, t_in, t_sems) = scratch[6:11]
    (panels, got, p_sems, q_sems) = scratch[11:15]
    (mine_all, c_out, c_came, z_out, z_came, sum_out, sum_came, cross_all) = scratch[15:23]
    (c_sems, z_sems, s_sems) = scratch[23:26]
    (e_mine, e_got, d_mine, d_got, e_sems) = scratch[26:31]
    (x_own, x_out, x_in, x_all, xr_sems, xa_sems) = scratch[31:37]
    (cf_mine, cf_got, b_mine, b_got, b_sems) = scratch[37:42]
    snap = lax.axis_index("snap")
    space = lax.axis_index("space")
    total = s * n
    me = snap * n + space
    half = s // 2
    bit = snap % 2
    upper = bit == 1
    partner = flipped(snap, 0)
    modes = vectors.shape[1]
    size = full.shape[0]
    rows = panels.shape[1]
    barrier = pltpu.get_barrier_semaphore()

    def device(k):
        other = lax.rem(me + k, total)
        return {"snap": other // n, "space": lax.rem(other, n)}

    small_loads = [
        pltpu.make_async_copy(start_in, start, start_sems.at[0]),
        pltpu.make_async_copy(starts_in, starts, start_sems.at[1]),
    ]

    def greet():
        for c in small_loads:
            c.start()

        def signal(k, carry):
            pl.semaphore_signal(barrier, inc=1, device_id=device(k), device_id_type=MESH)
            return carry

        lax.fori_loop(1, total, signal, 0)

    def share_of(part, index):
        share = g_in[part].shape[1]
        return pl.ds(pl.multiple_of(index * share, share), share)

    def spread(part, k):
        other = lax.rem(space + k, n)
        return remote(
            g_out[part].at[share_of(part, other)],
            g_in[part].at[k - 1],
            g_sems[part].at[0, k - 1],
            g_sems[part].at[1, k - 1],
            {"space": other},
        )

    def gather(part, k):
        return remote(
            g_all[part].at[share_of(part, space)],
            g_all[part].at[share_of(part, space)],
            a_sems[part].at[0, k - 1],
            a_sems[part].at[1, k - 1],
            {"space": lax.rem(space + k, n)},
        )

    def keep(part, index, block):
        at = slice(index * 128, (index + 1) * 128)
        g_own[part][at, :] = block
        g_out[part][at, :] = block.astype(BF16)

    def part_ready(part):
        side = size // 2
        blocks = parts_of(size)[part]
        right = weighted[:, part * side : (part + 1) * side]
        for h in range(part + 1):
            product = dot(weighted[:, h * side : (h + 1) * side], right, TN)
            for index, (i, j) in enumerate(blocks):
                if i * 128 // side == h:
                    row, col = i * 128 - h * side, j * 128 - part * side
                    keep(part, index, product[row : row + 128, col : col + 128])
        used = len(blocks) * 128
        rest = g_own[part].shape[0] - used
        if rest:
            g_own[part][used:, :] = jnp.zeros((rest, 128), F32)
            g_out[part][used:, :] = jnp.zeros((rest, 128), BF16)
        if part == 0:
            pl.semaphore_wait(barrier, total - 1)
        for k in range(1, n):
            spread(part, k).start()

    def part_summed(part):
        mine = g_own[part][share_of(part, space), :]
        for k in range(1, n):
            spread(part, k).wait_recv()
            mine = mine + g_in[part][k - 1].astype(F32)
        g_all[part][share_of(part, space), :] = mine.astype(BF16)
        for k in range(1, n):
            gather(part, k).start()

    load_and_weigh(
        cols, counts, snaps_in, blocks_in, snaps, blocks, weighted, load_sems, greet, part_ready
    )
    part_summed(0)

    chosen = n // 2
    for c in small_loads:
        c.wait()
    begin = start[...] * (1.0 / jnp.max(jnp.abs(start[...])))
    told = [
        remote(t_out, t_in, t_sems.at[0, k - 1], t_sems.at[1, 0], {"space": lax.rem(chosen + k, n)})
        for k in range(1, n)
    ]

    @pl.when(space == chosen)
    def _():
        unpack(g_out, full)
        first = dot(full[...], begin.astype(BF16)).astype(BF16)
        cross = dot(first, first, TN)
        scale = modes / jnp.maximum(trace(cross), 1e-30)
        factor = inverse_factor(cross * scale + jnp.where(eye(modes), RIDGE, 0.0))
        unit = factor / jnp.sum(jnp.where(eye(modes), factor, 0.0), axis=1, keepdims=True)
        packed = packed_factor(unit).astype(BF16)
        t_out[...] = packed
        t_in[...] = packed
        for c in told:
            c.start()

    part_summed(1)

    @pl.when(space != chosen)
    def _():
        told[0].wait_recv()

    normal = unpacked_factor(t_in[...].astype(F32)).astype(BF16)
    for part in (0, 1):
        for k in range(1, n):
            gather(part, k).wait_recv()
    unpack(g_all, full)
    trace_of = 0.0
    for i in range(size // 128):
        trace_of = trace_of + trace(
            full[i * 128 : (i + 1) * 128, i * 128 : (i + 1) * 128].astype(F32)
        )
    scale = size / trace_of
    first = wide(full[...], begin) * scale

    high, low = split(first)
    between = dot(high, normal, NT) + dot(low, normal, NT)
    vectors[...] = (wide(full[...], between) * scale).astype(BF16)

    def rows_at(q):
        return pl.ds(pl.multiple_of(q * rows, rows), rows)

    def piece(q):
        return dot(weighted[rows_at(q), :], vectors[...]).astype(BF16)

    def mine_at(q):
        return y.at[rows_at(q)]

    out_copies = []
    arrivals = []
    for h in range(1, half):
        for side in (0, 1):
            q = lax.rem(snap // 2 + h, half) * 2 + side
            source = lax.rem(snap // 2 + half - h, half) * 2 + side
            y[rows_at(q), :] = piece(q)
            send = p_sems.at[0, 2 * h + side]
            c = remote(mine_at(q), panels.at[snap], send, p_sems.at[1, 2 * h + bit], {"snap": q})
            c.start()
            out_copies.append(c)
            arrivals.append(
                remote(mine_at(q), panels.at[source], send, p_sems.at[1, 2 * h + side], {"snap": q})
            )
    pair_copies = []
    for h in range(half):
        q = lax.rem(snap // 2 + h, half) * 2 + 1 - bit
        if h == 0:
            y[rows_at(q), :] = piece(q)
        c = remote(mine_at(q), got.at[h], q_sems.at[0, h], q_sems.at[1, h], {"snap": partner})
        c.start()
        pair_copies.append(c)
    y[rows_at(snap), :] = piece(snap)

    cross = jnp.zeros((modes, modes), F32)
    for h in range(half):
        q = lax.rem(snap // 2 + h, half) * 2 + bit
        pair_copies[h].wait_recv()
        cross = cross + dot(y[rows_at(q), :], got[h], TN)
    panels[snap] = y[rows_at(snap), :]
    panels[partner] = got[0]
    cross = jnp.where(upper, cross.T, cross)
    part_rows = modes // 2

    def part_of(index):
        return pl.ds(pl.multiple_of(index * part_rows, part_rows), part_rows)

    mine_all[...] = cross
    c_out[...] = cross.astype(BF16)
    swap = remote(
        c_out.at[part_of(1 - bit)], c_came, c_sems.at[0], c_sems.at[1], {"snap": partner}
    )
    swap.start()
    moved = dot(full[...], vectors[...])
    product = wide(vectors[...].T, moved)
    square = dot(vectors[...], vectors[...], TN)
    swap.wait_recv()
    part = mine_all[part_of(bit), :] + c_came[...].astype(F32)
    z_out[...] = part.astype(BF16)
    steps = [
        remote(
            z_out,
            z_came.at[k - 1],
            z_sems.at[0, k - 1],
            z_sems.at[1, k - 1],
            {"space": lax.rem(space + k, n)},
        )
        for k in range(1, n)
    ]
    for c in steps:
        c.start()
    e_mine[...] = inverse_factor(square)
    d_mine[...] = sandwich(e_mine[...], product)
    tell = [
        remote(e_mine, e_got, e_sems.at[0, 0], e_sems.at[1, 0], {"snap": partner}),
        remote(d_mine, d_got, e_sems.at[0, 1], e_sems.at[1, 1], {"snap": partner}),
    ]
    for c in tell:
        c.start()
    for k, c in enumerate(steps):
        c.wait_recv()
        part = part + z_came[k].astype(F32)
    sum_out[...] = part.astype(BF16)
    collect = remote(sum_out, sum_came, s_sems.at[0], s_sems.at[1], {"snap": partner})
    collect.start()
    for c in tell:
        c.wait_recv()
    collect.wait_recv()
    cross_all[part_of(bit), :] = sum_out[...].astype(F32)
    cross_all[part_of(1 - bit), :] = sum_came[...].astype(F32)
    e_low = jnp.where(upper, e_got[...], e_mine[...])
    e_high = jnp.where(upper, e_mine[...], e_got[...])
    d_low = jnp.where(upper, d_got[...], d_mine[...])
    d_high = jnp.where(upper, d_mine[...], d_got[...])
    cross = dot(e_low, dot(cross_all[...], e_high, NT, HIGH), precision=HIGH)

    def merged(level, d_low, cross, d_high):
        index = s - (s >> level) + snap // (1 << (level + 1))
        pair = jnp.concatenate(
            [
                jnp.concatenate([d_low, cross], axis=1),
                jnp.concatenate([cross.T, d_high], axis=1),
            ],
            axis=0,
        )
        return pair, orthonormal(near(pair, starts[index]))

    def diagonal(pair, mixing):
        return near(mixing, near(pair, mixing), TN)

    for c in arrivals:
        c.wait_recv()
    done = 0
    for low_pair in range(half):
        for high_pair in range(low_pair + 1, half):
            sides = [
                jnp.concatenate([panels[2 * p], panels[2 * p + 1]], axis=1)
                for p in (low_pair, high_pair)
            ]
            blocks_of = dot(sides[0], sides[1], TN)
            for i in range(2):
                for j in range(2):
                    at = slice(done * 128, (done + 1) * 128)
                    block = blocks_of[i * modes : (i + 1) * modes, j * modes : (j + 1) * modes]
                    x_own[at, :] = block
                    x_out[at, :] = block.astype(BF16)
                    done = done + 1
    if done * 128 < x_own.shape[0]:
        x_own[done * 128 :, :] = jnp.zeros((x_own.shape[0] - done * 128, 128), F32)
        x_out[done * 128 :, :] = jnp.zeros((x_own.shape[0] - done * 128, 128), BF16)
    x_share = x_in.shape[1]

    def x_part(index):
        return pl.ds(pl.multiple_of(index * x_share, x_share), x_share)

    def x_spread(k):
        return remote(
            x_out.at[x_part(lax.rem(me + k, total))],
            x_in.at[k - 1],
            xr_sems.at[0, k - 1],
            xr_sems.at[1, k - 1],
            device(k),
        )

    def x_gather(k):
        return remote(
            x_all.at[x_part(me)],
            x_all.at[x_part(me)],
            xa_sems.at[0, k - 1],
            xa_sems.at[1, k - 1],
            device(k),
        )

    def each(act):
        if total <= 16:
            for k in range(1, total):
                act(k)
            return

        def step(k, carry):
            act(k)
            return carry

        lax.fori_loop(1, total, step, 0)

    each(lambda k: x_spread(k).start())
    pair, mixing = merged(0, d_low, cross, d_high)

    levels = s.bit_length() - 1
    sent = []

    def tell_factors(level, factors):
        count = 1 << level
        for i in range(count):
            cf_mine[level - 1, i] = factors[i].astype(BF16)
        c = remote(
            cf_mine.at[level - 1, pl.ds(0, count)],
            cf_got.at[level - 1, pl.ds(0, count)],
            b_sems.at[0, level - 1, 0],
            b_sems.at[1, level - 1, 0],
            {"snap": flipped(snap, level)},
        )
        c.start()
        sent.append(c)
        return c

    def tell_diagonal(level, pair, mixing):
        b_mine[level - 1] = diagonal(pair, mixing).astype(BF16)
        c = remote(
            b_mine.at[level - 1],
            b_got.at[level - 1],
            b_sems.at[0, level - 1, 1],
            b_sems.at[1, level - 1, 1],
            {"snap": flipped(snap, level)},
        )
        c.start()
        sent.append(c)
        return c

    factors = [near(e_low, mixing[:modes], TN), near(e_high, mixing[modes:], TN)]
    pass_on = [tell_factors(1, factors)]

    def add(k, so_far):
        x_spread(k).wait_recv()
        return so_far + x_in[k - 1].astype(F32)

    shared = x_own[x_part(me), :]
    if total <= 16:
        for k in range(1, total):
            shared = add(k, shared)
    else:
        shared = lax.fori_loop(1, total, add, shared)
    x_all[x_part(me), :] = shared.astype(BF16)
    each(lambda k: x_gather(k).start())
    pass_on.append(tell_diagonal(1, pair, mixing))
    for level in range(1, levels):
        count = 1 << level
        if level > 1:
            pass_on = [tell_factors(level, factors), tell_diagonal(level, pair, mixing)]
        for c in pass_on:
            c.wait_recv()
        high_side = snap // count % 2 == 1
        lows, highs = [], []
        for i in range(count):
            own, theirs = cf_mine[level - 1, i], cf_got[level - 1, i]
            lows.append(jnp.where(high_side, theirs, own))
            highs.append(jnp.where(high_side, own, theirs))
        own, theirs = b_mine[level - 1].astype(F32), b_got[level - 1].astype(F32)
        d_low = jnp.where(high_side, theirs, own)
        d_high = jnp.where(high_side, own, theirs)
        if level == 1:
            each(lambda k: x_gather(k).wait_recv())
        base = snap // (2 * count) * count
        cross = jnp.zeros((modes, modes), F32)
        for a in range(count // 2):
            pa = base + a
            for i in range(2):
                right = jnp.zeros((modes, modes), F32)
                for b in range(count // 2):
                    pb = base + count // 2 + b
                    place = pa * (2 * half - pa - 1) // 2 + pb - pa - 1
                    for j in range(2):
                        at = pl.multiple_of((place * 4 + i * 2 + j) * 128, 128)
                        right = right + dot(x_all[pl.ds(at, 128), :], highs[2 * b + j])
                cross = cross + wide(lows[2 * a + i].T, right)
        pair, mixing = merged(level, d_low, cross, d_high)
        low_mix, high_mix = mixing[:modes], mixing[modes:]
        factors = [wide(f, low_mix) for f in lows] + [wide(f, high_mix) for f in highs]
    depth = jnp.concatenate([f.astype(BF16) for f in factors], axis=0)
    out[...] = dot(jnp.concatenate([panels[i] for i in range(s)], axis=1), depth).astype(BF16)

    @pl.when(space == chosen)
    def _():
        for c in told:
            c.wait_send()

    for part in (0, 1):
        for k in range(1, n):
            spread(part, k).wait_send()
            gather(part, k).wait_send()
    for c in out_copies + pair_copies + [swap] + steps + tell + [collect] + sent:
        c.wait_send()
    each(lambda k: x_spread(k).wait_send())
    each(lambda k: x_gather(k).wait_send())


def padded(rows, parts):
    share = -(-rows // parts)
    return -(-share // 16) * 16


def local(snapshots, factor_blocks, factor_cols, factor_counts, start_basis, merge_starts):
    n = lax.axis_size("space")
    s = lax.axis_size("snap")
    total = s * n
    size, modes = start_basis.shape
    rows = snapshots.shape[0] // s
    half = s // 2
    width = factor_blocks.shape[2]
    blocked = snapshots.reshape(snapshots.shape[0] // width, width, size)
    levels = s.bit_length() - 1
    x_share = padded(4 * (half * (half - 1) // 2) * 128, total)
    dma = pltpu.SemaphoreType.DMA
    shares = [padded(len(blocks) * 128, n) for blocks in parts_of(size)]
    scratch = [
        pltpu.VMEM((blocked.shape[0], width, size // 2), BF16),
        pltpu.VMEM(factor_blocks.shape, BF16),
        pltpu.VMEM(snapshots.shape, BF16),
        dma((3, CHUNKS)),
        *[pltpu.VMEM((share * n, 128), F32) for share in shares],
        pltpu.VMEM((size, size), BF16),
        pltpu.VMEM((size, modes), BF16),
        pltpu.VMEM((modes // 2, modes), BF16),
        pltpu.VMEM((modes // 2, modes), BF16),
        dma((2, n - 1)),
        pltpu.VMEM((s, rows, modes), BF16),
        pltpu.VMEM((half, rows, modes), BF16),
        dma((2, s)),
        dma((2, half)),
        pltpu.VMEM((modes, modes), F32),
        pltpu.VMEM((modes, modes), BF16),
        pltpu.VMEM((modes // 2, modes), BF16),
        pltpu.VMEM((modes // 2, modes), BF16),
        pltpu.VMEM((n - 1, modes // 2, modes), BF16),
        pltpu.VMEM((modes // 2, modes), BF16),
        pltpu.VMEM((modes // 2, modes), BF16),
        pltpu.VMEM((modes, modes), F32),
        dma((2,)),
        dma((2, n - 1)),
        dma((2,)),
        pltpu.VMEM((modes, modes), F32),
        pltpu.VMEM((modes, modes), F32),
        pltpu.VMEM((modes, modes), F32),
        pltpu.VMEM((modes, modes), F32),
        dma((2, 2)),
        pltpu.VMEM((x_share * total, 128), F32),
        pltpu.VMEM((x_share * total, 128), BF16),
        pltpu.VMEM((total - 1, x_share, 128), BF16),
        pltpu.VMEM((x_share * total, 128), BF16),
        dma((2, total - 1)),
        dma((2, total - 1)),
        pltpu.VMEM((levels - 1, half, modes, modes), BF16),
        pltpu.VMEM((levels - 1, half, modes, modes), BF16),
        pltpu.VMEM((levels - 1, modes, modes), BF16),
        pltpu.VMEM((levels - 1, modes, modes), BF16),
        dma((2, levels - 1, 2)),
        pltpu.VMEM((snapshots.shape[0], modes), BF16),
        pltpu.VMEM(start_basis.shape, F32),
        pltpu.VMEM(merge_starts.shape, F32),
        dma((2,)),
        *[pltpu.VMEM((share * n, 128), BF16) for share in shares],
        *[pltpu.VMEM((n - 1, share, 128), BF16) for share in shares],
        *[pltpu.VMEM((share * n, 128), BF16) for share in shares],
        *[dma((2, n - 1)) for share in shares],
        *[dma((2, n - 1)) for share in shares],
        pltpu.VMEM((blocked.shape[0], width, size // 2), BF16),
    ]
    return pl.pallas_call(
        functools.partial(kernel, n, s),
        in_specs=[SMEM, SMEM, ANY, ANY, ANY, ANY],
        out_specs=VMEM,
        out_shape=jax.ShapeDtypeStruct((rows, modes), BF16),
        scratch_shapes=scratch,
        compiler_params=pltpu.CompilerParams(
            collective_id=0, has_side_effects=True, vmem_limit_bytes=VMEM_LIMIT
        ),
        name="modes",
    )(factor_cols.T, factor_counts, blocked, factor_blocks, start_basis, merge_starts)


def solution(mesh):
    return jax.shard_map(
        local,
        mesh=mesh,
        in_specs=(
            P("space", ("groups", "snap")),
            P("space", None, None, None),
            P("space", None),
            P("space"),
            P(("groups", "snap"), None),
            P(),
        ),
        out_specs=P(("space", "snap"), "groups"),
        check_vma=False,
    )
```

```python
import functools

import jax
import jax.numpy as jnp
from jax import lax
from jax.experimental import pallas as pl
from jax.experimental.pallas import tpu as pltpu
from jax.sharding import PartitionSpec as P

HIGH = lax.Precision.HIGHEST
MESH = pl.DeviceIdType.MESH
F32 = jnp.float32
BF16 = jnp.bfloat16
VMEM = pl.BlockSpec(memory_space=pltpu.VMEM)
SMEM = pl.BlockSpec(memory_space=pltpu.SMEM)
ANY = pl.BlockSpec(memory_space=pl.ANY)
CHUNKS = 4
VMEM_LIMIT = 54835 * 1024
RIDGE = 1e-4
TN = (((0,), (0,)), ((), ()))
NT = (((1,), (1,)), ((), ()))
NN = (((1,), (0,)), ((), ()))


def dot(a, b, dims=NN, precision=None):
    return lax.dot_general(a, b, dims, precision=precision, preferred_element_type=F32)


def split(x):
    high = x.astype(BF16)
    return high, (x - high.astype(F32)).astype(BF16)


def wide(a, x):
    size = x.shape[1]
    both = dot(a, jnp.concatenate(split(x), axis=1))
    return both[:, :size] + both[:, size:]


def upper_blocks(count):
    return [(i, j) for i in range(count) for j in range(i, count)]


def flipped(index, bit):
    return index + (1 - 2 * (index // (1 << bit) % 2)) * (1 << bit)


def remote(source, target, send, recv, device):
    return pltpu.make_async_remote_copy(
        src_ref=source,
        dst_ref=target,
        send_sem=send,
        recv_sem=recv,
        device_id=device,
        device_id_type=MESH,
    )


def eye(size):
    row = lax.broadcasted_iota(jnp.int32, (size, size), 0)
    col = lax.broadcasted_iota(jnp.int32, (size, size), 1)
    return row == col


def trace(x):
    return jnp.sum(jnp.where(eye(x.shape[0]), x, 0.0))


def rows_of(block):
    return pl.ds(block * 128, 128)


def eliminate(a, e, lane):
    a, e = list(a), list(e)
    groups = len(a)
    row = lax.broadcasted_iota(jnp.int32, (8, 128), 0)
    scale = [jnp.zeros((8, 128), F32)] * groups

    def spread(x, k):
        return jnp.broadcast_to(x[k : k + 1, :], (8, 128))

    for g in range(groups):
        cols = {
            h: [
                jnp.broadcast_to(a[h][:, lane + 8 * g + k : lane + 8 * g + k + 1], (8, 128))
                for k in range(8)
            ]
            for h in range(g, groups)
        }
        for k in range(0, 8, 2):
            p, q, r = spread(cols[g][k], k), spread(cols[g][k], k + 1), spread(cols[g][k + 1], k + 1)
            det = p * r - q * q
            over_det = 1.0 / det
            over_p = 1.0 / p
            i, j, l = r * over_det, q * over_det, p * over_det
            scale[g] = jnp.where(row == k, lax.rsqrt(p), scale[g])
            scale[g] = jnp.where(row == k + 1, lax.rsqrt(det * over_p), scale[g])
            a_rows = spread(a[g], k), spread(a[g], k + 1)
            e_rows = spread(e[g], k), spread(e[g], k + 1)
            heads = {
                m: (spread(cols[g][m], k), spread(cols[g][m], k + 1)) for m in range(k + 2, 8)
            }
            for h in range(g, groups):
                c, d = cols[h][k], cols[h][k + 1]
                f1 = c * i - d * j
                f2 = d * l - c * j
                if h == g:
                    f1 = jnp.where(row > k + 1, f1, jnp.where(row == k + 1, q * over_p, 0.0))
                    f2 = jnp.where(row > k + 1, f2, 0.0)
                for m in range(k + 2, 8):
                    cols[h][m] = cols[h][m] - (f1 * heads[m][0] + f2 * heads[m][1])
                a[h] = a[h] - (f1 * a_rows[0] + f2 * a_rows[1])
                e[h] = e[h] - (f1 * e_rows[0] + f2 * e_rows[1])
    return [x * s for x, s in zip(a, scale)], [x * s for x, s in zip(e, scale)]


def thirds(x):
    high = x.astype(BF16)
    rest = x - high.astype(F32)
    middle = rest.astype(BF16)
    return high, middle, (rest - middle.astype(F32)).astype(BF16)


def outer(a, b):
    a, b = thirds(a), thirds(b)
    left = jnp.concatenate([a[0], a[0], a[1], a[0], a[2], a[1]], axis=0)
    right = jnp.concatenate([b[0], b[1], b[0], b[2], b[0], b[1]], axis=0)
    return dot(left, right, TN)


def inverse_factor(cross):
    size = cross.shape[0]
    diagonal = jnp.where(eye(size), cross, 0.0)
    down = lax.rsqrt(jnp.sum(diagonal, axis=1, keepdims=True))
    along = lax.rsqrt(jnp.sum(diagonal, axis=0, keepdims=True))
    both = jnp.concatenate(
        [cross * down * along, jnp.where(eye(size), jnp.broadcast_to(along, cross.shape), 0.0)],
        axis=1,
    )
    done = []
    for p in range(size // 32):
        rows = [both[p * 32 + 8 * g : p * 32 + 8 * g + 8] for g in range(4)]
        a, e = eliminate([r[:, :size] for r in rows], [r[:, size:] for r in rows], p * 32)
        a, e = jnp.concatenate(a, axis=0), jnp.concatenate(e, axis=0)
        done.append(e)
        if p < size // 32 - 1:
            both = both - outer(a, jnp.concatenate([a, e], axis=1))
    return jnp.concatenate(done, axis=0)


def near(a, b, dims=NN):
    a, b = split(a), split(b)
    return dot(a[0], b[0], dims) + (dot(a[0], b[1], dims) + dot(a[1], b[0], dims))


def packed_factor(unit):
    half = unit.shape[0] // 2
    row = lax.broadcasted_iota(jnp.int32, (half, half), 0)
    col = lax.broadcasted_iota(jnp.int32, (half, half), 1)
    first = jnp.where(row > col, unit[:half, :half], 0.0)
    second = jnp.where(row > col, unit[half:, half:], 0.0)
    return jnp.concatenate([first + second.T, unit[half:, :half]], axis=1)


def unpacked_factor(packed):
    half = packed.shape[0]
    row = lax.broadcasted_iota(jnp.int32, (half, half), 0)
    col = lax.broadcasted_iota(jnp.int32, (half, half), 1)
    both = packed[:, :half]
    ones = (row == col).astype(F32)
    first = jnp.where(row > col, both, ones)
    second = jnp.where(row > col, both.T, ones)
    top = jnp.concatenate([first, jnp.zeros((half, half), F32)], axis=1)
    return jnp.concatenate([top, jnp.concatenate([packed[:, half:], second], axis=1)], axis=0)


def orthonormal(z):
    return near(z, inverse_factor(near(z, z, TN)), NT)


def sandwich(outer, inner):
    return dot(outer, dot(inner, outer, NT, HIGH), precision=HIGH)


def load_and_weigh(table, snaps_in, blocks_in, snaps, blocks, weighted, sems, greet, use):
    row_blocks, slots, width, _ = blocks.shape
    per = row_blocks // CHUNKS
    side = snaps[0].shape[2]

    def snap_load(h, c):
        at = pl.ds(c * per, per)
        source = snaps_in.at[at, pl.ds(0, width), pl.ds(h * side, side)]
        return pltpu.make_async_copy(source, snaps[h].at[at], sems.at[h, c])

    def block_load(c):
        at = pl.ds(c * per, per)
        return pltpu.make_async_copy(blocks_in.at[at], blocks.at[at], sems.at[2, c])

    for c in range(CHUNKS):
        snap_load(0, c).start()
    for c in range(CHUNKS):
        block_load(c).start()
    for c in range(CHUNKS):
        snap_load(1, c).start()
    greet()
    for h in (0, 1):
        for c in range(CHUNKS):
            snap_load(h, c).wait()

        def chunk(c, carry):
            if h == 0:
                block_load(c).wait()

            def weigh(k, carry):
                row = c * per + k
                count = table[slots, row]
                factors = []
                sources = []
                for slot in range(slots):
                    factor = blocks[row, slot]
                    live = jnp.full(factor.shape, count, jnp.int32) > slot
                    factors.append(jnp.where(live, factor, jnp.zeros_like(factor)))
                    sources.append(snaps[h][table[slot, row]])
                product = dot(jnp.concatenate(factors, axis=1), jnp.concatenate(sources, axis=0))
                at = pl.ds(pl.multiple_of(row * width, width), width)
                weighted[at, h * side : (h + 1) * side] = product.astype(BF16)
                return carry

            lax.fori_loop(0, per, weigh, 0, unroll=8)
            return carry

        lax.fori_loop(0, CHUNKS, chunk, 0)
        use(h)


def parts_of(size):
    blocks = upper_blocks(size // 128)
    half = size // 256
    return [b for b in blocks if b[1] < half], [b for b in blocks if b[1] >= half]


def unpack(flats, full):
    for flat, blocks in zip(flats, parts_of(full.shape[0])):
        for index, (i, j) in enumerate(blocks):
            block = flat[index * 128 : (index + 1) * 128, :]
            full[i * 128 : (i + 1) * 128, j * 128 : (j + 1) * 128] = block
            if i != j:
                full[j * 128 : (j + 1) * 128, i * 128 : (i + 1) * 128] = block.T


def kernel(n, s, table, snaps_in, blocks_in, start_in, starts_in, out, *scratch):
    (blocks, weighted, load_sems) = scratch[1:4]
    snaps = scratch[0], scratch[56]
    y, start, starts, start_sems = scratch[42:46]
    firsts = (4, 46, 48, 50, 52, 54)
    g_own, g_out, g_in, g_all, g_sems, a_sems = [scratch[a : a + 2] for a in firsts]
    (full, vectors, t_out, t_in, t_sems) = scratch[6:11]
    (panels, got, p_sems, q_sems) = scratch[11:15]
    (mine_all, c_out, c_came, z_out, z_came, sum_out, sum_came, cross_all) = scratch[15:23]
    (c_sems, z_sems, s_sems) = scratch[23:26]
    (e_mine, e_got, d_mine, d_got, e_sems) = scratch[26:31]
    (x_own, x_out, x_in, x_all, xr_sems, xa_sems) = scratch[31:37]
    (cf_mine, cf_got, b_mine, b_got, b_sems) = scratch[37:42]
    snap = lax.axis_index("snap")
    space = lax.axis_index("space")
    total = s * n
    me = snap * n + space
    half = s // 2
    bit = snap % 2
    upper = bit == 1
    partner = flipped(snap, 0)
    modes = vectors.shape[1]
    size = full.shape[0]
    rows = panels.shape[1]
    barrier = pltpu.get_barrier_semaphore()

    def device(k):
        other = lax.rem(me + k, total)
        return {"snap": other // n, "space": lax.rem(other, n)}

    small_loads = [
        pltpu.make_async_copy(start_in, start, start_sems.at[0]),
        pltpu.make_async_copy(starts_in, starts, start_sems.at[1]),
    ]

    def greet():
        for c in small_loads:
            c.start()

        def signal(k, carry):
            pl.semaphore_signal(barrier, inc=1, device_id=device(k), device_id_type=MESH)
            return carry

        lax.fori_loop(1, total, signal, 0)

    def share_of(part, index):
        share = g_in[part].shape[1]
        return pl.ds(pl.multiple_of(index * share, share), share)

    def spread(part, k):
        other = lax.rem(space + k, n)
        return remote(
            g_out[part].at[share_of(part, other)],
            g_in[part].at[k - 1],
            g_sems[part].at[0, k - 1],
            g_sems[part].at[1, k - 1],
            {"space": other},
        )

    def gather(part, k):
        return remote(
            g_all[part].at[share_of(part, space)],
            g_all[part].at[share_of(part, space)],
            a_sems[part].at[0, k - 1],
            a_sems[part].at[1, k - 1],
            {"space": lax.rem(space + k, n)},
        )

    def keep(part, index, block):
        at = slice(index * 128, (index + 1) * 128)
        g_own[part][at, :] = block
        g_out[part][at, :] = block.astype(BF16)

    def part_ready(part):
        side = size // 2
        blocks = parts_of(size)[part]
        right = weighted[:, part * side : (part + 1) * side]
        for h in range(part + 1):
            product = dot(weighted[:, h * side : (h + 1) * side], right, TN)
            for index, (i, j) in enumerate(blocks):
                if i * 128 // side == h:
                    row, col = i * 128 - h * side, j * 128 - part * side
                    keep(part, index, product[row : row + 128, col : col + 128])
        used = len(blocks) * 128
        rest = g_own[part].shape[0] - used
        if rest:
            g_own[part][used:, :] = jnp.zeros((rest, 128), F32)
            g_out[part][used:, :] = jnp.zeros((rest, 128), BF16)
        if part == 0:
            pl.semaphore_wait(barrier, total - 1)
        for k in range(1, n):
            spread(part, k).start()

    def part_summed(part):
        mine = g_own[part][share_of(part, space), :]
        for k in range(1, n):
            spread(part, k).wait_recv()
            mine = mine + g_in[part][k - 1].astype(F32)
        g_all[part][share_of(part, space), :] = mine.astype(BF16)
        for k in range(1, n):
            gather(part, k).start()

    load_and_weigh(
        table, snaps_in, blocks_in, snaps, blocks, weighted, load_sems, greet, part_ready
    )
    part_summed(0)

    chosen = n // 2
    for c in small_loads:
        c.wait()
    begin = start[...] * (1.0 / jnp.max(jnp.abs(start[...])))
    told = [
        remote(t_out, t_in, t_sems.at[0, k - 1], t_sems.at[1, 0], {"space": lax.rem(chosen + k, n)})
        for k in range(1, n)
    ]

    @pl.when(space == chosen)
    def _():
        unpack(g_out, full)
        first = dot(full[...], begin.astype(BF16)).astype(BF16)
        cross = dot(first, first, TN)
        scale = modes / jnp.maximum(trace(cross), 1e-30)
        factor = inverse_factor(cross * scale + jnp.where(eye(modes), RIDGE, 0.0))
        unit = factor / jnp.sum(jnp.where(eye(modes), factor, 0.0), axis=1, keepdims=True)
        packed = packed_factor(unit).astype(BF16)
        t_out[...] = packed
        t_in[...] = packed
        for c in told:
            c.start()

    part_summed(1)

    @pl.when(space != chosen)
    def _():
        told[0].wait_recv()

    normal = unpacked_factor(t_in[...].astype(F32)).astype(BF16)
    for part in (0, 1):
        for k in range(1, n):
            gather(part, k).wait_recv()
    unpack(g_all, full)
    trace_of = 0.0
    for i in range(size // 128):
        trace_of = trace_of + trace(
            full[i * 128 : (i + 1) * 128, i * 128 : (i + 1) * 128].astype(F32)
        )
    scale = size / trace_of
    first = wide(full[...], begin) * scale

    high, low = split(first)
    between = dot(high, normal, NT) + dot(low, normal, NT)
    vectors[...] = (wide(full[...], between) * scale).astype(BF16)

    def rows_at(q):
        return pl.ds(pl.multiple_of(q * rows, rows), rows)

    def piece(q):
        return dot(weighted[rows_at(q), :], vectors[...]).astype(BF16)

    def mine_at(q):
        return y.at[rows_at(q)]

    out_copies = []
    arrivals = []
    for h in range(1, half):
        for side in (0, 1):
            q = lax.rem(snap // 2 + h, half) * 2 + side
            source = lax.rem(snap // 2 + half - h, half) * 2 + side
            y[rows_at(q), :] = piece(q)
            send = p_sems.at[0, 2 * h + side]
            c = remote(mine_at(q), panels.at[snap], send, p_sems.at[1, 2 * h + bit], {"snap": q})
            c.start()
            out_copies.append(c)
            arrivals.append(
                remote(mine_at(q), panels.at[source], send, p_sems.at[1, 2 * h + side], {"snap": q})
            )
    pair_copies = []
    for h in range(half):
        q = lax.rem(snap // 2 + h, half) * 2 + 1 - bit
        if h == 0:
            y[rows_at(q), :] = piece(q)
        c = remote(mine_at(q), got.at[h], q_sems.at[0, h], q_sems.at[1, h], {"snap": partner})
        c.start()
        pair_copies.append(c)
    y[rows_at(snap), :] = piece(snap)

    cross = jnp.zeros((modes, modes), F32)
    for h in range(half):
        q = lax.rem(snap // 2 + h, half) * 2 + bit
        pair_copies[h].wait_recv()
        cross = cross + dot(y[rows_at(q), :], got[h], TN)
    panels[snap] = y[rows_at(snap), :]
    panels[partner] = got[0]
    cross = jnp.where(upper, cross.T, cross)
    part_rows = modes // 2

    def part_of(index):
        return pl.ds(pl.multiple_of(index * part_rows, part_rows), part_rows)

    mine_all[...] = cross
    c_out[...] = cross.astype(BF16)
    swap = remote(
        c_out.at[part_of(1 - bit)], c_came, c_sems.at[0], c_sems.at[1], {"snap": partner}
    )
    swap.start()
    moved = dot(full[...], vectors[...])
    product = wide(vectors[...].T, moved)
    square = dot(vectors[...], vectors[...], TN)
    swap.wait_recv()
    part = mine_all[part_of(bit), :] + c_came[...].astype(F32)
    z_out[...] = part.astype(BF16)
    steps = [
        remote(
            z_out,
            z_came.at[k - 1],
            z_sems.at[0, k - 1],
            z_sems.at[1, k - 1],
            {"space": lax.rem(space + k, n)},
        )
        for k in range(1, n)
    ]
    for c in steps:
        c.start()
    e_mine[...] = inverse_factor(square)
    d_mine[...] = sandwich(e_mine[...], product)
    tell = [
        remote(e_mine, e_got, e_sems.at[0, 0], e_sems.at[1, 0], {"snap": partner}),
        remote(d_mine, d_got, e_sems.at[0, 1], e_sems.at[1, 1], {"snap": partner}),
    ]
    for c in tell:
        c.start()
    for k, c in enumerate(steps):
        c.wait_recv()
        part = part + z_came[k].astype(F32)
    sum_out[...] = part.astype(BF16)
    collect = remote(sum_out, sum_came, s_sems.at[0], s_sems.at[1], {"snap": partner})
    collect.start()
    for c in tell:
        c.wait_recv()
    collect.wait_recv()
    cross_all[part_of(bit), :] = sum_out[...].astype(F32)
    cross_all[part_of(1 - bit), :] = sum_came[...].astype(F32)
    e_low = jnp.where(upper, e_got[...], e_mine[...])
    e_high = jnp.where(upper, e_mine[...], e_got[...])
    d_low = jnp.where(upper, d_got[...], d_mine[...])
    d_high = jnp.where(upper, d_mine[...], d_got[...])
    cross = dot(e_low, dot(cross_all[...], e_high, NT, HIGH), precision=HIGH)

    def merged(level, d_low, cross, d_high):
        index = s - (s >> level) + snap // (1 << (level + 1))
        pair = jnp.concatenate(
            [
                jnp.concatenate([d_low, cross], axis=1),
                jnp.concatenate([cross.T, d_high], axis=1),
            ],
            axis=0,
        )
        return pair, orthonormal(near(pair, starts[index]))

    def diagonal(pair, mixing):
        return near(mixing, near(pair, mixing), TN)

    for c in arrivals:
        c.wait_recv()
    done = 0
    for low_pair in range(half):
        for high_pair in range(low_pair + 1, half):
            sides = [
                jnp.concatenate([panels[2 * p], panels[2 * p + 1]], axis=1)
                for p in (low_pair, high_pair)
            ]
            blocks_of = dot(sides[0], sides[1], TN)
            for i in range(2):
                for j in range(2):
                    at = slice(done * 128, (done + 1) * 128)
                    block = blocks_of[i * modes : (i + 1) * modes, j * modes : (j + 1) * modes]
                    x_own[at, :] = block
                    x_out[at, :] = block.astype(BF16)
                    done = done + 1
    if done * 128 < x_own.shape[0]:
        x_own[done * 128 :, :] = jnp.zeros((x_own.shape[0] - done * 128, 128), F32)
        x_out[done * 128 :, :] = jnp.zeros((x_own.shape[0] - done * 128, 128), BF16)
    x_share = x_in.shape[1]

    def x_part(index):
        return pl.ds(pl.multiple_of(index * x_share, x_share), x_share)

    def x_spread(k):
        return remote(
            x_out.at[x_part(lax.rem(me + k, total))],
            x_in.at[k - 1],
            xr_sems.at[0, k - 1],
            xr_sems.at[1, k - 1],
            device(k),
        )

    def x_gather(k):
        return remote(
            x_all.at[x_part(me)],
            x_all.at[x_part(me)],
            xa_sems.at[0, k - 1],
            xa_sems.at[1, k - 1],
            device(k),
        )

    def each(act):
        if total <= 16:
            for k in range(1, total):
                act(k)
            return

        def step(k, carry):
            act(k)
            return carry

        lax.fori_loop(1, total, step, 0)

    each(lambda k: x_spread(k).start())
    pair, mixing = merged(0, d_low, cross, d_high)

    levels = s.bit_length() - 1
    sent = []

    def tell_factors(level, factors):
        count = 1 << level
        for i in range(count):
            cf_mine[level - 1, i] = factors[i].astype(BF16)
        c = remote(
            cf_mine.at[level - 1, pl.ds(0, count)],
            cf_got.at[level - 1, pl.ds(0, count)],
            b_sems.at[0, level - 1, 0],
            b_sems.at[1, level - 1, 0],
            {"snap": flipped(snap, level)},
        )
        c.start()
        sent.append(c)
        return c

    def tell_diagonal(level, pair, mixing):
        b_mine[level - 1] = diagonal(pair, mixing).astype(BF16)
        c = remote(
            b_mine.at[level - 1],
            b_got.at[level - 1],
            b_sems.at[0, level - 1, 1],
            b_sems.at[1, level - 1, 1],
            {"snap": flipped(snap, level)},
        )
        c.start()
        sent.append(c)
        return c

    factors = [near(e_low, mixing[:modes], TN), near(e_high, mixing[modes:], TN)]
    pass_on = [tell_factors(1, factors)]

    def add(k, so_far):
        x_spread(k).wait_recv()
        return so_far + x_in[k - 1].astype(F32)

    shared = x_own[x_part(me), :]
    if total <= 16:
        for k in range(1, total):
            shared = add(k, shared)
    else:
        shared = lax.fori_loop(1, total, add, shared)
    x_all[x_part(me), :] = shared.astype(BF16)
    each(lambda k: x_gather(k).start())
    pass_on.append(tell_diagonal(1, pair, mixing))
    for level in range(1, levels):
        count = 1 << level
        if level > 1:
            pass_on = [tell_factors(level, factors), tell_diagonal(level, pair, mixing)]
        for c in pass_on:
            c.wait_recv()
        high_side = snap // count % 2 == 1
        lows, highs = [], []
        for i in range(count):
            own, theirs = cf_mine[level - 1, i], cf_got[level - 1, i]
            lows.append(jnp.where(high_side, theirs, own))
            highs.append(jnp.where(high_side, own, theirs))
        own, theirs = b_mine[level - 1].astype(F32), b_got[level - 1].astype(F32)
        d_low = jnp.where(high_side, theirs, own)
        d_high = jnp.where(high_side, own, theirs)
        if level == 1:
            each(lambda k: x_gather(k).wait_recv())
        base = snap // (2 * count) * count
        cross = jnp.zeros((modes, modes), F32)
        for a in range(count // 2):
            pa = base + a
            for i in range(2):
                right = jnp.zeros((modes, modes), F32)
                for b in range(count // 2):
                    pb = base + count // 2 + b
                    place = pa * (2 * half - pa - 1) // 2 + pb - pa - 1
                    for j in range(2):
                        at = pl.multiple_of((place * 4 + i * 2 + j) * 128, 128)
                        right = right + dot(x_all[pl.ds(at, 128), :], highs[2 * b + j])
                cross = cross + wide(lows[2 * a + i].T, right)
        pair, mixing = merged(level, d_low, cross, d_high)
        low_mix, high_mix = mixing[:modes], mixing[modes:]
        factors = [wide(f, low_mix) for f in lows] + [wide(f, high_mix) for f in highs]
    depth = jnp.concatenate([f.astype(BF16) for f in factors], axis=0)
    out[...] = dot(jnp.concatenate([panels[i] for i in range(s)], axis=1), depth).astype(BF16)

    @pl.when(space == chosen)
    def _():
        for c in told:
            c.wait_send()

    for part in (0, 1):
        for k in range(1, n):
            spread(part, k).wait_send()
            gather(part, k).wait_send()
    for c in out_copies + pair_copies + [swap] + steps + tell + [collect] + sent:
        c.wait_send()
    each(lambda k: x_spread(k).wait_send())
    each(lambda k: x_gather(k).wait_send())


def padded(rows, parts):
    share = -(-rows // parts)
    return -(-share // 16) * 16


def local(snapshots, factor_blocks, factor_cols, factor_counts, start_basis, merge_starts):
    n = lax.axis_size("space")
    s = lax.axis_size("snap")
    total = s * n
    size, modes = start_basis.shape
    rows = snapshots.shape[0] // s
    half = s // 2
    width = factor_blocks.shape[2]
    blocked = snapshots.reshape(snapshots.shape[0] // width, width, size)
    levels = s.bit_length() - 1
    x_share = padded(4 * (half * (half - 1) // 2) * 128, total)
    dma = pltpu.SemaphoreType.DMA
    shares = [padded(len(blocks) * 128, n) for blocks in parts_of(size)]
    table = jnp.concatenate([factor_cols.T, factor_counts[None]])
    scratch = [
        pltpu.VMEM((blocked.shape[0], width, size // 2), BF16),
        pltpu.VMEM(factor_blocks.shape, BF16),
        pltpu.VMEM(snapshots.shape, BF16),
        dma((3, CHUNKS)),
        *[pltpu.VMEM((share * n, 128), F32) for share in shares],
        pltpu.VMEM((size, size), BF16),
        pltpu.VMEM((size, modes), BF16),
        pltpu.VMEM((modes // 2, modes), BF16),
        pltpu.VMEM((modes // 2, modes), BF16),
        dma((2, n - 1)),
        pltpu.VMEM((s, rows, modes), BF16),
        pltpu.VMEM((half, rows, modes), BF16),
        dma((2, s)),
        dma((2, half)),
        pltpu.VMEM((modes, modes), F32),
        pltpu.VMEM((modes, modes), BF16),
        pltpu.VMEM((modes // 2, modes), BF16),
        pltpu.VMEM((modes // 2, modes), BF16),
        pltpu.VMEM((n - 1, modes // 2, modes), BF16),
        pltpu.VMEM((modes // 2, modes), BF16),
        pltpu.VMEM((modes // 2, modes), BF16),
        pltpu.VMEM((modes, modes), F32),
        dma((2,)),
        dma((2, n - 1)),
        dma((2,)),
        pltpu.VMEM((modes, modes), F32),
        pltpu.VMEM((modes, modes), F32),
        pltpu.VMEM((modes, modes), F32),
        pltpu.VMEM((modes, modes), F32),
        dma((2, 2)),
        pltpu.VMEM((x_share * total, 128), F32),
        pltpu.VMEM((x_share * total, 128), BF16),
        pltpu.VMEM((total - 1, x_share, 128), BF16),
        pltpu.VMEM((x_share * total, 128), BF16),
        dma((2, total - 1)),
        dma((2, total - 1)),
        pltpu.VMEM((levels - 1, half, modes, modes), BF16),
        pltpu.VMEM((levels - 1, half, modes, modes), BF16),
        pltpu.VMEM((levels - 1, modes, modes), BF16),
        pltpu.VMEM((levels - 1, modes, modes), BF16),
        dma((2, levels - 1, 2)),
        pltpu.VMEM((snapshots.shape[0], modes), BF16),
        pltpu.VMEM(start_basis.shape, F32),
        pltpu.VMEM(merge_starts.shape, F32),
        dma((2,)),
        *[pltpu.VMEM((share * n, 128), BF16) for share in shares],
        *[pltpu.VMEM((n - 1, share, 128), BF16) for share in shares],
        *[pltpu.VMEM((share * n, 128), BF16) for share in shares],
        *[dma((2, n - 1)) for share in shares],
        *[dma((2, n - 1)) for share in shares],
        pltpu.VMEM((blocked.shape[0], width, size // 2), BF16),
    ]
    return pl.pallas_call(
        functools.partial(kernel, n, s),
        in_specs=[SMEM, ANY, ANY, ANY, ANY],
        out_specs=VMEM,
        out_shape=jax.ShapeDtypeStruct((rows, modes), BF16),
        scratch_shapes=scratch,
        compiler_params=pltpu.CompilerParams(
            collective_id=0, has_side_effects=True, vmem_limit_bytes=VMEM_LIMIT
        ),
        name="modes",
    )(table, blocked, factor_blocks, start_basis, merge_starts)


def solution(mesh):
    return jax.shard_map(
        local,
        mesh=mesh,
        in_specs=(
            P("space", ("groups", "snap")),
            P("space", None, None, None),
            P("space", None),
            P("space"),
            P(("groups", "snap"), None),
            P(),
        ),
        out_specs=P(("space", "snap"), "groups"),
        check_vma=False,
    )
```

```python
import functools

import jax
import jax.numpy as jnp
from jax import lax
from jax.experimental import pallas as pl
from jax.experimental.pallas import tpu as pltpu
from jax.sharding import PartitionSpec as P

HIGH = lax.Precision.HIGHEST
MESH = pl.DeviceIdType.MESH
F32 = jnp.float32
BF16 = jnp.bfloat16
VMEM = pl.BlockSpec(memory_space=pltpu.VMEM)
SMEM = pl.BlockSpec(memory_space=pltpu.SMEM)
ANY = pl.BlockSpec(memory_space=pl.ANY)
CHUNKS = 4
VMEM_LIMIT = 54835 * 1024
RIDGE = 1e-4
TN = (((0,), (0,)), ((), ()))
NT = (((1,), (1,)), ((), ()))
NN = (((1,), (0,)), ((), ()))


def dot(a, b, dims=NN, precision=None):
    return lax.dot_general(a, b, dims, precision=precision, preferred_element_type=F32)


def split(x):
    high = x.astype(BF16)
    return high, (x - high.astype(F32)).astype(BF16)


def wide(a, x):
    size = x.shape[1]
    both = dot(a, jnp.concatenate(split(x), axis=1))
    return both[:, :size] + both[:, size:]


def upper_blocks(count):
    return [(i, j) for i in range(count) for j in range(i, count)]


def flipped(index, bit):
    return index + (1 - 2 * (index // (1 << bit) % 2)) * (1 << bit)


def remote(source, target, send, recv, device):
    return pltpu.make_async_remote_copy(
        src_ref=source,
        dst_ref=target,
        send_sem=send,
        recv_sem=recv,
        device_id=device,
        device_id_type=MESH,
    )


def eye(size):
    row = lax.broadcasted_iota(jnp.int32, (size, size), 0)
    col = lax.broadcasted_iota(jnp.int32, (size, size), 1)
    return row == col


def trace(x):
    return jnp.sum(jnp.where(eye(x.shape[0]), x, 0.0))


def rows_of(block):
    return pl.ds(block * 128, 128)


def eliminate(a, e, lane):
    a, e = list(a), list(e)
    groups = len(a)
    row = lax.broadcasted_iota(jnp.int32, (8, 128), 0)
    scale = [jnp.zeros((8, 128), F32)] * groups

    def spread(x, k):
        return jnp.broadcast_to(x[k : k + 1, :], (8, 128))

    for g in range(groups):
        cols = {
            h: [
                jnp.broadcast_to(a[h][:, lane + 8 * g + k : lane + 8 * g + k + 1], (8, 128))
                for k in range(8)
            ]
            for h in range(g, groups)
        }
        for k in range(0, 8, 2):
            p, q, r = spread(cols[g][k], k), spread(cols[g][k], k + 1), spread(cols[g][k + 1], k + 1)
            det = p * r - q * q
            over_det = 1.0 / det
            over_p = 1.0 / p
            i, j, l = r * over_det, q * over_det, p * over_det
            scale[g] = jnp.where(row == k, lax.rsqrt(p), scale[g])
            scale[g] = jnp.where(row == k + 1, lax.rsqrt(det * over_p), scale[g])
            a_rows = spread(a[g], k), spread(a[g], k + 1)
            e_rows = spread(e[g], k), spread(e[g], k + 1)
            heads = {
                m: (spread(cols[g][m], k), spread(cols[g][m], k + 1)) for m in range(k + 2, 8)
            }
            for h in range(g, groups):
                c, d = cols[h][k], cols[h][k + 1]
                f1 = c * i - d * j
                f2 = d * l - c * j
                if h == g:
                    f1 = jnp.where(row > k + 1, f1, jnp.where(row == k + 1, q * over_p, 0.0))
                    f2 = jnp.where(row > k + 1, f2, 0.0)
                for m in range(k + 2, 8):
                    cols[h][m] = cols[h][m] - (f1 * heads[m][0] + f2 * heads[m][1])
                a[h] = a[h] - (f1 * a_rows[0] + f2 * a_rows[1])
                e[h] = e[h] - (f1 * e_rows[0] + f2 * e_rows[1])
    return [x * s for x, s in zip(a, scale)], [x * s for x, s in zip(e, scale)]


def thirds(x):
    high = x.astype(BF16)
    rest = x - high.astype(F32)
    middle = rest.astype(BF16)
    return high, middle, (rest - middle.astype(F32)).astype(BF16)


def outer(a, b):
    a, b = thirds(a), thirds(b)
    left = jnp.concatenate([a[0], a[0], a[1], a[0], a[2], a[1]], axis=0)
    right = jnp.concatenate([b[0], b[1], b[0], b[2], b[0], b[1]], axis=0)
    return dot(left, right, TN)


def inverse_factor(cross):
    size = cross.shape[0]
    diagonal = jnp.where(eye(size), cross, 0.0)
    down = lax.rsqrt(jnp.sum(diagonal, axis=1, keepdims=True))
    along = lax.rsqrt(jnp.sum(diagonal, axis=0, keepdims=True))
    both = jnp.concatenate(
        [cross * down * along, jnp.where(eye(size), jnp.broadcast_to(along, cross.shape), 0.0)],
        axis=1,
    )
    done = []
    for p in range(size // 32):
        rows = [both[p * 32 + 8 * g : p * 32 + 8 * g + 8] for g in range(4)]
        a, e = eliminate([r[:, :size] for r in rows], [r[:, size:] for r in rows], p * 32)
        a, e = jnp.concatenate(a, axis=0), jnp.concatenate(e, axis=0)
        done.append(e)
        if p < size // 32 - 1:
            both = both - outer(a, jnp.concatenate([a, e], axis=1))
    return jnp.concatenate(done, axis=0)


def near(a, b, dims=NN):
    a, b = split(a), split(b)
    return dot(a[0], b[0], dims) + (dot(a[0], b[1], dims) + dot(a[1], b[0], dims))


def packed_factor(unit):
    half = unit.shape[0] // 2
    row = lax.broadcasted_iota(jnp.int32, (half, half), 0)
    col = lax.broadcasted_iota(jnp.int32, (half, half), 1)
    first = jnp.where(row > col, unit[:half, :half], 0.0)
    second = jnp.where(row > col, unit[half:, half:], 0.0)
    return jnp.concatenate([first + second.T, unit[half:, :half]], axis=1)


def unpacked_factor(packed):
    half = packed.shape[0]
    row = lax.broadcasted_iota(jnp.int32, (half, half), 0)
    col = lax.broadcasted_iota(jnp.int32, (half, half), 1)
    both = packed[:, :half]
    ones = (row == col).astype(F32)
    first = jnp.where(row > col, both, ones)
    second = jnp.where(row > col, both.T, ones)
    top = jnp.concatenate([first, jnp.zeros((half, half), F32)], axis=1)
    return jnp.concatenate([top, jnp.concatenate([packed[:, half:], second], axis=1)], axis=0)


def orthonormal(z):
    return near(z, inverse_factor(near(z, z, TN)), NT)


def sandwich(outer, inner):
    return dot(outer, dot(inner, outer, NT, HIGH), precision=HIGH)


def load_and_weigh(table, snaps_in, blocks_in, snaps, blocks, weighted, sems, greet, use):
    row_blocks, slots, width, _ = blocks.shape
    per = row_blocks // CHUNKS
    side = snaps[0].shape[2]

    def snap_load(h, c):
        at = pl.ds(c * per, per)
        source = snaps_in.at[at, pl.ds(0, width), pl.ds(h * side, side)]
        return pltpu.make_async_copy(source, snaps[h].at[at], sems.at[h, c])

    def block_load(c):
        at = pl.ds(c * per, per)
        return pltpu.make_async_copy(blocks_in.at[at], blocks.at[at], sems.at[2, c])

    for c in range(CHUNKS):
        snap_load(0, c).start()
    for c in range(CHUNKS):
        block_load(c).start()
    for c in range(CHUNKS):
        snap_load(1, c).start()
    greet()
    for h in (0, 1):
        for c in range(CHUNKS):
            snap_load(h, c).wait()

        def chunk(c, carry):
            if h == 0:
                block_load(c).wait()

            def weigh(k, carry):
                row = c * per + k
                count = table[slots, row]
                factors = []
                sources = []
                for slot in range(slots):
                    factor = blocks[row, slot]
                    live = jnp.full(factor.shape, count, jnp.int32) > slot
                    factors.append(jnp.where(live, factor, jnp.zeros_like(factor)))
                    sources.append(snaps[h][table[slot, row]])
                product = dot(jnp.concatenate(factors, axis=1), jnp.concatenate(sources, axis=0))
                at = pl.ds(pl.multiple_of(row * width, width), width)
                weighted[at, h * side : (h + 1) * side] = product.astype(BF16)
                return carry

            lax.fori_loop(0, per, weigh, 0, unroll=8)
            return carry

        lax.fori_loop(0, CHUNKS, chunk, 0)
        use(h)


def parts_of(size):
    blocks = upper_blocks(size // 128)
    half = size // 256
    return [b for b in blocks if b[1] < half], [b for b in blocks if b[1] >= half]


def unpack(flats, full):
    for flat, blocks in zip(flats, parts_of(full.shape[0])):
        for index, (i, j) in enumerate(blocks):
            block = flat[index * 128 : (index + 1) * 128, :]
            full[i * 128 : (i + 1) * 128, j * 128 : (j + 1) * 128] = block
            if i != j:
                full[j * 128 : (j + 1) * 128, i * 128 : (i + 1) * 128] = block.T


def kernel(n, s, table, snaps_in, blocks_in, start_in, starts_in, out, *scratch):
    (blocks, weighted, load_sems) = scratch[1:4]
    snaps = scratch[0], scratch[56]
    y, start, starts, start_sems = scratch[42:46]
    firsts = (4, 46, 48, 50, 52, 54)
    g_own, g_out, g_in, g_all, g_sems, a_sems = [scratch[a : a + 2] for a in firsts]
    (full, vectors, t_out, t_in, t_sems) = scratch[6:11]
    (panels, got, p_sems, q_sems) = scratch[11:15]
    (mine_all, c_out, c_came, z_out, z_came, sum_out, sum_came, cross_all) = scratch[15:23]
    (c_sems, z_sems, s_sems) = scratch[23:26]
    (e_mine, e_got, d_mine, d_got, e_sems) = scratch[26:31]
    (x_own, x_out, x_in, x_all, xr_sems, xa_sems) = scratch[31:37]
    (cf_mine, cf_got, b_mine, b_got, b_sems) = scratch[37:42]
    snap = lax.axis_index("snap")
    space = lax.axis_index("space")
    total = s * n
    me = snap * n + space
    half = s // 2
    bit = snap % 2
    upper = bit == 1
    partner = flipped(snap, 0)
    modes = vectors.shape[1]
    size = full.shape[0]
    rows = panels.shape[1]
    barrier = pltpu.get_barrier_semaphore()

    def device(k):
        other = lax.rem(me + k, total)
        return {"snap": other // n, "space": lax.rem(other, n)}

    small_loads = [
        pltpu.make_async_copy(start_in, start, start_sems.at[0]),
        pltpu.make_async_copy(starts_in, starts, start_sems.at[1]),
    ]

    def greet():
        for c in small_loads:
            c.start()

        def signal(k, carry):
            pl.semaphore_signal(barrier, inc=1, device_id=device(k), device_id_type=MESH)
            return carry

        lax.fori_loop(1, total, signal, 0)

    def share_of(part, index):
        share = g_in[part].shape[1]
        return pl.ds(pl.multiple_of(index * share, share), share)

    def spread(part, k):
        other = lax.rem(space + k, n)
        return remote(
            g_out[part].at[share_of(part, other)],
            g_in[part].at[k - 1],
            g_sems[part].at[0, k - 1],
            g_sems[part].at[1, k - 1],
            {"space": other},
        )

    def gather(part, k):
        return remote(
            g_all[part].at[share_of(part, space)],
            g_all[part].at[share_of(part, space)],
            a_sems[part].at[0, k - 1],
            a_sems[part].at[1, k - 1],
            {"space": lax.rem(space + k, n)},
        )

    def keep(part, index, block):
        at = slice(index * 128, (index + 1) * 128)
        g_own[part][at, :] = block
        g_out[part][at, :] = block.astype(BF16)

    def part_ready(part):
        side = size // 2
        blocks = parts_of(size)[part]
        right = weighted[:, part * side : (part + 1) * side]
        for h in range(part + 1):
            product = dot(weighted[:, h * side : (h + 1) * side], right, TN)
            for index, (i, j) in enumerate(blocks):
                if i * 128 // side == h:
                    row, col = i * 128 - h * side, j * 128 - part * side
                    keep(part, index, product[row : row + 128, col : col + 128])
        used = len(blocks) * 128
        rest = g_own[part].shape[0] - used
        if rest:
            g_own[part][used:, :] = jnp.zeros((rest, 128), F32)
            g_out[part][used:, :] = jnp.zeros((rest, 128), BF16)
        if part == 0:
            pl.semaphore_wait(barrier, total - 1)
        for k in range(1, n):
            spread(part, k).start()

    def part_summed(part):
        mine = g_own[part][share_of(part, space), :]
        for k in range(1, n):
            spread(part, k).wait_recv()
            mine = mine + g_in[part][k - 1].astype(F32)
        g_all[part][share_of(part, space), :] = mine.astype(BF16)
        for k in range(1, n):
            gather(part, k).start()

    load_and_weigh(
        table, snaps_in, blocks_in, snaps, blocks, weighted, load_sems, greet, part_ready
    )
    part_summed(0)

    chosen = n // 2
    for c in small_loads:
        c.wait()
    begin = start[...] * (1.0 / jnp.max(jnp.abs(start[...])))
    told = [
        remote(t_out, t_in, t_sems.at[0, k - 1], t_sems.at[1, 0], {"space": lax.rem(chosen + k, n)})
        for k in range(1, n)
    ]

    @pl.when(space == chosen)
    def _():
        unpack(g_out, full)
        first = dot(full[...], begin.astype(BF16)).astype(BF16)
        cross = dot(first, first, TN)
        scale = modes / jnp.maximum(trace(cross), 1e-30)
        factor = inverse_factor(cross * scale + jnp.where(eye(modes), RIDGE, 0.0))
        unit = factor / jnp.sum(jnp.where(eye(modes), factor, 0.0), axis=1, keepdims=True)
        packed = packed_factor(unit).astype(BF16)
        t_out[...] = packed
        t_in[...] = packed
        for c in told:
            c.start()

    part_summed(1)

    @pl.when(space != chosen)
    def _():
        told[0].wait_recv()

    normal = unpacked_factor(t_in[...].astype(F32)).astype(BF16)
    for part in (0, 1):
        for k in range(1, n):
            gather(part, k).wait_recv()
    unpack(g_all, full)
    trace_of = 0.0
    for i in range(size // 128):
        trace_of = trace_of + trace(
            full[i * 128 : (i + 1) * 128, i * 128 : (i + 1) * 128].astype(F32)
        )
    scale = size / trace_of
    first = wide(full[...], begin) * scale

    high, low = split(first)
    between = dot(high, normal, NT) + dot(low, normal, NT)
    vectors[...] = (wide(full[...], between) * scale).astype(BF16)

    def rows_at(q):
        return pl.ds(pl.multiple_of(q * rows, rows), rows)

    def piece(q):
        return dot(weighted[rows_at(q), :], vectors[...]).astype(BF16)

    def mine_at(q):
        return y.at[rows_at(q)]

    out_copies = []
    arrivals = []
    for h in range(1, half):
        for side in (0, 1):
            q = lax.rem(snap // 2 + h, half) * 2 + side
            source = lax.rem(snap // 2 + half - h, half) * 2 + side
            y[rows_at(q), :] = piece(q)
            send = p_sems.at[0, 2 * h + side]
            c = remote(mine_at(q), panels.at[snap], send, p_sems.at[1, 2 * h + bit], {"snap": q})
            c.start()
            out_copies.append(c)
            arrivals.append(
                remote(mine_at(q), panels.at[source], send, p_sems.at[1, 2 * h + side], {"snap": q})
            )
    pair_copies = []
    for h in range(half):
        q = lax.rem(snap // 2 + h, half) * 2 + 1 - bit
        if h == 0:
            y[rows_at(q), :] = piece(q)
        c = remote(mine_at(q), got.at[h], q_sems.at[0, h], q_sems.at[1, h], {"snap": partner})
        c.start()
        pair_copies.append(c)
    y[rows_at(snap), :] = piece(snap)

    cross = jnp.zeros((modes, modes), F32)
    for h in range(half):
        q = lax.rem(snap // 2 + h, half) * 2 + bit
        pair_copies[h].wait_recv()
        cross = cross + dot(y[rows_at(q), :], got[h], TN)
    panels[snap] = y[rows_at(snap), :]
    panels[partner] = got[0]
    cross = jnp.where(upper, cross.T, cross)
    part_rows = modes // 2

    def part_of(index):
        return pl.ds(pl.multiple_of(index * part_rows, part_rows), part_rows)

    mine_all[...] = cross
    c_out[...] = cross.astype(BF16)
    swap = remote(
        c_out.at[part_of(1 - bit)], c_came, c_sems.at[0], c_sems.at[1], {"snap": partner}
    )
    swap.start()
    moved = dot(full[...], vectors[...])
    product = wide(vectors[...].T, moved)
    square = dot(vectors[...], vectors[...], TN)
    swap.wait_recv()
    part = mine_all[part_of(bit), :] + c_came[...].astype(F32)
    z_out[...] = part.astype(BF16)
    steps = [
        remote(
            z_out,
            z_came.at[k - 1],
            z_sems.at[0, k - 1],
            z_sems.at[1, k - 1],
            {"space": lax.rem(space + k, n)},
        )
        for k in range(1, n)
    ]
    for c in steps:
        c.start()
    e_mine[...] = inverse_factor(square)
    d_mine[...] = sandwich(e_mine[...], product)
    tell = [
        remote(e_mine, e_got, e_sems.at[0, 0], e_sems.at[1, 0], {"snap": partner}),
        remote(d_mine, d_got, e_sems.at[0, 1], e_sems.at[1, 1], {"snap": partner}),
    ]
    for c in tell:
        c.start()
    for k, c in enumerate(steps):
        c.wait_recv()
        part = part + z_came[k].astype(F32)
    sum_out[...] = part.astype(BF16)
    collect = remote(sum_out, sum_came, s_sems.at[0], s_sems.at[1], {"snap": partner})
    collect.start()
    for c in tell:
        c.wait_recv()
    collect.wait_recv()
    cross_all[part_of(bit), :] = sum_out[...].astype(F32)
    cross_all[part_of(1 - bit), :] = sum_came[...].astype(F32)
    e_low = jnp.where(upper, e_got[...], e_mine[...])
    e_high = jnp.where(upper, e_mine[...], e_got[...])
    d_low = jnp.where(upper, d_got[...], d_mine[...])
    d_high = jnp.where(upper, d_mine[...], d_got[...])
    cross = dot(e_low, dot(cross_all[...], e_high, NT, HIGH), precision=HIGH)

    def start_of(level):
        return starts[s - (s >> level) + snap // (1 << (level + 1))]

    def wait_gathered(level):
        if level == 1:
            each(lambda k: x_gather(k).wait_recv())

    def merged(level, d_low, cross, d_high):
        pair = jnp.concatenate(
            [
                jnp.concatenate([d_low, cross], axis=1),
                jnp.concatenate([cross.T, d_high], axis=1),
            ],
            axis=0,
        )
        return pair, orthonormal(near(pair, start_of(level)))

    def diagonal(pair, mixing):
        return near(mixing, near(pair, mixing), TN)

    for c in arrivals:
        c.wait_recv()
    done = 0
    for low_pair in range(half):
        for high_pair in range(low_pair + 1, half):
            sides = [
                jnp.concatenate([panels[2 * p], panels[2 * p + 1]], axis=1)
                for p in (low_pair, high_pair)
            ]
            blocks_of = dot(sides[0], sides[1], TN)
            for i in range(2):
                for j in range(2):
                    at = slice(done * 128, (done + 1) * 128)
                    block = blocks_of[i * modes : (i + 1) * modes, j * modes : (j + 1) * modes]
                    x_own[at, :] = block
                    x_out[at, :] = block.astype(BF16)
                    done = done + 1
    if done * 128 < x_own.shape[0]:
        x_own[done * 128 :, :] = jnp.zeros((x_own.shape[0] - done * 128, 128), F32)
        x_out[done * 128 :, :] = jnp.zeros((x_own.shape[0] - done * 128, 128), BF16)
    x_share = x_in.shape[1]

    def x_part(index):
        return pl.ds(pl.multiple_of(index * x_share, x_share), x_share)

    def x_spread(k):
        return remote(
            x_out.at[x_part(lax.rem(me + k, total))],
            x_in.at[k - 1],
            xr_sems.at[0, k - 1],
            xr_sems.at[1, k - 1],
            device(k),
        )

    def x_gather(k):
        return remote(
            x_all.at[x_part(me)],
            x_all.at[x_part(me)],
            xa_sems.at[0, k - 1],
            xa_sems.at[1, k - 1],
            device(k),
        )

    def each(act):
        if total <= 16:
            for k in range(1, total):
                act(k)
            return

        def step(k, carry):
            act(k)
            return carry

        lax.fori_loop(1, total, step, 0)

    each(lambda k: x_spread(k).start())
    pair, mixing = merged(0, d_low, cross, d_high)

    levels = s.bit_length() - 1
    sent = []

    def tell_factors(level, factors):
        count = 1 << level
        for i in range(count):
            cf_mine[level - 1, i] = factors[i].astype(BF16)
        c = remote(
            cf_mine.at[level - 1, pl.ds(0, count)],
            cf_got.at[level - 1, pl.ds(0, count)],
            b_sems.at[0, level - 1, 0],
            b_sems.at[1, level - 1, 0],
            {"snap": flipped(snap, level)},
        )
        c.start()
        sent.append(c)
        return c

    def tell_diagonal(level, pair, mixing):
        b_mine[level - 1] = diagonal(pair, mixing).astype(BF16)
        c = remote(
            b_mine.at[level - 1],
            b_got.at[level - 1],
            b_sems.at[0, level - 1, 1],
            b_sems.at[1, level - 1, 1],
            {"snap": flipped(snap, level)},
        )
        c.start()
        sent.append(c)
        return c

    factors = [near(e_low, mixing[:modes], TN), near(e_high, mixing[modes:], TN)]
    pass_on = [tell_factors(1, factors)]

    def add(k, so_far):
        x_spread(k).wait_recv()
        return so_far + x_in[k - 1].astype(F32)

    shared = x_own[x_part(me), :]
    if total <= 16:
        for k in range(1, total):
            shared = add(k, shared)
    else:
        shared = lax.fori_loop(1, total, add, shared)
    x_all[x_part(me), :] = shared.astype(BF16)
    each(lambda k: x_gather(k).start())
    pass_on.append(tell_diagonal(1, pair, mixing))
    for level in range(1, levels):
        count = 1 << level
        if level > 1:
            pass_on = [tell_factors(level, factors), tell_diagonal(level, pair, mixing)]
        for c in pass_on:
            c.wait_recv()
        high_side = snap // count % 2 == 1
        lows, highs = [], []
        for i in range(count):
            own, theirs = cf_mine[level - 1, i], cf_got[level - 1, i]
            lows.append(jnp.where(high_side, theirs, own))
            highs.append(jnp.where(high_side, own, theirs))
        own, theirs = b_mine[level - 1].astype(F32), b_got[level - 1].astype(F32)
        d_low = jnp.where(high_side, theirs, own)
        d_high = jnp.where(high_side, own, theirs)
        base = snap // (2 * count) * count

        def between(a, i, b, j):
            pa, pb = base + a, base + count // 2 + b
            place = pa * (2 * half - pa - 1) // 2 + pb - pa - 1
            return x_all[pl.ds(pl.multiple_of((place * 4 + i * 2 + j) * 128, 128), 128), :]

        every = [(a, i) for a in range(count // 2) for i in (0, 1)]
        inner = [r + c for r in every for c in every]
        if level < levels - 1:
            wait_gathered(level)
            cross = jnp.zeros((modes, modes), F32)
            for a, i, b, j in inner:
                right = dot(between(a, i, b, j), highs[2 * b + j])
                cross = cross + wide(lows[2 * a + i].T, right)
            pair, mixing = merged(level, d_low, cross, d_high)
            low_mix, high_mix = mixing[:modes], mixing[modes:]
            factors = [wide(f, low_mix) for f in lows] + [wide(f, high_mix) for f in highs]
            continue
        low_start, high_start = start_of(level)[:modes], start_of(level)[modes:]
        low_ahead = [wide(f, low_start) for f in lows]
        high_ahead = [wide(f, high_start) for f in highs]
        top, bottom = near(d_low, low_start), near(d_high, high_start)
        low_across = jnp.concatenate([f.T for f in lows], axis=1)
        high_across = jnp.concatenate([f.T for f in highs], axis=1)
        low_ahead = split(jnp.concatenate(low_ahead, axis=0))
        high_ahead = split(jnp.concatenate(high_ahead, axis=0))
        wait_gathered(level)
        table = {at: between(*at) for at in inner}
        block = jnp.concatenate(
            [jnp.concatenate([table[r + c] for c in every], axis=1) for r in every], axis=0
        )
        right = dot(block, high_ahead[0]) + dot(block, high_ahead[1])
        left = dot(block, low_ahead[0], TN) + dot(block, low_ahead[1], TN)
        z = jnp.concatenate([top + wide(low_across, right), bottom + wide(high_across, left)], axis=0)
        inverse = inverse_factor(near(z, z, TN))
        coefficients = [wide(f, z[:modes]) for f in lows] + [wide(f, z[modes:]) for f in highs]
        factors = [near(c, inverse, NT) for c in coefficients]
    depth = jnp.concatenate([f.astype(BF16) for f in factors], axis=0)
    out[...] = dot(jnp.concatenate([panels[i] for i in range(s)], axis=1), depth).astype(BF16)

    @pl.when(space == chosen)
    def _():
        for c in told:
            c.wait_send()

    for part in (0, 1):
        for k in range(1, n):
            spread(part, k).wait_send()
            gather(part, k).wait_send()
    for c in out_copies + pair_copies + [swap] + steps + tell + [collect] + sent:
        c.wait_send()
    each(lambda k: x_spread(k).wait_send())
    each(lambda k: x_gather(k).wait_send())


def padded(rows, parts):
    share = -(-rows // parts)
    return -(-share // 16) * 16


def local(snapshots, factor_blocks, factor_cols, factor_counts, start_basis, merge_starts):
    n = lax.axis_size("space")
    s = lax.axis_size("snap")
    total = s * n
    size, modes = start_basis.shape
    rows = snapshots.shape[0] // s
    half = s // 2
    width = factor_blocks.shape[2]
    blocked = snapshots.reshape(snapshots.shape[0] // width, width, size)
    levels = s.bit_length() - 1
    x_share = padded(4 * (half * (half - 1) // 2) * 128, total)
    dma = pltpu.SemaphoreType.DMA
    shares = [padded(len(blocks) * 128, n) for blocks in parts_of(size)]
    table = jnp.concatenate([factor_cols.T, factor_counts[None]])
    scratch = [
        pltpu.VMEM((blocked.shape[0], width, size // 2), BF16),
        pltpu.VMEM(factor_blocks.shape, BF16),
        pltpu.VMEM(snapshots.shape, BF16),
        dma((3, CHUNKS)),
        *[pltpu.VMEM((share * n, 128), F32) for share in shares],
        pltpu.VMEM((size, size), BF16),
        pltpu.VMEM((size, modes), BF16),
        pltpu.VMEM((modes // 2, modes), BF16),
        pltpu.VMEM((modes // 2, modes), BF16),
        dma((2, n - 1)),
        pltpu.VMEM((s, rows, modes), BF16),
        pltpu.VMEM((half, rows, modes), BF16),
        dma((2, s)),
        dma((2, half)),
        pltpu.VMEM((modes, modes), F32),
        pltpu.VMEM((modes, modes), BF16),
        pltpu.VMEM((modes // 2, modes), BF16),
        pltpu.VMEM((modes // 2, modes), BF16),
        pltpu.VMEM((n - 1, modes // 2, modes), BF16),
        pltpu.VMEM((modes // 2, modes), BF16),
        pltpu.VMEM((modes // 2, modes), BF16),
        pltpu.VMEM((modes, modes), F32),
        dma((2,)),
        dma((2, n - 1)),
        dma((2,)),
        pltpu.VMEM((modes, modes), F32),
        pltpu.VMEM((modes, modes), F32),
        pltpu.VMEM((modes, modes), F32),
        pltpu.VMEM((modes, modes), F32),
        dma((2, 2)),
        pltpu.VMEM((x_share * total, 128), F32),
        pltpu.VMEM((x_share * total, 128), BF16),
        pltpu.VMEM((total - 1, x_share, 128), BF16),
        pltpu.VMEM((x_share * total, 128), BF16),
        dma((2, total - 1)),
        dma((2, total - 1)),
        pltpu.VMEM((levels - 1, half, modes, modes), BF16),
        pltpu.VMEM((levels - 1, half, modes, modes), BF16),
        pltpu.VMEM((levels - 1, modes, modes), BF16),
        pltpu.VMEM((levels - 1, modes, modes), BF16),
        dma((2, levels - 1, 2)),
        pltpu.VMEM((snapshots.shape[0], modes), BF16),
        pltpu.VMEM(start_basis.shape, F32),
        pltpu.VMEM(merge_starts.shape, F32),
        dma((2,)),
        *[pltpu.VMEM((share * n, 128), BF16) for share in shares],
        *[pltpu.VMEM((n - 1, share, 128), BF16) for share in shares],
        *[pltpu.VMEM((share * n, 128), BF16) for share in shares],
        *[dma((2, n - 1)) for share in shares],
        *[dma((2, n - 1)) for share in shares],
        pltpu.VMEM((blocked.shape[0], width, size // 2), BF16),
    ]
    return pl.pallas_call(
        functools.partial(kernel, n, s),
        in_specs=[SMEM, ANY, ANY, ANY, ANY],
        out_specs=VMEM,
        out_shape=jax.ShapeDtypeStruct((rows, modes), BF16),
        scratch_shapes=scratch,
        compiler_params=pltpu.CompilerParams(
            collective_id=0, has_side_effects=True, vmem_limit_bytes=VMEM_LIMIT
        ),
        name="modes",
    )(table, blocked, factor_blocks, start_basis, merge_starts)


def solution(mesh):
    return jax.shard_map(
        local,
        mesh=mesh,
        in_specs=(
            P("space", ("groups", "snap")),
            P("space", None, None, None),
            P("space", None),
            P("space"),
            P(("groups", "snap"), None),
            P(),
        ),
        out_specs=P(("space", "snap"), "groups"),
        check_vma=False,
    )
```

```python
import functools

import jax
import jax.numpy as jnp
from jax import lax
from jax.experimental import pallas as pl
from jax.experimental.pallas import tpu as pltpu
from jax.sharding import PartitionSpec as P

HIGH = lax.Precision.HIGHEST
MESH = pl.DeviceIdType.MESH
F32 = jnp.float32
BF16 = jnp.bfloat16
VMEM = pl.BlockSpec(memory_space=pltpu.VMEM)
SMEM = pl.BlockSpec(memory_space=pltpu.SMEM)
ANY = pl.BlockSpec(memory_space=pl.ANY)
CHUNKS = 4
VMEM_LIMIT = 54835 * 1024
RIDGE = 1e-4
TN = (((0,), (0,)), ((), ()))
NT = (((1,), (1,)), ((), ()))
NN = (((1,), (0,)), ((), ()))


def dot(a, b, dims=NN, precision=None):
    return lax.dot_general(a, b, dims, precision=precision, preferred_element_type=F32)


def split(x):
    high = x.astype(BF16)
    return high, (x - high.astype(F32)).astype(BF16)


def wide(a, x):
    size = x.shape[1]
    both = dot(a, jnp.concatenate(split(x), axis=1))
    return both[:, :size] + both[:, size:]


def upper_blocks(count):
    return [(i, j) for i in range(count) for j in range(i, count)]


def flipped(index, bit):
    return index + (1 - 2 * (index // (1 << bit) % 2)) * (1 << bit)


def remote(source, target, send, recv, device):
    return pltpu.make_async_remote_copy(
        src_ref=source,
        dst_ref=target,
        send_sem=send,
        recv_sem=recv,
        device_id=device,
        device_id_type=MESH,
    )


def eye(size):
    row = lax.broadcasted_iota(jnp.int32, (size, size), 0)
    col = lax.broadcasted_iota(jnp.int32, (size, size), 1)
    return row == col


def trace(x):
    return jnp.sum(jnp.where(eye(x.shape[0]), x, 0.0))


def rows_of(block):
    return pl.ds(block * 128, 128)


def eliminate(a, e, lane):
    a, e = list(a), list(e)
    groups = len(a)
    row = lax.broadcasted_iota(jnp.int32, (8, 128), 0)
    scale = [jnp.zeros((8, 128), F32)] * groups

    def spread(x, k):
        return jnp.broadcast_to(x[k : k + 1, :], (8, 128))

    def columns(g, first):
        return {
            h: [
                jnp.broadcast_to(a[h][:, lane + 8 * g + k : lane + 8 * g + k + 1], (8, 128))
                for k in range(8)
            ]
            for h in range(first, groups)
        }

    ahead = columns(0, 0)
    for g in range(groups):
        cols = {h: ahead[h] for h in range(g, groups)}
        ahead = columns(g + 1, g) if g + 1 < groups else None
        for k in range(0, 8, 2):
            p, q, r = spread(cols[g][k], k), spread(cols[g][k], k + 1), spread(cols[g][k + 1], k + 1)
            det = p * r - q * q
            over_det = 1.0 / det
            over_p = 1.0 / p
            i, j, l = r * over_det, q * over_det, p * over_det
            scale[g] = jnp.where(row == k, lax.rsqrt(p), scale[g])
            scale[g] = jnp.where(row == k + 1, lax.rsqrt(det * over_p), scale[g])
            a_rows = spread(a[g], k), spread(a[g], k + 1)
            e_rows = spread(e[g], k), spread(e[g], k + 1)
            heads = {
                m: (spread(cols[g][m], k), spread(cols[g][m], k + 1)) for m in range(k + 2, 8)
            }
            far = []
            if ahead is not None:
                far = [(spread(x, k), spread(x, k + 1)) for x in ahead[g]]
            for h in range(g, groups):
                c, d = cols[h][k], cols[h][k + 1]
                f1 = c * i - d * j
                f2 = d * l - c * j
                if h == g:
                    f1 = jnp.where(row > k + 1, f1, jnp.where(row == k + 1, q * over_p, 0.0))
                    f2 = jnp.where(row > k + 1, f2, 0.0)
                for m in range(k + 2, 8):
                    cols[h][m] = cols[h][m] - (f1 * heads[m][0] + f2 * heads[m][1])
                for m, (x, y) in enumerate(far):
                    ahead[h][m] = ahead[h][m] - (f1 * x + f2 * y)
                a[h] = a[h] - (f1 * a_rows[0] + f2 * a_rows[1])
                e[h] = e[h] - (f1 * e_rows[0] + f2 * e_rows[1])
    return [x * s for x, s in zip(a, scale)], [x * s for x, s in zip(e, scale)]


def thirds(x):
    high = x.astype(BF16)
    rest = x - high.astype(F32)
    middle = rest.astype(BF16)
    return high, middle, (rest - middle.astype(F32)).astype(BF16)


def outer(a, b):
    a, b = thirds(a), thirds(b)
    left = jnp.concatenate([a[0], a[0], a[1], a[0], a[2], a[1]], axis=0)
    right = jnp.concatenate([b[0], b[1], b[0], b[2], b[0], b[1]], axis=0)
    return dot(left, right, TN)


def inverse_factor(cross):
    size = cross.shape[0]
    diagonal = jnp.where(eye(size), cross, 0.0)
    down = lax.rsqrt(jnp.sum(diagonal, axis=1, keepdims=True))
    along = lax.rsqrt(jnp.sum(diagonal, axis=0, keepdims=True))
    both = jnp.concatenate(
        [cross * down * along, jnp.where(eye(size), jnp.broadcast_to(along, cross.shape), 0.0)],
        axis=1,
    )
    done = []
    for p in range(size // 32):
        rows = [both[p * 32 + 8 * g : p * 32 + 8 * g + 8] for g in range(4)]
        a, e = eliminate([r[:, :size] for r in rows], [r[:, size:] for r in rows], p * 32)
        a, e = jnp.concatenate(a, axis=0), jnp.concatenate(e, axis=0)
        done.append(e)
        if p < size // 32 - 1:
            both = both - outer(a, jnp.concatenate([a, e], axis=1))
    return jnp.concatenate(done, axis=0)


def near(a, b, dims=NN):
    a, b = split(a), split(b)
    return dot(a[0], b[0], dims) + (dot(a[0], b[1], dims) + dot(a[1], b[0], dims))


def packed_factor(unit):
    half = unit.shape[0] // 2
    row = lax.broadcasted_iota(jnp.int32, (half, half), 0)
    col = lax.broadcasted_iota(jnp.int32, (half, half), 1)
    first = jnp.where(row > col, unit[:half, :half], 0.0)
    second = jnp.where(row > col, unit[half:, half:], 0.0)
    return jnp.concatenate([first + second.T, unit[half:, :half]], axis=1)


def unpacked_factor(packed):
    half = packed.shape[0]
    row = lax.broadcasted_iota(jnp.int32, (half, half), 0)
    col = lax.broadcasted_iota(jnp.int32, (half, half), 1)
    both = packed[:, :half]
    ones = (row == col).astype(F32)
    first = jnp.where(row > col, both, ones)
    second = jnp.where(row > col, both.T, ones)
    top = jnp.concatenate([first, jnp.zeros((half, half), F32)], axis=1)
    return jnp.concatenate([top, jnp.concatenate([packed[:, half:], second], axis=1)], axis=0)


def orthonormal(z):
    return near(z, inverse_factor(near(z, z, TN)), NT)


def sandwich(outer, inner):
    return dot(outer, dot(inner, outer, NT, HIGH), precision=HIGH)


def load_and_weigh(table, snaps_in, blocks_in, snaps, blocks, weighted, sems, greet, use):
    row_blocks, slots, width, _ = blocks.shape
    per = row_blocks // CHUNKS
    side = snaps[0].shape[2]

    def snap_load(h, c):
        at = pl.ds(c * per, per)
        source = snaps_in.at[at, pl.ds(0, width), pl.ds(h * side, side)]
        return pltpu.make_async_copy(source, snaps[h].at[at], sems.at[h, c])

    def block_load(c):
        at = pl.ds(c * per, per)
        return pltpu.make_async_copy(blocks_in.at[at], blocks.at[at], sems.at[2, c])

    for c in range(CHUNKS):
        snap_load(0, c).start()
    for c in range(CHUNKS):
        block_load(c).start()
    for c in range(CHUNKS):
        snap_load(1, c).start()
    greet()
    for h in (0, 1):
        for c in range(CHUNKS):
            snap_load(h, c).wait()

        def chunk(c, carry):
            if h == 0:
                block_load(c).wait()

            def weigh(k, carry):
                row = c * per + k
                count = table[slots, row]
                factors = []
                sources = []
                for slot in range(slots):
                    factor = blocks[row, slot]
                    live = jnp.full(factor.shape, count, jnp.int32) > slot
                    factors.append(jnp.where(live, factor, jnp.zeros_like(factor)))
                    sources.append(snaps[h][table[slot, row]])
                product = dot(jnp.concatenate(factors, axis=1), jnp.concatenate(sources, axis=0))
                at = pl.ds(pl.multiple_of(row * width, width), width)
                weighted[at, h * side : (h + 1) * side] = product.astype(BF16)
                return carry

            lax.fori_loop(0, per, weigh, 0, unroll=8)
            return carry

        lax.fori_loop(0, CHUNKS, chunk, 0)
        use(h)


def parts_of(size):
    blocks = upper_blocks(size // 128)
    half = size // 256
    return [b for b in blocks if b[1] < half], [b for b in blocks if b[1] >= half]


def unpack(flats, full):
    for flat, blocks in zip(flats, parts_of(full.shape[0])):
        for index, (i, j) in enumerate(blocks):
            block = flat[index * 128 : (index + 1) * 128, :]
            full[i * 128 : (i + 1) * 128, j * 128 : (j + 1) * 128] = block
            if i != j:
                full[j * 128 : (j + 1) * 128, i * 128 : (i + 1) * 128] = block.T


def kernel(n, s, table, snaps_in, blocks_in, start_in, starts_in, out, *scratch):
    (blocks, weighted, load_sems) = scratch[1:4]
    snaps = scratch[0], scratch[56]
    y, start, starts, start_sems = scratch[42:46]
    firsts = (4, 46, 48, 50, 52, 54)
    g_own, g_out, g_in, g_all, g_sems, a_sems = [scratch[a : a + 2] for a in firsts]
    (full, vectors, t_out, t_in, t_sems) = scratch[6:11]
    (panels, got, p_sems, q_sems) = scratch[11:15]
    (mine_all, c_out, c_came, z_out, z_came, sum_out, sum_came, cross_all) = scratch[15:23]
    (c_sems, z_sems, s_sems) = scratch[23:26]
    (e_mine, e_got, d_mine, d_got, e_sems) = scratch[26:31]
    (x_own, x_out, x_in, x_all, xr_sems, xa_sems) = scratch[31:37]
    (cf_mine, cf_got, b_mine, b_got, b_sems) = scratch[37:42]
    snap = lax.axis_index("snap")
    space = lax.axis_index("space")
    total = s * n
    me = snap * n + space
    half = s // 2
    bit = snap % 2
    upper = bit == 1
    partner = flipped(snap, 0)
    modes = vectors.shape[1]
    size = full.shape[0]
    rows = panels.shape[1]
    barrier = pltpu.get_barrier_semaphore()

    def device(k):
        other = lax.rem(me + k, total)
        return {"snap": other // n, "space": lax.rem(other, n)}

    small_loads = [
        pltpu.make_async_copy(start_in, start, start_sems.at[0]),
        pltpu.make_async_copy(starts_in, starts, start_sems.at[1]),
    ]

    def greet():
        for c in small_loads:
            c.start()

        def signal(k, carry):
            pl.semaphore_signal(barrier, inc=1, device_id=device(k), device_id_type=MESH)
            return carry

        lax.fori_loop(1, total, signal, 0)

    def share_of(part, index):
        share = g_in[part].shape[1]
        return pl.ds(pl.multiple_of(index * share, share), share)

    def spread(part, k):
        other = lax.rem(space + k, n)
        return remote(
            g_out[part].at[share_of(part, other)],
            g_in[part].at[k - 1],
            g_sems[part].at[0, k - 1],
            g_sems[part].at[1, k - 1],
            {"space": other},
        )

    def gather(part, k):
        return remote(
            g_all[part].at[share_of(part, space)],
            g_all[part].at[share_of(part, space)],
            a_sems[part].at[0, k - 1],
            a_sems[part].at[1, k - 1],
            {"space": lax.rem(space + k, n)},
        )

    def keep(part, index, block):
        at = slice(index * 128, (index + 1) * 128)
        g_own[part][at, :] = block
        g_out[part][at, :] = block.astype(BF16)

    def part_ready(part):
        side = size // 2
        blocks = parts_of(size)[part]
        right = weighted[:, part * side : (part + 1) * side]
        for h in range(part + 1):
            product = dot(weighted[:, h * side : (h + 1) * side], right, TN)
            for index, (i, j) in enumerate(blocks):
                if i * 128 // side == h:
                    row, col = i * 128 - h * side, j * 128 - part * side
                    keep(part, index, product[row : row + 128, col : col + 128])
        used = len(blocks) * 128
        rest = g_own[part].shape[0] - used
        if rest:
            g_own[part][used:, :] = jnp.zeros((rest, 128), F32)
            g_out[part][used:, :] = jnp.zeros((rest, 128), BF16)
        if part == 0:
            pl.semaphore_wait(barrier, total - 1)
        for k in range(1, n):
            spread(part, k).start()

    def part_summed(part):
        mine = g_own[part][share_of(part, space), :]
        for k in range(1, n):
            spread(part, k).wait_recv()
            mine = mine + g_in[part][k - 1].astype(F32)
        g_all[part][share_of(part, space), :] = mine.astype(BF16)
        for k in range(1, n):
            gather(part, k).start()

    load_and_weigh(
        table, snaps_in, blocks_in, snaps, blocks, weighted, load_sems, greet, part_ready
    )
    part_summed(0)

    chosen = n // 2
    for c in small_loads:
        c.wait()
    begin = start[...] * (1.0 / jnp.max(jnp.abs(start[...])))
    told = [
        remote(t_out, t_in, t_sems.at[0, k - 1], t_sems.at[1, 0], {"space": lax.rem(chosen + k, n)})
        for k in range(1, n)
    ]

    @pl.when(space == chosen)
    def _():
        unpack(g_out, full)
        first = dot(full[...], begin.astype(BF16)).astype(BF16)
        cross = dot(first, first, TN)
        scale = modes / jnp.maximum(trace(cross), 1e-30)
        factor = inverse_factor(cross * scale + jnp.where(eye(modes), RIDGE, 0.0))
        unit = factor / jnp.sum(jnp.where(eye(modes), factor, 0.0), axis=1, keepdims=True)
        packed = packed_factor(unit).astype(BF16)
        t_out[...] = packed
        t_in[...] = packed
        for c in told:
            c.start()

    part_summed(1)

    @pl.when(space != chosen)
    def _():
        told[0].wait_recv()

    normal = unpacked_factor(t_in[...].astype(F32)).astype(BF16)
    for part in (0, 1):
        for k in range(1, n):
            gather(part, k).wait_recv()
    unpack(g_all, full)
    trace_of = 0.0
    for i in range(size // 128):
        trace_of = trace_of + trace(
            full[i * 128 : (i + 1) * 128, i * 128 : (i + 1) * 128].astype(F32)
        )
    scale = size / trace_of
    first = wide(full[...], begin) * scale

    high, low = split(first)
    between = dot(high, normal, NT) + dot(low, normal, NT)
    vectors[...] = (wide(full[...], between) * scale).astype(BF16)

    def rows_at(q):
        return pl.ds(pl.multiple_of(q * rows, rows), rows)

    def piece(q):
        return dot(weighted[rows_at(q), :], vectors[...]).astype(BF16)

    def mine_at(q):
        return y.at[rows_at(q)]

    out_copies = []
    arrivals = []
    for h in range(1, half):
        for side in (0, 1):
            q = lax.rem(snap // 2 + h, half) * 2 + side
            source = lax.rem(snap // 2 + half - h, half) * 2 + side
            y[rows_at(q), :] = piece(q)
            send = p_sems.at[0, 2 * h + side]
            c = remote(mine_at(q), panels.at[snap], send, p_sems.at[1, 2 * h + bit], {"snap": q})
            c.start()
            out_copies.append(c)
            arrivals.append(
                remote(mine_at(q), panels.at[source], send, p_sems.at[1, 2 * h + side], {"snap": q})
            )
    pair_copies = []
    for h in range(half):
        q = lax.rem(snap // 2 + h, half) * 2 + 1 - bit
        if h == 0:
            y[rows_at(q), :] = piece(q)
        c = remote(mine_at(q), got.at[h], q_sems.at[0, h], q_sems.at[1, h], {"snap": partner})
        c.start()
        pair_copies.append(c)
    y[rows_at(snap), :] = piece(snap)

    cross = jnp.zeros((modes, modes), F32)
    for h in range(half):
        q = lax.rem(snap // 2 + h, half) * 2 + bit
        pair_copies[h].wait_recv()
        cross = cross + dot(y[rows_at(q), :], got[h], TN)
    panels[snap] = y[rows_at(snap), :]
    panels[partner] = got[0]
    cross = jnp.where(upper, cross.T, cross)
    part_rows = modes // 2

    def part_of(index):
        return pl.ds(pl.multiple_of(index * part_rows, part_rows), part_rows)

    mine_all[...] = cross
    c_out[...] = cross.astype(BF16)
    swap = remote(
        c_out.at[part_of(1 - bit)], c_came, c_sems.at[0], c_sems.at[1], {"snap": partner}
    )
    swap.start()
    moved = dot(full[...], vectors[...])
    product = wide(vectors[...].T, moved)
    square = dot(vectors[...], vectors[...], TN)
    swap.wait_recv()
    part = mine_all[part_of(bit), :] + c_came[...].astype(F32)
    z_out[...] = part.astype(BF16)
    steps = [
        remote(
            z_out,
            z_came.at[k - 1],
            z_sems.at[0, k - 1],
            z_sems.at[1, k - 1],
            {"space": lax.rem(space + k, n)},
        )
        for k in range(1, n)
    ]
    for c in steps:
        c.start()
    e_mine[...] = inverse_factor(square)
    d_mine[...] = sandwich(e_mine[...], product)
    tell = [
        remote(e_mine, e_got, e_sems.at[0, 0], e_sems.at[1, 0], {"snap": partner}),
        remote(d_mine, d_got, e_sems.at[0, 1], e_sems.at[1, 1], {"snap": partner}),
    ]
    for c in tell:
        c.start()
    for k, c in enumerate(steps):
        c.wait_recv()
        part = part + z_came[k].astype(F32)
    sum_out[...] = part.astype(BF16)
    collect = remote(sum_out, sum_came, s_sems.at[0], s_sems.at[1], {"snap": partner})
    collect.start()
    for c in tell:
        c.wait_recv()
    collect.wait_recv()
    cross_all[part_of(bit), :] = sum_out[...].astype(F32)
    cross_all[part_of(1 - bit), :] = sum_came[...].astype(F32)
    e_low = jnp.where(upper, e_got[...], e_mine[...])
    e_high = jnp.where(upper, e_mine[...], e_got[...])
    d_low = jnp.where(upper, d_got[...], d_mine[...])
    d_high = jnp.where(upper, d_mine[...], d_got[...])
    cross = dot(e_low, dot(cross_all[...], e_high, NT, HIGH), precision=HIGH)

    def start_of(level):
        return starts[s - (s >> level) + snap // (1 << (level + 1))]

    def wait_gathered(level):
        if level == 1:
            each(lambda k: x_gather(k).wait_recv())

    def merged(level, d_low, cross, d_high):
        pair = jnp.concatenate(
            [
                jnp.concatenate([d_low, cross], axis=1),
                jnp.concatenate([cross.T, d_high], axis=1),
            ],
            axis=0,
        )
        return pair, orthonormal(near(pair, start_of(level)))

    def diagonal(pair, mixing):
        return near(mixing, near(pair, mixing), TN)

    for c in arrivals:
        c.wait_recv()
    done = 0
    for low_pair in range(half):
        for high_pair in range(low_pair + 1, half):
            sides = [
                jnp.concatenate([panels[2 * p], panels[2 * p + 1]], axis=1)
                for p in (low_pair, high_pair)
            ]
            blocks_of = dot(sides[0], sides[1], TN)
            for i in range(2):
                for j in range(2):
                    at = slice(done * 128, (done + 1) * 128)
                    block = blocks_of[i * modes : (i + 1) * modes, j * modes : (j + 1) * modes]
                    x_own[at, :] = block
                    x_out[at, :] = block.astype(BF16)
                    done = done + 1
    if done * 128 < x_own.shape[0]:
        x_own[done * 128 :, :] = jnp.zeros((x_own.shape[0] - done * 128, 128), F32)
        x_out[done * 128 :, :] = jnp.zeros((x_own.shape[0] - done * 128, 128), BF16)
    x_share = x_in.shape[1]

    def x_part(index):
        return pl.ds(pl.multiple_of(index * x_share, x_share), x_share)

    def x_spread(k):
        return remote(
            x_out.at[x_part(lax.rem(me + k, total))],
            x_in.at[k - 1],
            xr_sems.at[0, k - 1],
            xr_sems.at[1, k - 1],
            device(k),
        )

    def x_gather(k):
        return remote(
            x_all.at[x_part(me)],
            x_all.at[x_part(me)],
            xa_sems.at[0, k - 1],
            xa_sems.at[1, k - 1],
            device(k),
        )

    def each(act):
        if total <= 16:
            for k in range(1, total):
                act(k)
            return

        def step(k, carry):
            act(k)
            return carry

        lax.fori_loop(1, total, step, 0)

    each(lambda k: x_spread(k).start())
    pair, mixing = merged(0, d_low, cross, d_high)

    levels = s.bit_length() - 1
    sent = []

    def tell_factors(level, factors):
        count = 1 << level
        for i in range(count):
            cf_mine[level - 1, i] = factors[i].astype(BF16)
        c = remote(
            cf_mine.at[level - 1, pl.ds(0, count)],
            cf_got.at[level - 1, pl.ds(0, count)],
            b_sems.at[0, level - 1, 0],
            b_sems.at[1, level - 1, 0],
            {"snap": flipped(snap, level)},
        )
        c.start()
        sent.append(c)
        return c

    def tell_diagonal(level, pair, mixing):
        b_mine[level - 1] = diagonal(pair, mixing).astype(BF16)
        c = remote(
            b_mine.at[level - 1],
            b_got.at[level - 1],
            b_sems.at[0, level - 1, 1],
            b_sems.at[1, level - 1, 1],
            {"snap": flipped(snap, level)},
        )
        c.start()
        sent.append(c)
        return c

    factors = [near(e_low, mixing[:modes], TN), near(e_high, mixing[modes:], TN)]
    pass_on = [tell_factors(1, factors)]

    def add(k, so_far):
        x_spread(k).wait_recv()
        return so_far + x_in[k - 1].astype(F32)

    shared = x_own[x_part(me), :]
    if total <= 16:
        for k in range(1, total):
            shared = add(k, shared)
    else:
        shared = lax.fori_loop(1, total, add, shared)
    x_all[x_part(me), :] = shared.astype(BF16)
    each(lambda k: x_gather(k).start())
    pass_on.append(tell_diagonal(1, pair, mixing))
    for level in range(1, levels):
        count = 1 << level
        if level > 1:
            pass_on = [tell_factors(level, factors), tell_diagonal(level, pair, mixing)]
        for c in pass_on:
            c.wait_recv()
        high_side = snap // count % 2 == 1
        lows, highs = [], []
        for i in range(count):
            own, theirs = cf_mine[level - 1, i], cf_got[level - 1, i]
            lows.append(jnp.where(high_side, theirs, own))
            highs.append(jnp.where(high_side, own, theirs))
        own, theirs = b_mine[level - 1].astype(F32), b_got[level - 1].astype(F32)
        d_low = jnp.where(high_side, theirs, own)
        d_high = jnp.where(high_side, own, theirs)
        base = snap // (2 * count) * count

        def between(a, i, b, j):
            pa, pb = base + a, base + count // 2 + b
            place = pa * (2 * half - pa - 1) // 2 + pb - pa - 1
            return x_all[pl.ds(pl.multiple_of((place * 4 + i * 2 + j) * 128, 128), 128), :]

        every = [(a, i) for a in range(count // 2) for i in (0, 1)]
        inner = [r + c for r in every for c in every]
        if level < levels - 1:
            wait_gathered(level)
            cross = jnp.zeros((modes, modes), F32)
            for a, i, b, j in inner:
                right = dot(between(a, i, b, j), highs[2 * b + j])
                cross = cross + wide(lows[2 * a + i].T, right)
            pair, mixing = merged(level, d_low, cross, d_high)
            low_mix, high_mix = mixing[:modes], mixing[modes:]
            factors = [wide(f, low_mix) for f in lows] + [wide(f, high_mix) for f in highs]
            continue
        low_start, high_start = start_of(level)[:modes], start_of(level)[modes:]
        low_ahead = [wide(f, low_start) for f in lows]
        high_ahead = [wide(f, high_start) for f in highs]
        top, bottom = near(d_low, low_start), near(d_high, high_start)
        low_across = jnp.concatenate([f.T for f in lows], axis=1)
        high_across = jnp.concatenate([f.T for f in highs], axis=1)
        low_ahead = split(jnp.concatenate(low_ahead, axis=0))
        high_ahead = split(jnp.concatenate(high_ahead, axis=0))
        wait_gathered(level)
        table = {at: between(*at) for at in inner}
        block = jnp.concatenate(
            [jnp.concatenate([table[r + c] for c in every], axis=1) for r in every], axis=0
        )
        right = dot(block, high_ahead[0]) + dot(block, high_ahead[1])
        left = dot(block, low_ahead[0], TN) + dot(block, low_ahead[1], TN)
        z = jnp.concatenate([top + wide(low_across, right), bottom + wide(high_across, left)], axis=0)
        inverse = inverse_factor(near(z, z, TN))
        coefficients = [wide(f, z[:modes]) for f in lows] + [wide(f, z[modes:]) for f in highs]
        factors = [near(c, inverse, NT) for c in coefficients]
    depth = jnp.concatenate([f.astype(BF16) for f in factors], axis=0)
    out[...] = dot(jnp.concatenate([panels[i] for i in range(s)], axis=1), depth).astype(BF16)

    @pl.when(space == chosen)
    def _():
        for c in told:
            c.wait_send()

    for part in (0, 1):
        for k in range(1, n):
            spread(part, k).wait_send()
            gather(part, k).wait_send()
    for c in out_copies + pair_copies + [swap] + steps + tell + [collect] + sent:
        c.wait_send()
    each(lambda k: x_spread(k).wait_send())
    each(lambda k: x_gather(k).wait_send())


def padded(rows, parts):
    share = -(-rows // parts)
    return -(-share // 16) * 16


def local(snapshots, factor_blocks, factor_cols, factor_counts, start_basis, merge_starts):
    n = lax.axis_size("space")
    s = lax.axis_size("snap")
    total = s * n
    size, modes = start_basis.shape
    rows = snapshots.shape[0] // s
    half = s // 2
    width = factor_blocks.shape[2]
    blocked = snapshots.reshape(snapshots.shape[0] // width, width, size)
    levels = s.bit_length() - 1
    x_share = padded(4 * (half * (half - 1) // 2) * 128, total)
    dma = pltpu.SemaphoreType.DMA
    shares = [padded(len(blocks) * 128, n) for blocks in parts_of(size)]
    table = jnp.concatenate([factor_cols.T, factor_counts[None]])
    scratch = [
        pltpu.VMEM((blocked.shape[0], width, size // 2), BF16),
        pltpu.VMEM(factor_blocks.shape, BF16),
        pltpu.VMEM(snapshots.shape, BF16),
        dma((3, CHUNKS)),
        *[pltpu.VMEM((share * n, 128), F32) for share in shares],
        pltpu.VMEM((size, size), BF16),
        pltpu.VMEM((size, modes), BF16),
        pltpu.VMEM((modes // 2, modes), BF16),
        pltpu.VMEM((modes // 2, modes), BF16),
        dma((2, n - 1)),
        pltpu.VMEM((s, rows, modes), BF16),
        pltpu.VMEM((half, rows, modes), BF16),
        dma((2, s)),
        dma((2, half)),
        pltpu.VMEM((modes, modes), F32),
        pltpu.VMEM((modes, modes), BF16),
        pltpu.VMEM((modes // 2, modes), BF16),
        pltpu.VMEM((modes // 2, modes), BF16),
        pltpu.VMEM((n - 1, modes // 2, modes), BF16),
        pltpu.VMEM((modes // 2, modes), BF16),
        pltpu.VMEM((modes // 2, modes), BF16),
        pltpu.VMEM((modes, modes), F32),
        dma((2,)),
        dma((2, n - 1)),
        dma((2,)),
        pltpu.VMEM((modes, modes), F32),
        pltpu.VMEM((modes, modes), F32),
        pltpu.VMEM((modes, modes), F32),
        pltpu.VMEM((modes, modes), F32),
        dma((2, 2)),
        pltpu.VMEM((x_share * total, 128), F32),
        pltpu.VMEM((x_share * total, 128), BF16),
        pltpu.VMEM((total - 1, x_share, 128), BF16),
        pltpu.VMEM((x_share * total, 128), BF16),
        dma((2, total - 1)),
        dma((2, total - 1)),
        pltpu.VMEM((levels - 1, half, modes, modes), BF16),
        pltpu.VMEM((levels - 1, half, modes, modes), BF16),
        pltpu.VMEM((levels - 1, modes, modes), BF16),
        pltpu.VMEM((levels - 1, modes, modes), BF16),
        dma((2, levels - 1, 2)),
        pltpu.VMEM((snapshots.shape[0], modes), BF16),
        pltpu.VMEM(start_basis.shape, F32),
        pltpu.VMEM(merge_starts.shape, F32),
        dma((2,)),
        *[pltpu.VMEM((share * n, 128), BF16) for share in shares],
        *[pltpu.VMEM((n - 1, share, 128), BF16) for share in shares],
        *[pltpu.VMEM((share * n, 128), BF16) for share in shares],
        *[dma((2, n - 1)) for share in shares],
        *[dma((2, n - 1)) for share in shares],
        pltpu.VMEM((blocked.shape[0], width, size // 2), BF16),
    ]
    return pl.pallas_call(
        functools.partial(kernel, n, s),
        in_specs=[SMEM, ANY, ANY, ANY, ANY],
        out_specs=VMEM,
        out_shape=jax.ShapeDtypeStruct((rows, modes), BF16),
        scratch_shapes=scratch,
        compiler_params=pltpu.CompilerParams(
            collective_id=0, has_side_effects=True, vmem_limit_bytes=VMEM_LIMIT
        ),
        name="modes",
    )(table, blocked, factor_blocks, start_basis, merge_starts)


def solution(mesh):
    return jax.shard_map(
        local,
        mesh=mesh,
        in_specs=(
            P("space", ("groups", "snap")),
            P("space", None, None, None),
            P("space", None),
            P("space"),
            P(("groups", "snap"), None),
            P(),
        ),
        out_specs=P(("space", "snap"), "groups"),
        check_vma=False,
    )
```

```python
import functools

import jax
import jax.numpy as jnp
from jax import lax
from jax.experimental import pallas as pl
from jax.experimental.pallas import tpu as pltpu
from jax.sharding import PartitionSpec as P

HIGH = lax.Precision.HIGHEST
MESH = pl.DeviceIdType.MESH
F32 = jnp.float32
BF16 = jnp.bfloat16
VMEM = pl.BlockSpec(memory_space=pltpu.VMEM)
SMEM = pl.BlockSpec(memory_space=pltpu.SMEM)
ANY = pl.BlockSpec(memory_space=pl.ANY)
CHUNKS = 4
VMEM_LIMIT = 54835 * 1024
RIDGE = 1e-4
TN = (((0,), (0,)), ((), ()))
NT = (((1,), (1,)), ((), ()))
NN = (((1,), (0,)), ((), ()))


def dot(a, b, dims=NN, precision=None):
    return lax.dot_general(a, b, dims, precision=precision, preferred_element_type=F32)


def split(x):
    high = x.astype(BF16)
    return high, (x - high.astype(F32)).astype(BF16)


def wide(a, x):
    size = x.shape[1]
    both = dot(a, jnp.concatenate(split(x), axis=1))
    return both[:, :size] + both[:, size:]


def upper_blocks(count):
    return [(i, j) for i in range(count) for j in range(i, count)]


def flipped(index, bit):
    return index + (1 - 2 * (index // (1 << bit) % 2)) * (1 << bit)


def remote(source, target, send, recv, device):
    return pltpu.make_async_remote_copy(
        src_ref=source,
        dst_ref=target,
        send_sem=send,
        recv_sem=recv,
        device_id=device,
        device_id_type=MESH,
    )


def eye(size):
    row = lax.broadcasted_iota(jnp.int32, (size, size), 0)
    col = lax.broadcasted_iota(jnp.int32, (size, size), 1)
    return row == col


def trace(x):
    return jnp.sum(jnp.where(eye(x.shape[0]), x, 0.0))


def rows_of(block):
    return pl.ds(block * 128, 128)


def eliminate(a, e, lane):
    a, e = list(a), list(e)
    groups = len(a)
    row = lax.broadcasted_iota(jnp.int32, (8, 128), 0)
    scale = [jnp.zeros((8, 128), F32)] * groups

    def spread(x, k):
        return jnp.broadcast_to(x[k : k + 1, :], (8, 128))

    def columns(g, first):
        return {
            h: [
                jnp.broadcast_to(a[h][:, lane + 8 * g + k : lane + 8 * g + k + 1], (8, 128))
                for k in range(8)
            ]
            for h in range(first, groups)
        }

    ahead = columns(0, 0)
    for g in range(groups):
        cols = {h: ahead[h] for h in range(g, groups)}
        ahead = columns(g + 1, g) if g + 1 < groups else None
        for k in range(0, 8, 2):
            p, q, r = spread(cols[g][k], k), spread(cols[g][k], k + 1), spread(cols[g][k + 1], k + 1)
            det = p * r - q * q
            over_det = 1.0 / det
            over_p = 1.0 / p
            i, j, l = r * over_det, q * over_det, p * over_det
            scale[g] = jnp.where(row == k, lax.rsqrt(p), scale[g])
            scale[g] = jnp.where(row == k + 1, lax.rsqrt(det * over_p), scale[g])
            a_rows = spread(a[g], k), spread(a[g], k + 1)
            e_rows = spread(e[g], k), spread(e[g], k + 1)
            heads = {
                m: (spread(cols[g][m], k), spread(cols[g][m], k + 1)) for m in range(k + 2, 8)
            }
            far = []
            if ahead is not None:
                far = [(spread(x, k), spread(x, k + 1)) for x in ahead[g]]
            for h in range(g, groups):
                c, d = cols[h][k], cols[h][k + 1]
                f1 = c * i - d * j
                f2 = d * l - c * j
                if h == g:
                    f1 = jnp.where(row > k + 1, f1, jnp.where(row == k + 1, q * over_p, 0.0))
                    f2 = jnp.where(row > k + 1, f2, 0.0)
                for m in range(k + 2, 8):
                    cols[h][m] = cols[h][m] - (f1 * heads[m][0] + f2 * heads[m][1])
                for m, (x, y) in enumerate(far):
                    ahead[h][m] = ahead[h][m] - (f1 * x + f2 * y)
                a[h] = a[h] - (f1 * a_rows[0] + f2 * a_rows[1])
                e[h] = e[h] - (f1 * e_rows[0] + f2 * e_rows[1])
    return [x * s for x, s in zip(a, scale)], [x * s for x, s in zip(e, scale)]


def thirds(x):
    high = x.astype(BF16)
    rest = x - high.astype(F32)
    middle = rest.astype(BF16)
    return high, middle, (rest - middle.astype(F32)).astype(BF16)


def outer(a, b):
    a, b = thirds(a), thirds(b)
    left = jnp.concatenate([a[0], a[0], a[1], a[0], a[2], a[1]], axis=0)
    right = jnp.concatenate([b[0], b[1], b[0], b[2], b[0], b[1]], axis=0)
    return dot(left, right, TN)


def inverse_factor(cross):
    size = cross.shape[0]
    diagonal = jnp.where(eye(size), cross, 0.0)
    down = lax.rsqrt(jnp.sum(diagonal, axis=1, keepdims=True))
    along = lax.rsqrt(jnp.sum(diagonal, axis=0, keepdims=True))
    both = jnp.concatenate(
        [cross * down * along, jnp.where(eye(size), jnp.broadcast_to(along, cross.shape), 0.0)],
        axis=1,
    )
    done = []
    for p in range(size // 32):
        rows = [both[p * 32 + 8 * g : p * 32 + 8 * g + 8] for g in range(4)]
        a, e = eliminate([r[:, :size] for r in rows], [r[:, size:] for r in rows], p * 32)
        a, e = jnp.concatenate(a, axis=0), jnp.concatenate(e, axis=0)
        done.append(e)
        if p < size // 32 - 1:
            both = both - outer(a, jnp.concatenate([a, e], axis=1))
    return jnp.concatenate(done, axis=0)


def near(a, b, dims=NN):
    a, b = split(a), split(b)
    return dot(a[0], b[0], dims) + (dot(a[0], b[1], dims) + dot(a[1], b[0], dims))


def packed_factor(unit):
    half = unit.shape[0] // 2
    row = lax.broadcasted_iota(jnp.int32, (half, half), 0)
    col = lax.broadcasted_iota(jnp.int32, (half, half), 1)
    first = jnp.where(row > col, unit[:half, :half], 0.0)
    second = jnp.where(row > col, unit[half:, half:], 0.0)
    return jnp.concatenate([first + second.T, unit[half:, :half]], axis=1)


def unpacked_factor(packed):
    half = packed.shape[0]
    row = lax.broadcasted_iota(jnp.int32, (half, half), 0)
    col = lax.broadcasted_iota(jnp.int32, (half, half), 1)
    both = packed[:, :half]
    ones = (row == col).astype(F32)
    first = jnp.where(row > col, both, ones)
    second = jnp.where(row > col, both.T, ones)
    top = jnp.concatenate([first, jnp.zeros((half, half), F32)], axis=1)
    return jnp.concatenate([top, jnp.concatenate([packed[:, half:], second], axis=1)], axis=0)


def orthonormal(z):
    return near(z, inverse_factor(near(z, z, TN)), NT)


def sandwich(outer, inner):
    return dot(outer, dot(inner, outer, NT, HIGH), precision=HIGH)


def load_and_weigh(table, snaps_in, blocks_in, snaps, blocks, weighted, sems, greet, use):
    row_blocks, slots, width, _ = blocks.shape
    per = row_blocks // CHUNKS
    side = snaps[0].shape[2]

    def snap_load(h, c):
        at = pl.ds(c * per, per)
        source = snaps_in.at[at, pl.ds(0, width), pl.ds(h * side, side)]
        return pltpu.make_async_copy(source, snaps[h].at[at], sems.at[h, c])

    def block_load(c):
        at = pl.ds(c * per, per)
        return pltpu.make_async_copy(blocks_in.at[at], blocks.at[at], sems.at[2, c])

    for c in range(CHUNKS):
        snap_load(0, c).start()
    for c in range(CHUNKS):
        block_load(c).start()
    for c in range(CHUNKS):
        snap_load(1, c).start()
    greet()
    for h in (0, 1):
        for c in range(CHUNKS):
            snap_load(h, c).wait()

        def chunk(c, carry):
            if h == 0:
                block_load(c).wait()

            def weigh(k, carry):
                row = c * per + k
                count = table[slots, row]
                factors = []
                sources = []
                for slot in range(slots):
                    factor = blocks[row, slot]
                    live = jnp.full(factor.shape, count, jnp.int32) > slot
                    factors.append(jnp.where(live, factor, jnp.zeros_like(factor)))
                    sources.append(snaps[h][table[slot, row]])
                product = dot(jnp.concatenate(factors, axis=1), jnp.concatenate(sources, axis=0))
                at = pl.ds(pl.multiple_of(row * width, width), width)
                weighted[at, h * side : (h + 1) * side] = product.astype(BF16)
                return carry

            lax.fori_loop(0, per, weigh, 0, unroll=8)
            return carry

        lax.fori_loop(0, CHUNKS, chunk, 0)
        use(h)


def parts_of(size):
    blocks = upper_blocks(size // 128)
    half = size // 256
    return [b for b in blocks if b[1] < half], [b for b in blocks if b[1] >= half]


def unpack(flats, full):
    for flat, blocks in zip(flats, parts_of(full.shape[0])):
        for index, (i, j) in enumerate(blocks):
            block = flat[index * 128 : (index + 1) * 128, :]
            full[i * 128 : (i + 1) * 128, j * 128 : (j + 1) * 128] = block
            if i != j:
                full[j * 128 : (j + 1) * 128, i * 128 : (i + 1) * 128] = block.T


def kernel(n, s, table, snaps_in, blocks_in, start_in, starts_in, out, *scratch):
    (blocks, weighted, load_sems) = scratch[1:4]
    snaps = scratch[0], scratch[56]
    y, start, starts, start_sems = scratch[42:46]
    firsts = (4, 46, 48, 50, 52, 54)
    g_own, g_out, g_in, g_all, g_sems, a_sems = [scratch[a : a + 2] for a in firsts]
    (full, vectors, t_out, t_in, t_sems) = scratch[6:11]
    (panels, got, p_sems, q_sems) = scratch[11:15]
    (mine_all, c_out, c_came, z_out, z_came, sum_out, sum_came, cross_all) = scratch[15:23]
    (c_sems, z_sems, s_sems) = scratch[23:26]
    (e_mine, e_got, d_mine, d_got, e_sems) = scratch[26:31]
    (x_own, x_out, x_in, x_all, xr_sems, xa_sems) = scratch[31:37]
    (cf_mine, cf_got, b_mine, b_got, b_sems) = scratch[37:42]
    snap = lax.axis_index("snap")
    space = lax.axis_index("space")
    total = s * n
    me = snap * n + space
    half = s // 2
    bit = snap % 2
    upper = bit == 1
    partner = flipped(snap, 0)
    modes = vectors.shape[1]
    size = full.shape[0]
    rows = panels.shape[1]
    barrier = pltpu.get_barrier_semaphore()

    def device(k):
        other = lax.rem(me + k, total)
        return {"snap": other // n, "space": lax.rem(other, n)}

    small_loads = [
        pltpu.make_async_copy(start_in, start, start_sems.at[0]),
        pltpu.make_async_copy(starts_in, starts, start_sems.at[1]),
    ]

    def greet():
        for c in small_loads:
            c.start()

        def signal(k, carry):
            pl.semaphore_signal(barrier, inc=1, device_id=device(k), device_id_type=MESH)
            return carry

        lax.fori_loop(1, total, signal, 0)

    def share_of(part, index):
        share = g_in[part].shape[1]
        return pl.ds(pl.multiple_of(index * share, share), share)

    def spread(part, k):
        other = lax.rem(space + k, n)
        return remote(
            g_out[part].at[share_of(part, other)],
            g_in[part].at[k - 1],
            g_sems[part].at[0, k - 1],
            g_sems[part].at[1, k - 1],
            {"space": other},
        )

    def gather(part, k):
        return remote(
            g_all[part].at[share_of(part, space)],
            g_all[part].at[share_of(part, space)],
            a_sems[part].at[0, k - 1],
            a_sems[part].at[1, k - 1],
            {"space": lax.rem(space + k, n)},
        )

    def keep(part, index, block):
        at = slice(index * 128, (index + 1) * 128)
        g_own[part][at, :] = block
        g_out[part][at, :] = block.astype(BF16)

    def part_ready(part):
        side = size // 2
        blocks = parts_of(size)[part]
        right = weighted[:, part * side : (part + 1) * side]
        for h in range(part + 1):
            product = dot(weighted[:, h * side : (h + 1) * side], right, TN)
            for index, (i, j) in enumerate(blocks):
                if i * 128 // side == h:
                    row, col = i * 128 - h * side, j * 128 - part * side
                    keep(part, index, product[row : row + 128, col : col + 128])
        used = len(blocks) * 128
        rest = g_own[part].shape[0] - used
        if rest:
            g_own[part][used:, :] = jnp.zeros((rest, 128), F32)
            g_out[part][used:, :] = jnp.zeros((rest, 128), BF16)
        if part == 0:
            pl.semaphore_wait(barrier, total - 1)
        for k in range(1, n):
            spread(part, k).start()

    def part_summed(part):
        mine = g_own[part][share_of(part, space), :]
        for k in range(1, n):
            spread(part, k).wait_recv()
            mine = mine + g_in[part][k - 1].astype(F32)
        g_all[part][share_of(part, space), :] = mine.astype(BF16)
        for k in range(1, n):
            gather(part, k).start()

    load_and_weigh(
        table, snaps_in, blocks_in, snaps, blocks, weighted, load_sems, greet, part_ready
    )
    part_summed(0)

    chosen = n // 2
    for c in small_loads:
        c.wait()
    begin = start[...] * (1.0 / jnp.max(jnp.abs(start[...])))
    told = [
        remote(t_out, t_in, t_sems.at[0, k - 1], t_sems.at[1, 0], {"space": lax.rem(chosen + k, n)})
        for k in range(1, n)
    ]

    @pl.when(space == chosen)
    def _():
        unpack(g_out, full)
        first = dot(full[...], begin.astype(BF16)).astype(BF16)
        cross = dot(first, first, TN)
        scale = modes / jnp.maximum(trace(cross), 1e-30)
        factor = inverse_factor(cross * scale + jnp.where(eye(modes), RIDGE, 0.0))
        unit = factor / jnp.sum(jnp.where(eye(modes), factor, 0.0), axis=1, keepdims=True)
        packed = packed_factor(unit).astype(BF16)
        t_out[...] = packed
        t_in[...] = packed
        for c in told:
            c.start()

    part_summed(1)

    @pl.when(space != chosen)
    def _():
        told[0].wait_recv()

    normal = unpacked_factor(t_in[...].astype(F32)).astype(BF16)
    for part in (0, 1):
        for k in range(1, n):
            gather(part, k).wait_recv()
    unpack(g_all, full)
    trace_of = 0.0
    for i in range(size // 128):
        trace_of = trace_of + trace(
            full[i * 128 : (i + 1) * 128, i * 128 : (i + 1) * 128].astype(F32)
        )
    scale = size / trace_of
    first = wide(full[...], begin) * scale

    high, low = split(first)
    between = dot(high, normal, NT) + dot(low, normal, NT)
    vectors[...] = (wide(full[...], between) * scale).astype(BF16)

    def rows_at(q):
        return pl.ds(pl.multiple_of(q * rows, rows), rows)

    def piece(q):
        return dot(weighted[rows_at(q), :], vectors[...]).astype(BF16)

    def mine_at(q):
        return y.at[rows_at(q)]

    out_copies = []
    arrivals = []
    for h in range(1, half):
        for side in (0, 1):
            q = lax.rem(snap // 2 + h, half) * 2 + side
            source = lax.rem(snap // 2 + half - h, half) * 2 + side
            y[rows_at(q), :] = piece(q)
            send = p_sems.at[0, 2 * h + side]
            c = remote(mine_at(q), panels.at[snap], send, p_sems.at[1, 2 * h + bit], {"snap": q})
            c.start()
            out_copies.append(c)
            arrivals.append(
                remote(mine_at(q), panels.at[source], send, p_sems.at[1, 2 * h + side], {"snap": q})
            )
    pair_copies = []
    for h in range(half):
        q = lax.rem(snap // 2 + h, half) * 2 + 1 - bit
        if h == 0:
            y[rows_at(q), :] = piece(q)
        c = remote(mine_at(q), got.at[h], q_sems.at[0, h], q_sems.at[1, h], {"snap": partner})
        c.start()
        pair_copies.append(c)
    y[rows_at(snap), :] = piece(snap)

    cross = jnp.zeros((modes, modes), F32)
    for h in range(half):
        q = lax.rem(snap // 2 + h, half) * 2 + bit
        pair_copies[h].wait_recv()
        cross = cross + dot(y[rows_at(q), :], got[h], TN)
    panels[snap] = y[rows_at(snap), :]
    panels[partner] = got[0]
    cross = jnp.where(upper, cross.T, cross)
    part_rows = modes // 2

    def part_of(index):
        return pl.ds(pl.multiple_of(index * part_rows, part_rows), part_rows)

    mine_all[...] = cross
    c_out[...] = cross.astype(BF16)
    swap = remote(
        c_out.at[part_of(1 - bit)], c_came, c_sems.at[0], c_sems.at[1], {"snap": partner}
    )
    swap.start()
    moved = dot(full[...], vectors[...])
    product = wide(vectors[...].T, moved)
    square = dot(vectors[...], vectors[...], TN)
    swap.wait_recv()
    part = mine_all[part_of(bit), :] + c_came[...].astype(F32)
    z_out[...] = part.astype(BF16)
    steps = [
        remote(
            z_out,
            z_came.at[k - 1],
            z_sems.at[0, k - 1],
            z_sems.at[1, k - 1],
            {"space": lax.rem(space + k, n)},
        )
        for k in range(1, n)
    ]
    for c in steps:
        c.start()
    e_mine[...] = inverse_factor(square)
    d_mine[...] = sandwich(e_mine[...], product)
    tell = [
        remote(e_mine, e_got, e_sems.at[0, 0], e_sems.at[1, 0], {"snap": partner}),
        remote(d_mine, d_got, e_sems.at[0, 1], e_sems.at[1, 1], {"snap": partner}),
    ]
    for c in tell:
        c.start()
    for k, c in enumerate(steps):
        c.wait_recv()
        part = part + z_came[k].astype(F32)
    sum_out[...] = part.astype(BF16)
    collect = remote(sum_out, sum_came, s_sems.at[0], s_sems.at[1], {"snap": partner})
    collect.start()
    for c in tell:
        c.wait_recv()
    collect.wait_recv()
    cross_all[part_of(bit), :] = sum_out[...].astype(F32)
    cross_all[part_of(1 - bit), :] = sum_came[...].astype(F32)
    e_low = jnp.where(upper, e_got[...], e_mine[...])
    e_high = jnp.where(upper, e_mine[...], e_got[...])
    d_low = jnp.where(upper, d_got[...], d_mine[...])
    d_high = jnp.where(upper, d_mine[...], d_got[...])
    cross = dot(e_low, dot(cross_all[...], e_high, NT, HIGH), precision=HIGH)

    def start_of(level):
        return starts[s - (s >> level) + snap // (1 << (level + 1))]

    def wait_gathered(level):
        if level == 1:
            each(lambda k: x_gather(k).wait_recv())

    def merged(level, d_low, cross, d_high):
        pair = jnp.concatenate(
            [
                jnp.concatenate([d_low, cross], axis=1),
                jnp.concatenate([cross.T, d_high], axis=1),
            ],
            axis=0,
        )
        return pair, orthonormal(near(pair, start_of(level)))

    def diagonal(pair, mixing):
        return near(mixing, near(pair, mixing), TN)

    for c in arrivals:
        c.wait_recv()
    done = 0
    for low_pair in range(half):
        for high_pair in range(low_pair + 1, half):
            sides = [
                jnp.concatenate([panels[2 * p], panels[2 * p + 1]], axis=1)
                for p in (low_pair, high_pair)
            ]
            blocks_of = dot(sides[0], sides[1], TN)
            for i in range(2):
                for j in range(2):
                    at = slice(done * 128, (done + 1) * 128)
                    block = blocks_of[i * modes : (i + 1) * modes, j * modes : (j + 1) * modes]
                    x_own[at, :] = block
                    x_out[at, :] = block.astype(BF16)
                    done = done + 1
    if done * 128 < x_own.shape[0]:
        x_own[done * 128 :, :] = jnp.zeros((x_own.shape[0] - done * 128, 128), F32)
        x_out[done * 128 :, :] = jnp.zeros((x_own.shape[0] - done * 128, 128), BF16)
    x_share = x_in.shape[1]

    def x_part(index):
        return pl.ds(pl.multiple_of(index * x_share, x_share), x_share)

    def x_spread(k):
        return remote(
            x_out.at[x_part(lax.rem(me + k, total))],
            x_in.at[k - 1],
            xr_sems.at[0, k - 1],
            xr_sems.at[1, k - 1],
            device(k),
        )

    def x_gather(k):
        return remote(
            x_all.at[x_part(me)],
            x_all.at[x_part(me)],
            xa_sems.at[0, k - 1],
            xa_sems.at[1, k - 1],
            device(k),
        )

    def each(act):
        if total <= 16:
            for k in sorted(range(1, total), key=lambda k: abs(2 * k - total)):
                act(k)
            return

        def step(k, carry):
            act(k)
            return carry

        lax.fori_loop(1, total, step, 0)

    each(lambda k: x_spread(k).start())
    pair, mixing = merged(0, d_low, cross, d_high)

    levels = s.bit_length() - 1
    sent = []

    def tell_factors(level, factors):
        count = 1 << level
        for i in range(count):
            cf_mine[level - 1, i] = factors[i].astype(BF16)
        c = remote(
            cf_mine.at[level - 1, pl.ds(0, count)],
            cf_got.at[level - 1, pl.ds(0, count)],
            b_sems.at[0, level - 1, 0],
            b_sems.at[1, level - 1, 0],
            {"snap": flipped(snap, level)},
        )
        c.start()
        sent.append(c)
        return c

    def tell_diagonal(level, pair, mixing):
        b_mine[level - 1] = diagonal(pair, mixing).astype(BF16)
        c = remote(
            b_mine.at[level - 1],
            b_got.at[level - 1],
            b_sems.at[0, level - 1, 1],
            b_sems.at[1, level - 1, 1],
            {"snap": flipped(snap, level)},
        )
        c.start()
        sent.append(c)
        return c

    factors = [near(e_low, mixing[:modes], TN), near(e_high, mixing[modes:], TN)]
    pass_on = [tell_factors(1, factors)]

    def add(k, so_far):
        x_spread(k).wait_recv()
        return so_far + x_in[k - 1].astype(F32)

    shared = x_own[x_part(me), :]
    if total <= 16:
        for k in range(1, total):
            shared = add(k, shared)
    else:
        shared = lax.fori_loop(1, total, add, shared)
    x_all[x_part(me), :] = shared.astype(BF16)
    each(lambda k: x_gather(k).start())
    pass_on.append(tell_diagonal(1, pair, mixing))
    for level in range(1, levels):
        count = 1 << level
        if level > 1:
            pass_on = [tell_factors(level, factors), tell_diagonal(level, pair, mixing)]
        for c in pass_on:
            c.wait_recv()
        high_side = snap // count % 2 == 1
        lows, highs = [], []
        for i in range(count):
            own, theirs = cf_mine[level - 1, i], cf_got[level - 1, i]
            lows.append(jnp.where(high_side, theirs, own))
            highs.append(jnp.where(high_side, own, theirs))
        own, theirs = b_mine[level - 1].astype(F32), b_got[level - 1].astype(F32)
        d_low = jnp.where(high_side, theirs, own)
        d_high = jnp.where(high_side, own, theirs)
        base = snap // (2 * count) * count

        def between(a, i, b, j):
            pa, pb = base + a, base + count // 2 + b
            place = pa * (2 * half - pa - 1) // 2 + pb - pa - 1
            return x_all[pl.ds(pl.multiple_of((place * 4 + i * 2 + j) * 128, 128), 128), :]

        every = [(a, i) for a in range(count // 2) for i in (0, 1)]
        inner = [r + c for r in every for c in every]
        if level < levels - 1:
            wait_gathered(level)
            cross = jnp.zeros((modes, modes), F32)
            for a, i, b, j in inner:
                right = dot(between(a, i, b, j), highs[2 * b + j])
                cross = cross + wide(lows[2 * a + i].T, right)
            pair, mixing = merged(level, d_low, cross, d_high)
            low_mix, high_mix = mixing[:modes], mixing[modes:]
            factors = [wide(f, low_mix) for f in lows] + [wide(f, high_mix) for f in highs]
            continue
        low_start, high_start = start_of(level)[:modes], start_of(level)[modes:]
        low_ahead = [wide(f, low_start) for f in lows]
        high_ahead = [wide(f, high_start) for f in highs]
        top, bottom = near(d_low, low_start), near(d_high, high_start)
        low_across = jnp.concatenate([f.T for f in lows], axis=1)
        high_across = jnp.concatenate([f.T for f in highs], axis=1)
        low_ahead = split(jnp.concatenate(low_ahead, axis=0))
        high_ahead = split(jnp.concatenate(high_ahead, axis=0))
        wait_gathered(level)
        table = {at: between(*at) for at in inner}
        block = jnp.concatenate(
            [jnp.concatenate([table[r + c] for c in every], axis=1) for r in every], axis=0
        )
        right = dot(block, high_ahead[0]) + dot(block, high_ahead[1])
        left = dot(block, low_ahead[0], TN) + dot(block, low_ahead[1], TN)
        z = jnp.concatenate([top + wide(low_across, right), bottom + wide(high_across, left)], axis=0)
        inverse = inverse_factor(near(z, z, TN))
        coefficients = [wide(f, z[:modes]) for f in lows] + [wide(f, z[modes:]) for f in highs]
        factors = [near(c, inverse, NT) for c in coefficients]
    depth = jnp.concatenate([f.astype(BF16) for f in factors], axis=0)
    out[...] = dot(jnp.concatenate([panels[i] for i in range(s)], axis=1), depth).astype(BF16)

    @pl.when(space == chosen)
    def _():
        for c in told:
            c.wait_send()

    for part in (0, 1):
        for k in range(1, n):
            spread(part, k).wait_send()
            gather(part, k).wait_send()
    for c in out_copies + pair_copies + [swap] + steps + tell + [collect] + sent:
        c.wait_send()
    each(lambda k: x_spread(k).wait_send())
    each(lambda k: x_gather(k).wait_send())


def padded(rows, parts):
    share = -(-rows // parts)
    return -(-share // 16) * 16


def local(snapshots, factor_blocks, factor_cols, factor_counts, start_basis, merge_starts):
    n = lax.axis_size("space")
    s = lax.axis_size("snap")
    total = s * n
    size, modes = start_basis.shape
    rows = snapshots.shape[0] // s
    half = s // 2
    width = factor_blocks.shape[2]
    blocked = snapshots.reshape(snapshots.shape[0] // width, width, size)
    levels = s.bit_length() - 1
    x_share = padded(4 * (half * (half - 1) // 2) * 128, total)
    dma = pltpu.SemaphoreType.DMA
    shares = [padded(len(blocks) * 128, n) for blocks in parts_of(size)]
    table = jnp.concatenate([factor_cols.T, factor_counts[None]])
    scratch = [
        pltpu.VMEM((blocked.shape[0], width, size // 2), BF16),
        pltpu.VMEM(factor_blocks.shape, BF16),
        pltpu.VMEM(snapshots.shape, BF16),
        dma((3, CHUNKS)),
        *[pltpu.VMEM((share * n, 128), F32) for share in shares],
        pltpu.VMEM((size, size), BF16),
        pltpu.VMEM((size, modes), BF16),
        pltpu.VMEM((modes // 2, modes), BF16),
        pltpu.VMEM((modes // 2, modes), BF16),
        dma((2, n - 1)),
        pltpu.VMEM((s, rows, modes), BF16),
        pltpu.VMEM((half, rows, modes), BF16),
        dma((2, s)),
        dma((2, half)),
        pltpu.VMEM((modes, modes), F32),
        pltpu.VMEM((modes, modes), BF16),
        pltpu.VMEM((modes // 2, modes), BF16),
        pltpu.VMEM((modes // 2, modes), BF16),
        pltpu.VMEM((n - 1, modes // 2, modes), BF16),
        pltpu.VMEM((modes // 2, modes), BF16),
        pltpu.VMEM((modes // 2, modes), BF16),
        pltpu.VMEM((modes, modes), F32),
        dma((2,)),
        dma((2, n - 1)),
        dma((2,)),
        pltpu.VMEM((modes, modes), F32),
        pltpu.VMEM((modes, modes), F32),
        pltpu.VMEM((modes, modes), F32),
        pltpu.VMEM((modes, modes), F32),
        dma((2, 2)),
        pltpu.VMEM((x_share * total, 128), F32),
        pltpu.VMEM((x_share * total, 128), BF16),
        pltpu.VMEM((total - 1, x_share, 128), BF16),
        pltpu.VMEM((x_share * total, 128), BF16),
        dma((2, total - 1)),
        dma((2, total - 1)),
        pltpu.VMEM((levels - 1, half, modes, modes), BF16),
        pltpu.VMEM((levels - 1, half, modes, modes), BF16),
        pltpu.VMEM((levels - 1, modes, modes), BF16),
        pltpu.VMEM((levels - 1, modes, modes), BF16),
        dma((2, levels - 1, 2)),
        pltpu.VMEM((snapshots.shape[0], modes), BF16),
        pltpu.VMEM(start_basis.shape, F32),
        pltpu.VMEM(merge_starts.shape, F32),
        dma((2,)),
        *[pltpu.VMEM((share * n, 128), BF16) for share in shares],
        *[pltpu.VMEM((n - 1, share, 128), BF16) for share in shares],
        *[pltpu.VMEM((share * n, 128), BF16) for share in shares],
        *[dma((2, n - 1)) for share in shares],
        *[dma((2, n - 1)) for share in shares],
        pltpu.VMEM((blocked.shape[0], width, size // 2), BF16),
    ]
    return pl.pallas_call(
        functools.partial(kernel, n, s),
        in_specs=[SMEM, ANY, ANY, ANY, ANY],
        out_specs=VMEM,
        out_shape=jax.ShapeDtypeStruct((rows, modes), BF16),
        scratch_shapes=scratch,
        compiler_params=pltpu.CompilerParams(
            collective_id=0, has_side_effects=True, vmem_limit_bytes=VMEM_LIMIT
        ),
        name="modes",
    )(table, blocked, factor_blocks, start_basis, merge_starts)


def solution(mesh):
    return jax.shard_map(
        local,
        mesh=mesh,
        in_specs=(
            P("space", ("groups", "snap")),
            P("space", None, None, None),
            P("space", None),
            P("space"),
            P(("groups", "snap"), None),
            P(),
        ),
        out_specs=P(("space", "snap"), "groups"),
        check_vma=False,
    )
```
